128 devices in a mesh: dy: 16 (over y, x), dx: 8 (over z, core).
Axes of the slice: x: 4, y: 4, z: 4, core: 2. Of those that a mesh axis runs over, the one named last changes fastest.
Arguments:
- heights: float32 [8192, 4096], P('dy', 'dx'), may hold values from -4 to 4
- albedo: float32 [8192, 4096], P('dy', 'dx'), may hold values from 0.5 to 1.5
- observed: bfloat16 [2048, 384, 384], P(('dy', 'dx')), may hold values from -2 to 2
- resample: bfloat16 [2048, 2, 384, 384], P(('dy', 'dx')), may hold values from -1 to 1
- exposure: float32 [8, 16], P('dx'), may hold values from -0.5 to 0.5
- sun_azimuth: float32 [8, 16], P('dx'), may hold values from -3.140625 to 3.140625
- sun_elevation: float32 [8, 16], P('dx'), may hold values from 0.02 to 0.3
- send_plan: int32 [16, 8, 4, 32], P('dy', 'dx'), may hold values from 0 to 128, as said below
- recv_plan: int32 [16, 8, 16], P('dy', 'dx'), may hold values from 0 to 31, as said below
Outputs:
- height_gradient: float32 [8192, 4096], P('dy', 'dx')
- camera_gradient: float32 [8, 16, 7], P('dx', 'dy')
The draws below stay inside these ranges and needn't reach their ends.
Inputs may be any that keep to these rules, and one draw needn't show every extreme that they name: send_plan[s, c, :, r * 2 + j] describes slot j of the crops that the DEM tile (s, c) serves to the device (r, c): row offset and column offset of the crop's window in the tile (multiples of 128, at most 128 and 128), the image m, and 1; unused slots are all zeros. Every device is served exactly 2 crops by at least one tile. recv_plan[r, c, m] = s * 2 + j names the used slot send_plan[s, c, :, r * 2 + j] whose image is m; the values of one device are distinct.
All inputs are finite; a program needn't handle non-finite values.
Results may differ from the reference program's by a relative error of at most 0.005.
Values may be sent and summed in bfloat16 or wider, within the bound.
No kernel may reach another device: no remote copies, remote signals or barrier semaphores. Data moves between devices by JAX's collectives and lax.ppermute only.
A program may use at most 384 MiB of HBM per device.

```python
import jax
import jax.numpy as jnp
from jax import lax

TY = 512
TX = 512
IMG_BAND = 16
CROP = 384
BLK = 128
MOST = 2
NY = 8192
NX = 4096
CROPS = 2048
N_DY = 16
N_DX = 8


DENSE_WEIGHT = 0.4


DENSE_LIMIT = 0.25


def plan_tables(key):
    base_key = jax.random.fold_in(key, 4242)
    key_rank, key_full, key_row, key_col = jax.random.split(base_key, 4)
    slot_count = N_DY * MOST
    owners = N_DY * N_DX
    slot_rank = jax.vmap(lambda rank_key: jax.random.permutation(rank_key, slot_count))(jax.random.split(key_rank, owners))
    slot_rank = slot_rank.reshape(N_DY, N_DX, slot_count).astype(jnp.int32)
    full_source = jax.random.randint(key_full, (N_DY, N_DX), 0, N_DY).astype(jnp.int32)
    full_source = full_source.at[0, 0].set(N_DY - 1)
    slot_source = jnp.arange(slot_count, dtype=jnp.int32) // MOST
    scores = jnp.where(slot_source[None, None, :] == full_source[:, :, None], -1, slot_rank)
    slot_order = jnp.argsort(scores, axis=-1, stable=True)
    chosen = slot_order[:, :, :IMG_BAND].astype(jnp.int32)
    row_steps = TY // BLK - CROP // BLK + 1
    col_steps = TX // BLK - CROP // BLK + 1
    shape_all = (N_DY, N_DX, IMG_BAND)
    row_off = jax.random.randint(key_row, shape_all, 0, row_steps).astype(jnp.int32) * BLK
    col_off = jax.random.randint(key_col, shape_all, 0, col_steps).astype(jnp.int32) * BLK
    image_ids = jnp.broadcast_to(jnp.arange(IMG_BAND, dtype=jnp.int32)[None, None, :], shape_all)
    row_off = jnp.where(image_ids == 0, TY - CROP, row_off)
    col_off = jnp.where(image_ids == 0, TX - CROP, col_off)
    dest_row = jnp.broadcast_to(jnp.arange(N_DY, dtype=jnp.int32)[:, None, None], shape_all)
    column = jnp.broadcast_to(jnp.arange(N_DX, dtype=jnp.int32)[None, :, None], shape_all)
    source = chosen // MOST
    lane_index = dest_row * MOST + chosen % MOST
    plan_table = jnp.zeros((N_DY, N_DX, 4, slot_count), jnp.int32)
    plan_table = plan_table.at[source, column, 0, lane_index].set(row_off)
    plan_table = plan_table.at[source, column, 1, lane_index].set(col_off)
    plan_table = plan_table.at[source, column, 2, lane_index].set(image_ids)
    plan_table = plan_table.at[source, column, 3, lane_index].set(jnp.ones(shape_all, jnp.int32))
    return (plan_table, chosen)


def draw_send_plan(key, part):
    return plan_tables(key)[0]


def draw_recv_plan(key, part):
    return plan_tables(key)[1]


def one_matrix_pair(crop_key):
    key_frac, key_shift, key_dense = jax.random.split(crop_key, 3)
    frac = jax.random.uniform(key_frac, (2, CROP, 1), jnp.float32, 0.0, 1.0)
    offset = jax.random.randint(key_shift, (2, 1, 1), -3, 4).astype(jnp.int32)
    row_pos = jnp.arange(CROP, dtype=jnp.int32)[:, None]
    col_pos = jnp.arange(CROP, dtype=jnp.int32)[None, :]
    distance = (col_pos - row_pos)[None] - offset
    frac_sq = frac * frac
    frac_cu = frac_sq * frac
    tap_minus = 0.5 * (-frac_cu + 2.0 * frac_sq - frac)
    tap_zero = 0.5 * (3.0 * frac_cu - 5.0 * frac_sq + 2.0)
    tap_one = 0.5 * (-3.0 * frac_cu + 4.0 * frac_sq + frac)
    tap_two = 0.5 * (frac_cu - frac_sq)
    band = jnp.where(distance == -1, tap_minus, 0.0) + jnp.where(distance == 0, tap_zero, 0.0) + jnp.where(distance == 1, tap_one, 0.0) + jnp.where(distance == 2, tap_two, 0.0)
    spread = DENSE_WEIGHT / CROP ** 0.5
    dense = jax.random.normal(key_dense, (2, CROP, CROP), jnp.float32) * spread
    band_scale = 0.75
    dense = jnp.clip(dense, -DENSE_LIMIT, DENSE_LIMIT)
    return (band_scale * band + dense).astype(jnp.bfloat16)


def draw_resample(key, part):
    crop_keys = jax.random.split(jax.random.fold_in(key, 99), CROPS)
    return lax.map(one_matrix_pair, crop_keys)


def levels(own_key, dims, shards, low, high):
    def one(axis_at, parts):
        draws = jax.random.uniform(jax.random.fold_in(jax.random.fold_in(own_key, 6), axis_at), (parts,), jnp.float32, low / len(shards), high / len(shards))
        return jnp.repeat(jnp.exp(draws), dims[axis_at] // parts).reshape((-1,) + (1,) * (len(dims) - axis_at - 1))

    level = one(*shards[0])
    for cut in shards[1:]:
        level = level * one(*cut)
    return level


def centred(stream_key, dims, width, reach, pieces=(), kind=jnp.bfloat16):
    values = jax.random.normal(stream_key, dims, jnp.float32) * width
    if len(pieces) > 0:
        values = levels(stream_key, dims, pieces, -0.22, 0.18) * values
    return jnp.clip(values, min=-reach, max=reach).astype(kind)


def setup_inputs(seed: int = 0) -> dict:
    keys = jax.random.split(jax.random.key(seed), 10)
    return {
        "heights": centred(keys[0], (NY, NX), 0.5, 4.0, ((0, 16), (1, 8)), jnp.float32),
        "albedo": jnp.clip(0.5 + 1.0 * jax.random.uniform(keys[1], (NY, NX), jnp.float32) ** levels(keys[1], (NY, NX), ((0, 16), (1, 8)), -0.2, 0.2), 0.5, 1.5),
        "observed": centred(keys[2], (CROPS, CROP, CROP), 0.3, 2.0, ((0, 128),)),
        "resample": draw_resample(jax.random.fold_in(keys[9], 71), 0),
        "exposure": jnp.clip(jax.random.uniform(keys[4], (N_DX, IMG_BAND), jnp.float32, -0.5, 0.5) * levels(keys[4], (N_DX, IMG_BAND), ((0, 8),), -0.4, 0.0), -0.5, 0.5),
        "sun_azimuth": jnp.clip(jax.random.uniform(keys[5], (N_DX, IMG_BAND), jnp.float32, -3.140625, 3.140625), -3.140625, 3.140625),
        "sun_elevation": jnp.clip(0.02 + 0.28 * jax.random.uniform(keys[6], (N_DX, IMG_BAND), jnp.float32) ** levels(keys[6], (N_DX, IMG_BAND), ((0, 8),), -0.2, 0.2), 0.02, 0.3),
        "send_plan": draw_send_plan(jax.random.fold_in(keys[9], 71), 0),
        "recv_plan": draw_recv_plan(jax.random.fold_in(keys[9], 71), 0),
    }


SMOOTHING_WEIGHT = 0.02

def slopes(padded):
    slope_x = (padded[1:-1, 2:] - padded[1:-1, :-2]) * 0.5
    slope_y = (padded[2:, 1:-1] - padded[:-2, 1:-1]) * 0.5
    return (slope_x, slope_y)

def laplace(padded):
    return padded[:-2, 1:-1] + padded[2:, 1:-1] + padded[1:-1, :-2] + padded[1:-1, 2:] - 4.0 * padded[1:-1, 1:-1]

def shading(slope_x, slope_y, albedo):
    length = jnp.sqrt(1.0 + slope_x * slope_x + slope_y * slope_y)
    normal = jnp.stack([-slope_x, -slope_y, jnp.ones_like(slope_x)])
    return albedo[None] * normal / length[None]

def sun_vectors(solar_azimuth, elevation):
    return jnp.stack([jnp.cos(elevation) * jnp.cos(solar_azimuth), jnp.cos(elevation) * jnp.sin(solar_azimuth), jnp.sin(elevation)])

def edge_diff(values):
    step_diff = values[..., 1:] - values[..., :-1]
    return jnp.concatenate([step_diff[..., :1], 0.5 * (step_diff[..., 1:] + step_diff[..., :-1]), step_diff[..., -1:]], axis=-1)

def crop_terms(predicted, residual):
    crop_size = predicted.shape[-1]
    coordinate = (jnp.arange(crop_size, dtype=jnp.float32) - 0.5 * (crop_size - 1)) / crop_size
    deriv_u = edge_diff(predicted)
    deriv_v = jnp.swapaxes(edge_diff(jnp.swapaxes(predicted, -1, -2)), -1, -2)
    resid_u = residual * deriv_u
    resid_v = residual * deriv_v
    col_coord = coordinate[None, None, :]
    row_coord = coordinate[None, :, None]
    sum_list = [lax.optimization_barrier(jnp.sum(resid_u, axis=(1, 2))), lax.optimization_barrier(jnp.sum(resid_u * col_coord, axis=(1, 2))), lax.optimization_barrier(jnp.sum(resid_u * row_coord, axis=(1, 2))), lax.optimization_barrier(jnp.sum(resid_v, axis=(1, 2))), lax.optimization_barrier(jnp.sum(resid_v * col_coord, axis=(1, 2))), lax.optimization_barrier(jnp.sum(resid_v * row_coord, axis=(1, 2)))]
    pose_part = jnp.stack(sum_list, axis=-1) / crop_size
    exposure_part = lax.optimization_barrier(jnp.sum(residual * predicted, axis=(1, 2))) / (crop_size * crop_size)
    return jnp.concatenate([pose_part, exposure_part[:, None]], axis=-1)

def render(shaded, observed, resample, exposure_gain):
    row_mat = resample[:, 0].astype(jnp.float32)
    col_mat = resample[:, 1].astype(jnp.float32)
    first_pass = jnp.einsum('nij,njk->nik', row_mat, shaded.astype(jnp.float32)).astype(jnp.bfloat16)
    predicted = exposure_gain[:, None, None] * jnp.einsum('nil,nkl->nik', first_pass.astype(jnp.float32), col_mat)
    residual = predicted - observed.astype(jnp.float32)
    crop_sums = crop_terms(predicted, residual)
    weighted = (exposure_gain[:, None, None] * residual).astype(jnp.bfloat16)
    back_pass = jnp.einsum('nji,njk->nik', row_mat, weighted.astype(jnp.float32)).astype(jnp.bfloat16)
    crop_grad = jnp.einsum('njk,nkl->njl', back_pass.astype(jnp.float32), col_mat).astype(jnp.bfloat16)
    return (crop_sums, crop_grad)

def reference(heights, albedo, observed, resample, exposure, sun_azimuth, sun_elevation, send_plan, recv_plan):
    padded = jnp.pad(heights, 1)
    slope_x, slope_y = slopes(padded)
    fields = shading(slope_x, slope_y, albedo)
    sun_table = sun_vectors(sun_azimuth, sun_elevation)
    crop_ids = jnp.arange(N_DY * N_DX * IMG_BAND, dtype=jnp.int32)
    dest_row = crop_ids // (N_DX * IMG_BAND)
    column = crop_ids // IMG_BAND % N_DX
    image_ids = crop_ids % IMG_BAND
    slot_ids = recv_plan.reshape(-1).astype(jnp.int32)
    source = slot_ids // MOST
    lane_index = dest_row * MOST + slot_ids % MOST
    top_row = (source * TY + send_plan[source, column, 0, lane_index]).astype(jnp.int32)
    left_col = (column * TX + send_plan[source, column, 1, lane_index]).astype(jnp.int32)
    crop_sun = sun_table[:, column, image_ids]
    exposure_gain = jnp.exp(exposure[column, image_ids])

    def cut(crop_index):
        image_window = lax.dynamic_slice(fields, (jnp.int32(0), top_row[crop_index], left_col[crop_index]), (3, CROP, CROP))
        return lax.optimization_barrier(jnp.sum(crop_sun[:, crop_index][:, None, None] * image_window, axis=0)).astype(jnp.bfloat16)
    shaded = lax.map(cut, crop_ids)
    groups = N_DY * N_DX

    def group_render(bundle_in):
        return render(bundle_in[0], bundle_in[1], bundle_in[2], bundle_in[3])
    crop_sums, crop_grad = lax.map(group_render, (shaded.reshape(groups, IMG_BAND, CROP, CROP), observed.reshape(groups, IMG_BAND, CROP, CROP), resample.reshape(groups, IMG_BAND, 2, CROP, CROP), exposure_gain.reshape(groups, IMG_BAND)))
    crop_grad = crop_grad.reshape(-1, CROP, CROP)

    def place(running, crop_index):
        start = (jnp.int32(0), top_row[crop_index], left_col[crop_index])
        image_window = lax.dynamic_slice(running, start, (3, CROP, CROP))
        update = image_window + crop_sun[:, crop_index][:, None, None] * crop_grad[crop_index].astype(jnp.float32)[None]
        return (lax.dynamic_update_slice(running, update, start), None)
    field_grads, _ = lax.scan(place, jnp.zeros((3, NY, NX), jnp.float32), crop_ids)

    def shade_local(slope_a, slope_b):
        return shading(slope_a, slope_b, albedo)
    _, pull_back = jax.vjp(shade_local, slope_x, slope_y)
    grad_x, grad_y = pull_back(field_grads)
    padded_x = jnp.pad(grad_x, 1)
    padded_y = jnp.pad(grad_y, 1)
    data_term_gradient = (padded_x[1:-1, :-2] - padded_x[1:-1, 2:]) * 0.5 + (padded_y[:-2, 1:-1] - padded_y[2:, 1:-1]) * 0.5
    laplacian = laplace(padded)
    smoothness_term = laplace(jnp.pad(laplacian, 1))
    height_gradient = data_term_gradient + SMOOTHING_WEIGHT * smoothness_term
    camera_gradient = lax.optimization_barrier(jnp.sum(crop_sums.reshape(N_DY, N_DX, IMG_BAND, 7), axis=0))
    return (height_gradient, camera_gradient)
```

```python
import jax
import jax.numpy as jnp
from jax import lax
from jax.experimental import pallas as pl
from jax.experimental.pallas import tpu as pltpu
from jax.sharding import PartitionSpec as P

SMOOTHING_WEIGHT = 0.02
H_SCALE = 8191.0
A_SCALE = 65534.0
T = 512
C = 384
EXTRA = 8
SPILL = 16
CH = 32
F32 = jnp.float32
BF16 = jnp.bfloat16
I32 = jnp.int32


def pack(high, low):
    return lax.shift_left(high, 16) | (low & 0xFFFF)


def high_of(word):
    return lax.shift_right_arithmetic(word, 16).astype(F32)


def low_of(word):
    return lax.shift_right_arithmetic(lax.shift_left(word, 16), 16).astype(F32)


def tile_kernel(
    used, image, row_off, col_off, sun, gain,
    tile_ref, res_ref, obs_ref,
    out_ref, sums_ref,
    hbuf, halo, sx_ref, sy_ref, w_ref, r2_ref, gx_ref, gy_ref,
    shaded, pbuf, weighted, grad,
):
    step = pl.program_id(0)
    first = (step // 2) * 2
    slot_odd = step % 2
    mine = used[step] == 1
    any_used = used[first] + used[first + 1] > 0

    @pl.when(step == 0)
    def _():
        sums_ref[...] = jnp.zeros_like(sums_ref)

    @pl.when((slot_odd == 0) & any_used)
    def _():
        words = tile_ref[0, T : T + EXTRA]
        halo[0:8] = high_of(words)
        halo[8:16] = low_of(words)
        hbuf[7:8] = halo[1:2]
        hbuf[T + 8 : T + 9] = halo[2:3]

        def unpack(k, _):
            base = pl.multiple_of(k * CH, CH)
            hbuf[pl.ds(base + 8, CH)] = high_of(tile_ref[0, pl.ds(base, CH)])
            gx_ref[pl.ds(base, CH)] = jnp.zeros((CH, T), F32)
            gy_ref[pl.ds(base + 8, CH)] = jnp.zeros((CH, T), F32)
            return 0

        lax.fori_loop(0, T // CH, unpack, 0)
        gy_ref[0:8] = jnp.zeros((8, T), F32)
        gy_ref[T + 8 : T + 16] = jnp.zeros((8, T), F32)

        def slope(k, _):
            base = pl.multiple_of(k * CH, CH)
            block = pl.multiple_of((k * CH // 128) * 128, 128)
            rows = hbuf[pl.ds(base, CH + 16)]
            h = rows[8 : 8 + CH]
            lane = lax.broadcasted_iota(I32, (CH, T), 1)
            pick = (
                lax.broadcasted_iota(I32, (CH, 128), 0) + (base - block)
                == lax.broadcasted_iota(I32, (CH, 128), 1)
            )
            left_col = jnp.sum(
                jnp.where(pick, halo[0:1, pl.ds(block, 128)], 0.0), axis=1, keepdims=True
            )
            right_col = jnp.sum(
                jnp.where(pick, halo[8:9, pl.ds(block, 128)], 0.0), axis=1, keepdims=True
            )
            left = jnp.where(lane == 0, left_col, pltpu.roll(h, 1, 1))
            right = jnp.where(lane == T - 1, right_col, pltpu.roll(h, T - 1, 1))
            sx = (right - left) * (0.5 / H_SCALE)
            sy = (rows[9 : 9 + CH] - rows[7 : 7 + CH]) * (0.5 / H_SCALE)
            albedo = low_of(tile_ref[0, pl.ds(base, CH)]) * (1.0 / A_SCALE) + 1.0
            r = lax.rsqrt(1.0 + sx * sx + sy * sy)
            sx_ref[pl.ds(base, CH)] = sx
            sy_ref[pl.ds(base, CH)] = sy
            w_ref[pl.ds(base, CH)] = albedo * r
            r2_ref[pl.ds(base, CH)] = r * r
            return 0

        lax.fori_loop(0, T // CH, slope, 0)

    @pl.when(mine)
    def _():
        m = image[step]
        oy = pl.multiple_of(row_off[step], 128)
        ox = pl.multiple_of(col_off[step], 128)
        s1 = sun[m]
        s2 = sun[16 + m]
        s3 = sun[32 + m]
        e = gain[m]
        cols = pl.ds(ox, C)

        def shade(k, _):
            base = pl.multiple_of(k * CH, CH)
            rows = pl.ds(pl.multiple_of(oy + base, CH), CH)
            q = s3 - s1 * sx_ref[rows, cols] - s2 * sy_ref[rows, cols]
            shaded[pl.ds(base, CH)] = (w_ref[rows, cols] * q).astype(BF16)
            return 0

        lax.fori_loop(0, C // CH, shade, 0)
        row_mat = res_ref[0, 0]
        col_mat = res_ref[0, 1]
        first_pass = jnp.dot(row_mat, shaded[...], preferred_element_type=F32).astype(BF16)
        pbuf[8 : 8 + C] = e * lax.dot_general(
            first_pass, col_mat, (((1,), (1,)), ((), ())), preferred_element_type=F32
        )
        pbuf[7:8] = 2.0 * pbuf[8:9] - pbuf[9:10]
        pbuf[C + 8 : C + 9] = 2.0 * pbuf[C + 7 : C + 8] - pbuf[C + 6 : C + 7]

        def fold(v):
            return v.reshape(CH // 8, 8, C)

        def terms(k, carry):
            a_x, a_xg, a_y, a_yg, a_e = carry
            base = pl.multiple_of(k * CH, CH)
            rows = pbuf[pl.ds(base, CH + 16)]
            p = rows[8 : 8 + CH]
            lane = lax.broadcasted_iota(I32, (CH, C), 1)
            residual = p - obs_ref[0, pl.ds(base, CH)].astype(F32)
            left = jnp.where(lane == 0, p, pltpu.roll(p, 1, 1))
            right = jnp.where(lane == C - 1, p, pltpu.roll(p, C - 1, 1))
            xs = fold(residual * (right - left))
            ys = fold(residual * (rows[9 : 9 + CH] - rows[7 : 7 + CH]))
            es = fold(residual * p)
            weighted[pl.ds(base, CH)] = (e * residual).astype(BF16)
            for g in range(CH // 8):
                at = (base + 8 * g).astype(F32)
                a_x = a_x + xs[g]
                a_xg = a_xg + xs[g] * at
                a_y = a_y + ys[g]
                a_yg = a_yg + ys[g] * at
                a_e = a_e + es[g]
            return a_x, a_xg, a_y, a_yg, a_e

        zero = jnp.zeros((8, C), F32)
        parts = lax.fori_loop(0, C // CH, terms, (zero,) * 5)
        for n in range(5):
            sums_ref[m, n] = parts[n]
        back_pass = lax.dot_general(
            row_mat, weighted[...], (((0,), (0,)), ((), ())), preferred_element_type=F32
        ).astype(BF16)
        grad[...] = jnp.dot(back_pass, col_mat, preferred_element_type=F32).astype(BF16)

        def pull(k, _):
            base = pl.multiple_of(k * CH, CH)
            rows = pl.ds(pl.multiple_of(oy + base, CH), CH)
            rows_y = pl.ds(pl.multiple_of(oy + base + 8, 8), CH)
            sx = sx_ref[rows, cols]
            sy = sy_ref[rows, cols]
            t = (s3 - s1 * sx - s2 * sy) * r2_ref[rows, cols]
            wg = w_ref[rows, cols] * grad[pl.ds(base, CH)].astype(F32)
            gx_ref[rows, cols] = gx_ref[rows, cols] - wg * (s1 + t * sx)
            gy_ref[rows_y, cols] = gy_ref[rows_y, cols] - wg * (s2 + t * sy)
            return 0

        lax.fori_loop(0, C // CH, pull, 0)

    @pl.when((slot_odd == 1) & any_used)
    def _():
        def stencil(k, _):
            base = pl.multiple_of(k * CH, CH)
            lane = lax.broadcasted_iota(I32, (CH, T), 1)
            gx = gx_ref[pl.ds(base, CH)]
            rows = gy_ref[pl.ds(base, CH + 16)]
            left = jnp.where(lane == 0, 0.0, pltpu.roll(gx, 1, 1))
            right = jnp.where(lane == T - 1, 0.0, pltpu.roll(gx, T - 1, 1))
            total = (left - right) + (rows[7 : 7 + CH] - rows[9 : 9 + CH])
            out_ref[0, pl.ds(base, CH)] = (0.5 * total).astype(BF16)
            return 0

        lax.fori_loop(0, T // CH, stencil, 0)
        eye = lax.broadcasted_iota(I32, (128, 128), 0) == lax.broadcasted_iota(
            I32, (128, 128), 1
        )
        low = []
        high = []
        for b in range(T // 128):
            first_col = gx_ref[128 * b : 128 * (b + 1), 0:128][:, 0:1]
            last_col = gx_ref[128 * b : 128 * (b + 1), T - 128 : T][:, 127:128]
            low.append(jnp.sum(jnp.where(eye, first_col, 0.0), axis=0, keepdims=True))
            high.append(jnp.sum(jnp.where(eye, last_col, 0.0), axis=0, keepdims=True))
        spill = jnp.concatenate(
            [
                -0.5 * gy_ref[8:9],
                0.5 * gy_ref[T + 7 : T + 8],
                -0.5 * jnp.concatenate(low, axis=1),
                0.5 * jnp.concatenate(high, axis=1),
                jnp.zeros((SPILL - 4, T), F32),
            ],
            axis=0,
        )
        out_ref[0, T : T + SPILL] = spill.astype(BF16)

    @pl.when((slot_odd == 1) & jnp.logical_not(any_used))
    def _():
        out_ref[...] = jnp.zeros_like(out_ref)


def run_tiles(tiles, resample, observed, used, image, row_off, col_off, sun, gain):
    count = tiles.shape[0]
    grid_spec = pltpu.PrefetchScalarGridSpec(
        num_scalar_prefetch=6,
        grid=(2 * count,),
        in_specs=[
            pl.BlockSpec((1, T + EXTRA, T), lambda i, *s: (i // 2, 0, 0)),
            pl.BlockSpec((1, 2, C, C), lambda i, u, m, *s: (m[i], 0, 0, 0)),
            pl.BlockSpec((1, C, C), lambda i, u, m, *s: (m[i], 0, 0)),
        ],
        out_specs=[
            pl.BlockSpec((1, T + SPILL, T), lambda i, *s: (i // 2, 0, 0)),
            pl.BlockSpec((16, 5, 8, C), lambda i, *s: (0, 0, 0, 0)),
        ],
        scratch_shapes=[
            pltpu.VMEM((T + 16, T), F32),
            pltpu.VMEM((16, T), F32),
            pltpu.VMEM((T, T), F32),
            pltpu.VMEM((T, T), F32),
            pltpu.VMEM((T, T), F32),
            pltpu.VMEM((T, T), F32),
            pltpu.VMEM((T, T), F32),
            pltpu.VMEM((T + 16, T), F32),
            pltpu.VMEM((C, C), BF16),
            pltpu.VMEM((C + 16, C), F32),
            pltpu.VMEM((C, C), BF16),
            pltpu.VMEM((C, C), BF16),
        ],
    )
    return pl.pallas_call(
        tile_kernel,
        grid_spec=grid_spec,
        out_shape=[
            jax.ShapeDtypeStruct((count, T + SPILL, T), BF16),
            jax.ShapeDtypeStruct((16, 5, 8, C), F32),
        ],
        compiler_params=pltpu.CompilerParams(dimension_semantics=("arbitrary",)),
        name="tiles",
    )(used, image, row_off, col_off, sun, gain, tiles, resample, observed)


def next_images(used, image):
    count = used.shape[0]
    ids = jnp.arange(count, dtype=I32)
    is_used = used == 1
    ahead = jnp.min(
        jnp.where(is_used[None, :] & (ids[None, :] >= ids[:, None]), ids[None, :], count), axis=1
    )
    last = jnp.maximum(jnp.max(jnp.where(is_used, ids, -1)), 0)
    at = jnp.where(ahead < count, ahead, last)
    return jnp.sum(jnp.where(at[:, None] == ids[None, :], image[None, :], 0), axis=1)


def sun_vectors(azimuth, elevation):
    return jnp.stack(
        [
            jnp.cos(elevation) * jnp.cos(azimuth),
            jnp.cos(elevation) * jnp.sin(azimuth),
            jnp.sin(elevation),
        ]
    )


def laplace(padded):
    return (
        padded[:-2, 1:-1]
        + padded[2:, 1:-1]
        + padded[1:-1, :-2]
        + padded[1:-1, 2:]
        - 4.0 * padded[1:-1, 1:-1]
    )


def shifted(value, axis, up):
    count = lax.axis_size(axis)
    pairs = [(i, i + 1) for i in range(count - 1)]
    return lax.ppermute(value, axis, pairs if up else [(b, a) for a, b in pairs])


def quantize(heights):
    return jnp.round(heights * H_SCALE).astype(I32)


def smoothness(heights, top, bottom):
    tall = jnp.concatenate([top, heights, bottom], axis=0)
    left = shifted(tall[:, -2:], "dx", True)
    right = shifted(tall[:, :2], "dx", False)
    wide = jnp.concatenate([left, tall, right], axis=1)
    field = laplace(wide)
    rows, cols = heights.shape
    row_ids = jnp.arange(rows + 2)
    col_ids = jnp.arange(cols + 2)
    row_keep = ~(
        (row_ids == 0) & (lax.axis_index("dy") == 0)
        | (row_ids == rows + 1) & (lax.axis_index("dy") == lax.axis_size("dy") - 1)
    )
    col_keep = ~(
        (col_ids == 0) & (lax.axis_index("dx") == 0)
        | (col_ids == cols + 1) & (lax.axis_index("dx") == lax.axis_size("dx") - 1)
    )
    return SMOOTHING_WEIGHT * laplace(jnp.where(row_keep[:, None] & col_keep[None, :], field, 0.0))


def finish_sums(parts):
    ids = jnp.arange(C, dtype=F32)
    coord = (ids - 0.5 * (C - 1)) / C
    edge = jnp.where((ids == 0) | (ids == C - 1), 1.0, 0.5)
    start = (jnp.arange(8, dtype=F32) - 0.5 * (C - 1)) / C
    x_sum, x_row, y_sum, y_row, e_sum = (parts[:, n] for n in range(5))
    x_v = x_row / C + x_sum * start[None, :, None]
    y_v = y_row / C + y_sum * start[None, :, None]

    def total(v):
        return jnp.sum(v, axis=(1, 2))

    pose = [
        total(x_sum * edge),
        total(x_sum * (edge * coord)),
        total(x_v * edge),
        total(y_sum) * 0.5,
        total(y_sum * coord) * 0.5,
        total(y_v) * 0.5,
    ]
    return jnp.concatenate(
        [jnp.stack(pose, axis=-1) / C, (total(e_sum) / (C * C))[:, None]], axis=-1
    )


def per_device(
    heights, albedo, observed, resample, exposure, sun_azimuth, sun_elevation, send_plan, recv_plan
):
    offsets = send_plan[0, 0, 0:2].reshape(2, 16, 2).transpose(1, 0, 2)
    offsets = lax.all_to_all(offsets, "dy", split_axis=0, concat_axis=0, tiled=True)
    row_off = offsets[:, 0].reshape(-1)
    col_off = offsets[:, 1].reshape(-1)
    slots = jnp.arange(32, dtype=I32)
    match = recv_plan[0, 0][None, :] == slots[:, None]
    used = jnp.any(match, axis=1).astype(I32)
    image = jnp.sum(jnp.where(match, jnp.arange(16, dtype=I32)[None, :], 0), axis=1)
    image = next_images(used, image)
    sun = sun_vectors(sun_azimuth[0], sun_elevation[0]).reshape(-1)
    gain = jnp.exp(exposure[0])

    top = shifted(heights[-2:], "dy", True)
    bottom = shifted(heights[:2], "dy", False)
    left = shifted(heights[:, -1], "dx", True)
    right = shifted(heights[:, 0], "dx", False)
    rims = jnp.stack(
        [
            pack(quantize(left), quantize(right)),
            pack(quantize(top[1]), jnp.zeros_like(quantize(top[1]))),
            pack(quantize(bottom[0]), jnp.zeros_like(quantize(bottom[0]))),
        ]
    )
    words = pack(quantize(heights), jnp.round((albedo - 1.0) * A_SCALE).astype(I32))
    words = jnp.concatenate([words, rims, jnp.zeros((EXTRA - 3, T), I32)], axis=0)
    tiles = lax.all_gather(words, "dy", axis=0)
    smooth = smoothness(heights, top, bottom)
    outs, parts = run_tiles(
        tiles, resample, observed, used, image, row_off, col_off, sun, gain
    )
    crop_sums = finish_sums(parts)
    arrived = lax.all_to_all(crop_sums[:, None], "dy", split_axis=0, concat_axis=0, tiled=True)
    camera = arrived.sum(axis=0)
    own = lax.psum_scatter(outs, "dy", scatter_dimension=0).astype(F32)
    from_below = shifted(own[T], "dy", False)
    from_above = shifted(own[T + 1], "dy", True)
    from_right = shifted(own[T + 2], "dx", False)
    from_left = shifted(own[T + 3], "dx", True)
    row_ids = lax.broadcasted_iota(I32, (T, T), 0)
    col_ids = lax.broadcasted_iota(I32, (T, T), 1)
    data = own[:T]
    data = data + jnp.where(row_ids == T - 1, from_below[None, :], 0.0)
    data = data + jnp.where(row_ids == 0, from_above[None, :], 0.0)
    data = data + jnp.where(col_ids == T - 1, from_right[:, None], 0.0)
    data = data + jnp.where(col_ids == 0, from_left[:, None], 0.0)
    return (data + smooth, camera[None])


def solution(mesh):
    placed = (
        P("dy", "dx"),
        P("dy", "dx"),
        P(("dy", "dx"), None, None),
        P(("dy", "dx"), None, None, None),
        P("dx", None),
        P("dx", None),
        P("dx", None),
        P("dy", "dx", None, None),
        P("dy", "dx", None),
    )
    return jax.shard_map(
        per_device,
        mesh=mesh,
        in_specs=placed,
        out_specs=(P("dy", "dx"), P("dx", "dy", None)),
        check_vma=False,
    )
```

```python
import jax
import jax.numpy as jnp
from jax import lax
from jax.experimental import pallas as pl
from jax.experimental.pallas import tpu as pltpu
from jax.sharding import PartitionSpec as P

SMOOTHING_WEIGHT = 0.02
H_SCALE = 8191.0
A_SCALE = 65534.0
T = 512
C = 384
EXTRA = 8
SPILL = 16
CH = 32
F32 = jnp.float32
BF16 = jnp.bfloat16
I32 = jnp.int32


def pack(high, low):
    return lax.shift_left(high, 16) | (low & 0xFFFF)


def high_of(word):
    return lax.shift_right_arithmetic(word, 16).astype(F32)


def low_of(word):
    return lax.shift_right_arithmetic(lax.shift_left(word, 16), 16).astype(F32)


def tile_kernel(
    used, image, row_off, col_off, sun, gain,
    tile_ref, res_ref, obs_ref,
    out_ref, sums_ref,
    hbuf, hcol, sx_ref, sy_ref, w_ref, r2_ref, gx_ref, gy_ref,
    shaded, tbuf, pbuf, weighted, grad,
):
    step = pl.program_id(0)
    first = (step // 2) * 2
    slot_odd = step % 2
    mine = used[step] == 1
    any_used = used[first] + used[first + 1] > 0
    lane = lax.broadcasted_iota(I32, (CH, 128), 1)
    at_first = lane == 0
    at_last = lane == 127

    def lanes(b):
        return slice(128 * b, 128 * (b + 1))

    @pl.when(step == 0)
    def _():
        sums_ref[...] = jnp.zeros_like(sums_ref)

    @pl.when((slot_odd == 0) & any_used)
    def _():
        words = tile_ref[0, T : T + EXTRA]
        high = lax.shift_right_arithmetic(words, 16)
        low = lax.shift_right_arithmetic(lax.shift_left(words, 16), 16)
        pieces = jnp.concatenate(
            [
                lax.shift_right_arithmetic(high, 8),
                high & 255,
                lax.shift_right_arithmetic(low, 8),
                low & 255,
            ],
            axis=0,
        ).astype(F32).astype(BF16)
        row_id = lax.broadcasted_iota(I32, (32, 256), 0)
        side = lax.broadcasted_iota(I32, (32, 256), 1) // 128
        scale = jnp.where(row_id == 16 * side, 256.0, 0.0) + jnp.where(
            row_id == 16 * side + 8, 1.0, 0.0
        )
        columns = lax.dot_general(
            pieces, scale.astype(BF16), (((0,), (0,)), ((), ())), preferred_element_type=F32
        )
        for side_id in range(2):
            hcol[side_id] = columns[:, lanes(side_id)]
        rims = high.astype(F32)
        for b in range(4):
            hbuf[b, 7:8] = rims[1:2, lanes(b)]
            hbuf[b, T + 8 : T + 9] = rims[2:3, lanes(b)]
            gy_ref[b, 0:8] = jnp.zeros((8, 128), F32)
            gy_ref[b, T + 8 : T + 16] = jnp.zeros((8, 128), F32)

        def unpack(k, _):
            base = pl.multiple_of(k * CH, CH)
            for b in range(4):
                hbuf[b, pl.ds(base + 8, CH)] = high_of(tile_ref[0, pl.ds(base, CH), lanes(b)])
            return 0

        lax.fori_loop(0, T // CH, unpack, 0, unroll=2)

        def slope(k, _):
            base = pl.multiple_of(k * CH, CH)
            rows = pl.ds(base, CH)
            here = [hbuf[b, pl.ds(base + 8, CH)] for b in range(4)]
            right_turn = [pltpu.roll(h, 1, 1) for h in here]
            left_turn = [pltpu.roll(h, 127, 1) for h in here]
            before = [hcol[0, rows]] + right_turn[:3]
            after = left_turn[1:] + [hcol[1, rows]]
            for b in range(4):
                left = jnp.where(at_first, before[b], right_turn[b])
                right = jnp.where(at_last, after[b], left_turn[b])
                sx = (right - left) * (0.5 / H_SCALE)
                sy = (hbuf[b, pl.ds(base + 9, CH)] - hbuf[b, pl.ds(base + 7, CH)]) * (
                    0.5 / H_SCALE
                )
                albedo = low_of(tile_ref[0, rows, lanes(b)]) * (1.0 / A_SCALE) + 1.0
                r = lax.rsqrt(1.0 + sx * sx + sy * sy)
                sx_ref[b, rows] = sx
                sy_ref[b, rows] = sy
                w_ref[b, rows] = albedo * r
                r2_ref[b, rows] = r * r
                gx_ref[b, rows] = jnp.zeros((CH, 128), F32)
                gy_ref[b, pl.ds(base + 8, CH)] = jnp.zeros((CH, 128), F32)
            return 0

        lax.fori_loop(0, T // CH, slope, 0, unroll=4)

    @pl.when(mine)
    def _():
        m = image[step]
        oy = pl.multiple_of(row_off[step], 128)
        ob = col_off[step] // 128
        s1 = sun[m]
        s2 = sun[16 + m]
        s3 = sun[32 + m]
        e = gain[m]

        def shade(k, _):
            base = pl.multiple_of(k * CH, CH)
            rows = pl.ds(pl.multiple_of(oy + base, CH), CH)
            for b in range(3):
                q = s3 - s1 * sx_ref[ob + b, rows] - s2 * sy_ref[ob + b, rows]
                shaded[pl.ds(base, CH), lanes(b)] = (w_ref[ob + b, rows] * q).astype(BF16)
                tbuf[b, pl.ds(base, CH)] = q * r2_ref[ob + b, rows]
            return 0

        lax.fori_loop(0, C // CH, shade, 0, unroll=4)
        row_mat = res_ref[0, 0]
        col_mat = res_ref[0, 1]
        first_pass = jnp.dot(row_mat, shaded[...], preferred_element_type=F32).astype(BF16)
        predicted = e * lax.dot_general(
            first_pass, col_mat, (((1,), (1,)), ((), ())), preferred_element_type=F32
        )
        for b in range(3):
            pbuf[b, 8 : 8 + C] = predicted[:, lanes(b)]
            pbuf[b, 7:8] = 2.0 * pbuf[b, 8:9] - pbuf[b, 9:10]
            pbuf[b, C + 8 : C + 9] = 2.0 * pbuf[b, C + 7 : C + 8] - pbuf[b, C + 6 : C + 7]

        def add_up(v, base, total, by_row):
            groups = [v[8 * g : 8 * g + 8] for g in range(CH // 8)]
            tail = groups[-1]
            lead = tail
            for g in range(CH // 8 - 2, 0, -1):
                tail = groups[g] + tail
                lead = lead + tail
            tail = groups[0] + tail
            return total + tail, by_row + lead * 8.0 + tail * base

        def terms(k, carry):
            base = pl.multiple_of(k * CH, CH)
            at = base.astype(F32)
            rows = pl.ds(base, CH)
            here = [pbuf[b, pl.ds(base + 8, CH)] for b in range(3)]
            right_turn = [pltpu.roll(p, 1, 1) for p in here]
            left_turn = [pltpu.roll(p, 127, 1) for p in here]
            before = [here[0]] + right_turn[:2]
            after = left_turn[1:] + [here[2]]
            result = []
            for b in range(3):
                a_x, a_xg, a_y, a_yg, a_e = carry[b]
                p = here[b]
                residual = p - obs_ref[0, rows, lanes(b)].astype(F32)
                weighted[rows, lanes(b)] = (e * residual).astype(BF16)
                left = jnp.where(at_first, before[b], right_turn[b])
                right = jnp.where(at_last, after[b], left_turn[b])
                a_x, a_xg = add_up(residual * (right - left), at, a_x, a_xg)
                down = pbuf[b, pl.ds(base + 9, CH)]
                up = pbuf[b, pl.ds(base + 7, CH)]
                a_y, a_yg = add_up(residual * (down - up), at, a_y, a_yg)
                squares = residual * p
                a_e = a_e + squares.reshape(CH // 8, 8, 128).sum(axis=0)
                result.append((a_x, a_xg, a_y, a_yg, a_e))
            return tuple(result)

        zero = jnp.zeros((8, 128), F32)
        parts = lax.fori_loop(0, C // CH, terms, ((zero,) * 5,) * 3, unroll=3)
        for b in range(3):
            for n in range(5):
                sums_ref[m, n, :, lanes(b)] = parts[b][n]
        back_pass = lax.dot_general(
            row_mat, weighted[...], (((0,), (0,)), ((), ())), preferred_element_type=F32
        ).astype(BF16)
        crop_grad = jnp.dot(back_pass, col_mat, preferred_element_type=F32)
        for b in range(3):
            grad[b] = crop_grad[:, lanes(b)]

        def pull(k, _):
            base = pl.multiple_of(k * CH, CH)
            rows = pl.ds(pl.multiple_of(oy + base, CH), CH)
            rows_y = pl.ds(pl.multiple_of(oy + base + 8, 8), CH)
            for b in range(3):
                t = tbuf[b, pl.ds(base, CH)]
                wg = w_ref[ob + b, rows] * grad[b, pl.ds(base, CH)]
                gx_ref[ob + b, rows] = gx_ref[ob + b, rows] - wg * (s1 + t * sx_ref[ob + b, rows])
                gy_ref[ob + b, rows_y] = gy_ref[ob + b, rows_y] - wg * (
                    s2 + t * sy_ref[ob + b, rows]
                )
            return 0

        lax.fori_loop(0, C // CH, pull, 0, unroll=4)

    @pl.when((slot_odd == 1) & any_used)
    def _():
        def stencil(k, _):
            base = pl.multiple_of(k * CH, CH)
            rows = pl.ds(base, CH)
            here = [gx_ref[b, rows] for b in range(4)]
            right_turn = [pltpu.roll(g, 1, 1) for g in here]
            left_turn = [pltpu.roll(g, 127, 1) for g in here]
            blank = jnp.zeros((CH, 128), F32)
            before = [blank] + right_turn[:3]
            after = left_turn[1:] + [blank]
            for b in range(4):
                left = jnp.where(at_first, before[b], right_turn[b])
                right = jnp.where(at_last, after[b], left_turn[b])
                up = gy_ref[b, pl.ds(base + 7, CH)]
                down = gy_ref[b, pl.ds(base + 9, CH)]
                total = (left - right) + (up - down)
                out_ref[0, rows, lanes(b)] = (0.5 * total).astype(BF16)
            return 0

        lax.fori_loop(0, T // CH, stencil, 0, unroll=4)
        sub = lax.broadcasted_iota(I32, (16, 128), 0)
        lane16 = lax.broadcasted_iota(I32, (16, 128), 1)
        pick_low = jnp.where((sub == 2) & (lane16 == 0), -0.5, 0.0).astype(BF16)
        pick_high = jnp.where((sub == 3) & (lane16 == 127), 0.5, 0.0).astype(BF16)
        cross = (((1,), (1,)), ((), ()))
        spill = lax.dot_general(
            pick_low, gx_ref[0].astype(BF16), cross, preferred_element_type=F32
        ) + lax.dot_general(pick_high, gx_ref[3].astype(BF16), cross, preferred_element_type=F32)
        for b in range(4):
            rims = jnp.where(
                sub == 0,
                -0.5 * gy_ref[b, 8:9],
                jnp.where(sub == 1, 0.5 * gy_ref[b, T + 7 : T + 8], spill[:, lanes(b)]),
            )
            out_ref[0, T : T + SPILL, lanes(b)] = rims.astype(BF16)

    @pl.when((slot_odd == 1) & jnp.logical_not(any_used))
    def _():
        out_ref[...] = jnp.zeros_like(out_ref)


SCRATCH = [
    pltpu.VMEM((4, T + 16, 128), F32),
    pltpu.VMEM((2, T, 128), F32),
    pltpu.VMEM((4, T, 128), F32),
    pltpu.VMEM((4, T, 128), F32),
    pltpu.VMEM((4, T, 128), F32),
    pltpu.VMEM((4, T, 128), F32),
    pltpu.VMEM((4, T, 128), F32),
    pltpu.VMEM((4, T + 16, 128), F32),
    pltpu.VMEM((C, C), BF16),
    pltpu.VMEM((3, C, 128), F32),
    pltpu.VMEM((3, C + 16, 128), F32),
    pltpu.VMEM((C, C), BF16),
    pltpu.VMEM((3, C, 128), F32),
]


def run_tiles(tiles, resample, observed, used, image, row_off, col_off, sun, gain):
    count = tiles.shape[0]
    grid_spec = pltpu.PrefetchScalarGridSpec(
        num_scalar_prefetch=6,
        grid=(2 * count,),
        in_specs=[
            pl.BlockSpec((1, T + EXTRA, T), lambda i, *s: (i // 2, 0, 0)),
            pl.BlockSpec((1, 2, C, C), lambda i, u, m, *s: (m[i], 0, 0, 0)),
            pl.BlockSpec((1, C, C), lambda i, u, m, *s: (m[i], 0, 0)),
        ],
        out_specs=[
            pl.BlockSpec((1, T + SPILL, T), lambda i, *s: (i // 2, 0, 0)),
            pl.BlockSpec((16, 5, 8, C), lambda i, *s: (0, 0, 0, 0)),
        ],
        scratch_shapes=SCRATCH,
    )
    return pl.pallas_call(
        tile_kernel,
        grid_spec=grid_spec,
        out_shape=[
            jax.ShapeDtypeStruct((count, T + SPILL, T), BF16),
            jax.ShapeDtypeStruct((16, 5, 8, C), F32),
        ],
        compiler_params=pltpu.CompilerParams(dimension_semantics=("arbitrary",)),
        name="tiles",
    )(used, image, row_off, col_off, sun, gain, tiles, resample, observed)


def next_images(used, image):
    count = used.shape[0]
    ids = jnp.arange(count, dtype=I32)
    is_used = used == 1
    ahead = jnp.min(
        jnp.where(is_used[None, :] & (ids[None, :] >= ids[:, None]), ids[None, :], count), axis=1
    )
    last = jnp.maximum(jnp.max(jnp.where(is_used, ids, -1)), 0)
    at = jnp.where(ahead < count, ahead, last)
    return jnp.sum(jnp.where(at[:, None] == ids[None, :], image[None, :], 0), axis=1)


def sun_vectors(azimuth, elevation):
    return jnp.stack(
        [
            jnp.cos(elevation) * jnp.cos(azimuth),
            jnp.cos(elevation) * jnp.sin(azimuth),
            jnp.sin(elevation),
        ]
    )


def laplace(padded):
    return (
        padded[:-2, 1:-1]
        + padded[2:, 1:-1]
        + padded[1:-1, :-2]
        + padded[1:-1, 2:]
        - 4.0 * padded[1:-1, 1:-1]
    )


def shifted(value, axis, up):
    count = lax.axis_size(axis)
    pairs = [(i, i + 1) for i in range(count - 1)]
    return lax.ppermute(value, axis, pairs if up else [(b, a) for a, b in pairs])


def quantize(heights):
    return jnp.round(heights * H_SCALE).astype(I32)


def smoothness(heights, top, bottom):
    tall = jnp.concatenate([top, heights, bottom], axis=0)
    left = shifted(tall[:, -2:], "dx", True)
    right = shifted(tall[:, :2], "dx", False)
    wide = jnp.concatenate([left, tall, right], axis=1)
    field = laplace(wide)
    rows, cols = heights.shape
    row_ids = jnp.arange(rows + 2)
    col_ids = jnp.arange(cols + 2)
    row_keep = ~(
        (row_ids == 0) & (lax.axis_index("dy") == 0)
        | (row_ids == rows + 1) & (lax.axis_index("dy") == lax.axis_size("dy") - 1)
    )
    col_keep = ~(
        (col_ids == 0) & (lax.axis_index("dx") == 0)
        | (col_ids == cols + 1) & (lax.axis_index("dx") == lax.axis_size("dx") - 1)
    )
    return SMOOTHING_WEIGHT * laplace(jnp.where(row_keep[:, None] & col_keep[None, :], field, 0.0))


def finish_sums(parts):
    ids = jnp.arange(C, dtype=F32)
    coord = (ids - 0.5 * (C - 1)) / C
    edge = jnp.where((ids == 0) | (ids == C - 1), 1.0, 0.5)
    start = (jnp.arange(8, dtype=F32) - 0.5 * (C - 1)) / C
    x_sum, x_row, y_sum, y_row, e_sum = (parts[:, n] for n in range(5))
    x_v = x_row / C + x_sum * start[None, :, None]
    y_v = y_row / C + y_sum * start[None, :, None]

    def total(v):
        return jnp.sum(v, axis=(1, 2))

    pose = [
        total(x_sum * edge),
        total(x_sum * (edge * coord)),
        total(x_v * edge),
        total(y_sum) * 0.5,
        total(y_sum * coord) * 0.5,
        total(y_v) * 0.5,
    ]
    return jnp.concatenate(
        [jnp.stack(pose, axis=-1) / C, (total(e_sum) / (C * C))[:, None]], axis=-1
    )


def per_device(
    heights, albedo, observed, resample, exposure, sun_azimuth, sun_elevation, send_plan, recv_plan
):
    offsets = send_plan[0, 0, 0:2].reshape(2, 16, 2).transpose(1, 0, 2)
    offsets = lax.all_to_all(offsets, "dy", split_axis=0, concat_axis=0, tiled=True)
    row_off = offsets[:, 0].reshape(-1)
    col_off = offsets[:, 1].reshape(-1)
    slots = jnp.arange(32, dtype=I32)
    match = recv_plan[0, 0][None, :] == slots[:, None]
    used = jnp.any(match, axis=1).astype(I32)
    image = jnp.sum(jnp.where(match, jnp.arange(16, dtype=I32)[None, :], 0), axis=1)
    image = next_images(used, image)
    sun = sun_vectors(sun_azimuth[0], sun_elevation[0]).reshape(-1)
    gain = jnp.exp(exposure[0])

    top = shifted(heights[-2:], "dy", True)
    bottom = shifted(heights[:2], "dy", False)
    left = shifted(heights[:, -1], "dx", True)
    right = shifted(heights[:, 0], "dx", False)
    rims = jnp.stack(
        [
            pack(quantize(left), quantize(right)),
            pack(quantize(top[1]), jnp.zeros_like(quantize(top[1]))),
            pack(quantize(bottom[0]), jnp.zeros_like(quantize(bottom[0]))),
        ]
    )
    words = pack(quantize(heights), jnp.round((albedo - 1.0) * A_SCALE).astype(I32))
    words = jnp.concatenate([words, rims, jnp.zeros((EXTRA - 3, T), I32)], axis=0)
    tiles = lax.all_gather(words, "dy", axis=0)
    smooth = smoothness(heights, top, bottom)
    outs, parts = run_tiles(
        tiles, resample, observed, used, image, row_off, col_off, sun, gain
    )
    crop_sums = finish_sums(parts)
    arrived = lax.all_to_all(crop_sums[:, None], "dy", split_axis=0, concat_axis=0, tiled=True)
    camera = arrived.sum(axis=0)
    own = lax.psum_scatter(outs, "dy", scatter_dimension=0).astype(F32)
    from_below = shifted(own[T], "dy", False)
    from_above = shifted(own[T + 1], "dy", True)
    from_right = shifted(own[T + 2], "dx", False)
    from_left = shifted(own[T + 3], "dx", True)
    row_ids = lax.broadcasted_iota(I32, (T, T), 0)
    col_ids = lax.broadcasted_iota(I32, (T, T), 1)
    data = own[:T]
    data = data + jnp.where(row_ids == T - 1, from_below[None, :], 0.0)
    data = data + jnp.where(row_ids == 0, from_above[None, :], 0.0)
    data = data + jnp.where(col_ids == T - 1, from_right[:, None], 0.0)
    data = data + jnp.where(col_ids == 0, from_left[:, None], 0.0)
    return (data + smooth, camera[None])


def solution(mesh):
    placed = (
        P("dy", "dx"),
        P("dy", "dx"),
        P(("dy", "dx"), None, None),
        P(("dy", "dx"), None, None, None),
        P("dx", None),
        P("dx", None),
        P("dx", None),
        P("dy", "dx", None, None),
        P("dy", "dx", None),
    )
    return jax.shard_map(
        per_device,
        mesh=mesh,
        in_specs=placed,
        out_specs=(P("dy", "dx"), P("dx", "dy", None)),
        check_vma=False,
    )
```

```python
import functools

import jax
import jax.numpy as jnp
from jax import lax
from jax.experimental import pallas as pl
from jax.experimental.pallas import tpu as pltpu
from jax.sharding import PartitionSpec as P


SMOOTHING_WEIGHT = 0.02
H_SCALE = 8191.0
A_SCALE = 65534.0
T = 512
C = 384
HALF = 256
PIECE = 264
BACK = 272
CH = 32
F32 = jnp.float32
BF16 = jnp.bfloat16
I32 = jnp.int32


def pack(high, low):
    return lax.shift_left(high, 16) | (low & 0xFFFF)


def high_of(word):
    return lax.shift_right_arithmetic(word, 16).astype(F32)


def low_of(word):
    return lax.shift_right_arithmetic(lax.shift_left(word, 16), 16).astype(F32)


def tile_kernel(pieces, operands, *refs):
    used, image, row_off, col_off, sun, gain = refs[:6]
    tiles = refs[6 : 6 + operands]
    (
        res_ref, obs_ref,
        out_ref, sums_ref,
        rim, hbuf, hcol, sx_ref, sy_ref, w_ref, r2_ref, gx_ref, gy_ref,
        shaded, tbuf, pbuf, weighted, grad,
    ) = refs[6 + operands :]
    step = pl.program_id(0)
    first = (step // 2) * 2
    slot_odd = step % 2
    mine = used[step] == 1
    any_used = used[first] + used[first + 1] > 0
    lane = lax.broadcasted_iota(I32, (CH, 128), 1)
    at_first = lane == 0
    at_last = lane == 127

    def lanes(b):
        return slice(128 * b, 128 * (b + 1))

    @pl.when(step == 0)
    def _():
        sums_ref[...] = jnp.zeros_like(sums_ref)

    for t, sources in enumerate(pieces):

        @pl.when((step == 2 * t) & any_used)
        def _(sources=sources):
            for half, (operand, at) in enumerate(sources):
                ref = tiles[operand]
                rim[half] = ref[at, HALF:PIECE]

                def unpack(k, _, ref=ref, at=at, half=half):
                    base = pl.multiple_of(k * CH, CH)
                    to = pl.multiple_of(base + HALF * half, CH)
                    for b in range(4):
                        words = ref[at, pl.ds(base, CH), lanes(b)]
                        hbuf[b, pl.ds(to + 8, CH)] = high_of(words)
                        w_ref[b, pl.ds(to, CH)] = low_of(words) * (1.0 / A_SCALE) + 1.0
                    return 0

                lax.fori_loop(0, HALF // CH, unpack, 0)

    @pl.when((slot_odd == 0) & any_used)
    def _():
        row_id = lax.broadcasted_iota(I32, (32, 256), 0)
        side = lax.broadcasted_iota(I32, (32, 256), 1) // 128
        scale = jnp.where(row_id == 16 * side, 256.0, 0.0) + jnp.where(
            row_id == 16 * side + 8, 1.0, 0.0
        )
        for half in range(2):
            words = rim[half, :, 0:HALF]
            high = lax.shift_right_arithmetic(words, 16)
            low = lax.shift_right_arithmetic(lax.shift_left(words, 16), 16)
            parts = jnp.concatenate(
                [
                    lax.shift_right_arithmetic(high, 8),
                    high & 255,
                    lax.shift_right_arithmetic(low, 8),
                    low & 255,
                ],
                axis=0,
            ).astype(F32).astype(BF16)
            columns = lax.dot_general(
                parts, scale.astype(BF16), (((0,), (0,)), ((), ())), preferred_element_type=F32
            )
            for side_id in range(2):
                hcol[side_id, HALF * half : HALF * (half + 1)] = columns[:, lanes(side_id)]
        top = high_of(rim[0])
        bottom = high_of(rim[1])
        for b in range(4):
            hbuf[b, 7:8] = top[1:2, lanes(b)]
            hbuf[b, T + 8 : T + 9] = bottom[1:2, lanes(b)]
            gy_ref[b, 0:8] = jnp.zeros((8, 128), F32)
            gy_ref[b, T + 8 : T + 16] = jnp.zeros((8, 128), F32)

        def slope(k, _):
            base = pl.multiple_of(k * CH, CH)
            rows = pl.ds(base, CH)
            here = [hbuf[b, pl.ds(base + 8, CH)] for b in range(4)]
            right_turn = [pltpu.roll(h, 1, 1) for h in here]
            left_turn = [pltpu.roll(h, 127, 1) for h in here]
            before = [hcol[0, rows]] + right_turn[:3]
            after = left_turn[1:] + [hcol[1, rows]]
            for b in range(4):
                left = jnp.where(at_first, before[b], right_turn[b])
                right = jnp.where(at_last, after[b], left_turn[b])
                sx = (right - left) * (0.5 / H_SCALE)
                sy = (hbuf[b, pl.ds(base + 9, CH)] - hbuf[b, pl.ds(base + 7, CH)]) * (
                    0.5 / H_SCALE
                )
                r = lax.rsqrt(1.0 + sx * sx + sy * sy)
                sx_ref[b, rows] = sx
                sy_ref[b, rows] = sy
                w_ref[b, rows] = w_ref[b, rows] * r
                r2_ref[b, rows] = r * r
                gx_ref[b, rows] = jnp.zeros((CH, 128), F32)
                gy_ref[b, pl.ds(base + 8, CH)] = jnp.zeros((CH, 128), F32)
            return 0

        lax.fori_loop(0, T // CH, slope, 0, unroll=2)

    @pl.when(mine)
    def _():
        m = image[step]
        oy = pl.multiple_of(row_off[step], 128)
        ob = col_off[step] // 128
        s1 = sun[m]
        s2 = sun[16 + m]
        s3 = sun[32 + m]
        e = gain[m]

        def shade(k, _):
            base = pl.multiple_of(k * CH, CH)
            rows = pl.ds(pl.multiple_of(oy + base, CH), CH)
            for b in range(3):
                q = s3 - s1 * sx_ref[ob + b, rows] - s2 * sy_ref[ob + b, rows]
                shaded[pl.ds(base, CH), lanes(b)] = (w_ref[ob + b, rows] * q).astype(BF16)
                tbuf[b, pl.ds(base, CH)] = q * r2_ref[ob + b, rows]
            return 0

        lax.fori_loop(0, C // CH, shade, 0, unroll=2)
        row_mat = res_ref[0, 0]
        col_mat = res_ref[0, 1]
        first_pass = jnp.dot(row_mat, shaded[...], preferred_element_type=F32).astype(BF16)
        predicted = e * lax.dot_general(
            first_pass, col_mat, (((1,), (1,)), ((), ())), preferred_element_type=F32
        )
        for b in range(3):
            pbuf[b, 8 : 8 + C] = predicted[:, lanes(b)]
            pbuf[b, 7:8] = 2.0 * pbuf[b, 8:9] - pbuf[b, 9:10]
            pbuf[b, C + 8 : C + 9] = 2.0 * pbuf[b, C + 7 : C + 8] - pbuf[b, C + 6 : C + 7]

        def add_up(v, base, total, by_row):
            groups = [v[8 * g : 8 * g + 8] for g in range(CH // 8)]
            tail = groups[-1]
            lead = tail
            for g in range(CH // 8 - 2, 0, -1):
                tail = groups[g] + tail
                lead = lead + tail
            tail = groups[0] + tail
            return total + tail, by_row + lead * 8.0 + tail * base

        def terms(k, carry):
            base = pl.multiple_of(k * CH, CH)
            at = base.astype(F32)
            rows = pl.ds(base, CH)
            here = [pbuf[b, pl.ds(base + 8, CH)] for b in range(3)]
            right_turn = [pltpu.roll(p, 1, 1) for p in here]
            left_turn = [pltpu.roll(p, 127, 1) for p in here]
            before = [here[0]] + right_turn[:2]
            after = left_turn[1:] + [here[2]]
            result = []
            for b in range(3):
                a_x, a_xg, a_y, a_yg, a_e = carry[b]
                p = here[b]
                residual = p - obs_ref[0, rows, lanes(b)].astype(F32)
                weighted[rows, lanes(b)] = (e * residual).astype(BF16)
                left = jnp.where(at_first, before[b], right_turn[b])
                right = jnp.where(at_last, after[b], left_turn[b])
                a_x, a_xg = add_up(residual * (right - left), at, a_x, a_xg)
                down = pbuf[b, pl.ds(base + 9, CH)]
                up = pbuf[b, pl.ds(base + 7, CH)]
                a_y, a_yg = add_up(residual * (down - up), at, a_y, a_yg)
                squares = residual * p
                a_e = a_e + squares.reshape(CH // 8, 8, 128).sum(axis=0)
                result.append((a_x, a_xg, a_y, a_yg, a_e))
            return tuple(result)

        zero = jnp.zeros((8, 128), F32)
        parts = lax.fori_loop(0, C // CH, terms, ((zero,) * 5,) * 3, unroll=3)
        for b in range(3):
            for n in range(5):
                sums_ref[m, n, :, lanes(b)] = parts[b][n]
        back_pass = lax.dot_general(
            row_mat, weighted[...], (((0,), (0,)), ((), ())), preferred_element_type=F32
        ).astype(BF16)
        crop_grad = jnp.dot(back_pass, col_mat, preferred_element_type=F32)
        for b in range(3):
            grad[b] = crop_grad[:, lanes(b)]

        def pull(k, _):
            base = pl.multiple_of(k * CH, CH)
            rows = pl.ds(pl.multiple_of(oy + base, CH), CH)
            rows_y = pl.ds(pl.multiple_of(oy + base + 8, 8), CH)
            for b in range(3):
                t = tbuf[b, pl.ds(base, CH)]
                wg = w_ref[ob + b, rows] * grad[b, pl.ds(base, CH)]
                gx_ref[ob + b, rows] = gx_ref[ob + b, rows] - wg * (s1 + t * sx_ref[ob + b, rows])
                gy_ref[ob + b, rows_y] = gy_ref[ob + b, rows_y] - wg * (
                    s2 + t * sy_ref[ob + b, rows]
                )
            return 0

        lax.fori_loop(0, C // CH, pull, 0, unroll=2)

    @pl.when((slot_odd == 1) & any_used)
    def _():
        def stencil(k, _):
            base = pl.multiple_of(k * CH, CH)
            rows = pl.ds(base, CH)
            half = k // (HALF // CH)
            to = pl.ds(pl.multiple_of(base - half * HALF, CH), CH)
            here = [gx_ref[b, rows] for b in range(4)]
            right_turn = [pltpu.roll(g, 1, 1) for g in here]
            left_turn = [pltpu.roll(g, 127, 1) for g in here]
            blank = jnp.zeros((CH, 128), F32)
            before = [blank] + right_turn[:3]
            after = left_turn[1:] + [blank]
            for b in range(4):
                left = jnp.where(at_first, before[b], right_turn[b])
                right = jnp.where(at_last, after[b], left_turn[b])
                up = gy_ref[b, pl.ds(base + 7, CH)]
                down = gy_ref[b, pl.ds(base + 9, CH)]
                total = (left - right) + (up - down)
                out_ref[0, half, to, lanes(b)] = (0.5 * total).astype(BF16)
            return 0

        lax.fori_loop(0, T // CH, stencil, 0, unroll=2)
        sub = lax.broadcasted_iota(I32, (16, 128), 0)
        lane16 = lax.broadcasted_iota(I32, (16, 128), 1)
        pick_low = jnp.where((sub == 1) & (lane16 == 0), -0.5, 0.0).astype(BF16)
        pick_high = jnp.where((sub == 2) & (lane16 == 127), 0.5, 0.0).astype(BF16)
        cross = (((1,), (1,)), ((), ()))
        for half in range(2):
            rows = slice(HALF * half, HALF * (half + 1))
            spill = lax.dot_general(
                pick_low, gx_ref[0, rows].astype(BF16), cross, preferred_element_type=F32
            ) + lax.dot_general(
                pick_high, gx_ref[3, rows].astype(BF16), cross, preferred_element_type=F32
            )
            for b in range(4):
                edge = 0.5 * gy_ref[b, T + 7 : T + 8] if half else -0.5 * gy_ref[b, 8:9]
                rest = spill[:, lanes(b)] if b < 2 else jnp.zeros((16, 128), F32)
                out_ref[0, half, HALF:BACK, lanes(b)] = jnp.where(sub == 0, edge, rest).astype(
                    BF16
                )

    @pl.when((slot_odd == 1) & jnp.logical_not(any_used))
    def _():
        out_ref[...] = jnp.zeros_like(out_ref)


SCRATCH = [
    pltpu.VMEM((2, PIECE - HALF, T), I32),
    pltpu.VMEM((4, T + 16, 128), F32),
    pltpu.VMEM((2, T, 128), F32),
    pltpu.VMEM((4, T, 128), F32),
    pltpu.VMEM((4, T, 128), F32),
    pltpu.VMEM((4, T, 128), F32),
    pltpu.VMEM((4, T, 128), F32),
    pltpu.VMEM((4, T, 128), F32),
    pltpu.VMEM((4, T + 16, 128), F32),
    pltpu.VMEM((C, C), BF16),
    pltpu.VMEM((3, C, 128), F32),
    pltpu.VMEM((3, C + 16, 128), F32),
    pltpu.VMEM((C, C), BF16),
    pltpu.VMEM((3, C, 128), F32),
]


def run_tiles(arrays, pieces, resample, observed, plan, sun, gain):
    used, image, row_off, col_off = plan
    count = len(pieces)
    tile_specs = [pl.BlockSpec(v.shape, lambda i, *s: (0, 0, 0)) for v in arrays]
    grid_spec = pltpu.PrefetchScalarGridSpec(
        num_scalar_prefetch=6,
        grid=(2 * count,),
        in_specs=tile_specs
        + [
            pl.BlockSpec((1, 2, C, C), lambda i, u, m, *s: (m[i], 0, 0, 0)),
            pl.BlockSpec((1, C, C), lambda i, u, m, *s: (m[i], 0, 0)),
        ],
        out_specs=[
            pl.BlockSpec((1, 2, BACK, T), lambda i, *s: (i // 2, 0, 0, 0)),
            pl.BlockSpec((16, 5, 8, C), lambda i, *s: (0, 0, 0, 0)),
        ],
        scratch_shapes=SCRATCH,
    )
    return pl.pallas_call(
        functools.partial(tile_kernel, pieces, len(arrays)),
        grid_spec=grid_spec,
        out_shape=[
            jax.ShapeDtypeStruct((count, 2, BACK, T), BF16),
            jax.ShapeDtypeStruct((16, 5, 8, C), F32),
        ],
        compiler_params=pltpu.CompilerParams(dimension_semantics=("arbitrary",)),
        cost_estimate=pl.CostEstimate(
            flops=count * 8 * C * C * C, bytes_accessed=count * 8_000_000, transcendentals=0
        ),
    )(used, image, row_off, col_off, sun, gain, *arrays, resample, observed)


def around(step_x, step_y):
    return [
        (4 * y + x, 4 * ((y + step_y) % 4) + (x + step_x) % 4) for y in range(4) for x in range(4)
    ]


STEPS = {"x+": around(1, 0), "x-": around(-1, 0), "y+": around(0, 1), "y-": around(0, -1)}
NEAR = [(0, 0), (-1, 0), (1, 0), (0, -1), (0, 1)]
MIDDLE = [(-1, -1), (-1, 1), (1, -1), (1, 1), (2, 0), (0, 2)]
FAR = [(2, -1), (2, 1), (-1, 2), (1, 2)]
LAST = [(2, 2)]


def send(messages):
    return {way: lax.ppermute(v, "dy", STEPS[way]) for way, v in messages.items()}


def send_middle(near):
    a = {k: v[0] for k, v in near.items()}
    b = {k: v[1] for k, v in near.items()}
    return send(
        {
            "x+": jnp.stack([a["x+"], b["y+"], b["y-"]]),
            "x-": jnp.stack([b["x-"], b["y+"], b["y-"]]),
            "y+": jnp.stack([a["y+"], a["x+"], a["x-"]]),
            "y-": jnp.stack([b["y-"], a["x+"], a["x-"]]),
        }
    )


def send_far(middle):
    return send(
        {
            "x+": jnp.stack([middle["y+"][1], middle["y-"][1]]),
            "x-": middle["x-"][1:3],
            "y+": middle["y+"][1:3],
            "y-": jnp.stack([middle["x+"][2], middle["x-"][2]]),
        }
    )


def send_last(far, cut):
    got = send(
        {
            "x+": far["y+"][0, :cut],
            "x-": far["y+"][1, cut:],
            "y+": far["x-"][0, :cut],
            "y-": far["x-"][1, cut:],
        }
    )
    return jnp.stack(
        [
            jnp.concatenate([got["x+"], got["x-"]]),
            jnp.concatenate([got["y+"], got["y-"]]),
        ]
    )


def return_sums(near, middle, far, last, cut):
    def wide(v):
        return v.astype(F32)

    def slim(v):
        return v.astype(BF16)

    got = send(
        {
            "x-": last[0, 0, :cut],
            "x+": last[0, 0, cut:],
            "y-": last[0, 1, :cut],
            "y+": last[0, 1, cut:],
        }
    )

    def top_added(v, extra):
        return jnp.concatenate([slim(wide(v[:cut]) + wide(extra)), v[cut:]])

    def low_added(v, extra):
        return jnp.concatenate([v[:cut], slim(wide(v[cut:]) + wide(extra))])

    got = send(
        {
            "x-": far[0:2, 0],
            "x+": jnp.stack([top_added(far[0, 1], got["y-"]), low_added(far[1, 1], got["y+"])]),
            "y-": jnp.stack([top_added(far[2, 0], got["x-"]), low_added(far[3, 0], got["x+"])]),
            "y+": far[2:4, 1],
        }
    )
    a_mm = slim(wide(middle[0, 0]) + wide(got["x-"][0]) + wide(got["y-"][0]))
    a_mp = slim(wide(middle[1, 0]) + wide(got["x-"][1]))
    b_mp = slim(wide(middle[1, 1]) + wide(got["y+"][0]))
    a_pm = slim(wide(middle[2, 0]) + wide(got["y-"][1]))
    b_pm = slim(wide(middle[2, 1]) + wide(got["x+"][0]))
    b_pp = slim(wide(middle[3, 1]) + wide(got["x+"][1]) + wide(got["y+"][1]))
    got = send(
        {
            "x-": jnp.stack([middle[4, 0], middle[0, 1], b_mp]),
            "x+": jnp.stack([middle[4, 1], b_pm, b_pp]),
            "y-": jnp.stack([middle[5, 0], a_mm, a_pm]),
            "y+": jnp.stack([middle[5, 1], a_mp, middle[3, 0]]),
        }
    )
    xm, xp, ym, yp = (wide(got[k]) for k in ("x-", "x+", "y-", "y+"))
    mine = wide(near)
    got = send(
        {
            "x-": slim(jnp.stack([mine[1, 0] + xm[0] + ym[1] + yp[1], mine[1, 1]])),
            "x+": slim(jnp.stack([mine[2, 0] + ym[2] + yp[2], mine[2, 1] + xp[0]])),
            "y-": slim(jnp.stack([mine[3, 0] + ym[0], mine[3, 1] + xm[1] + xp[1]])),
            "y+": slim(jnp.stack([mine[4, 0], mine[4, 1] + xm[2] + xp[2] + yp[0]])),
        }
    )
    return mine[0] + wide(got["x-"]) + wide(got["x+"]) + wide(got["y-"]) + wide(got["y+"])


def next_images(used, image):
    count = used.shape[0]
    ids = jnp.arange(count, dtype=I32)
    is_used = used == 1
    ahead = jnp.min(
        jnp.where(is_used[None, :] & (ids[None, :] >= ids[:, None]), ids[None, :], count), axis=1
    )
    last = jnp.maximum(jnp.max(jnp.where(is_used, ids, -1)), 0)
    at = jnp.where(ahead < count, ahead, last)
    return jnp.sum(jnp.where(at[:, None] == ids[None, :], image[None, :], 0), axis=1)


def sun_vectors(azimuth, elevation):
    return jnp.stack(
        [
            jnp.cos(elevation) * jnp.cos(azimuth),
            jnp.cos(elevation) * jnp.sin(azimuth),
            jnp.sin(elevation),
        ]
    )


def laplace(padded):
    return (
        padded[:-2, 1:-1]
        + padded[2:, 1:-1]
        + padded[1:-1, :-2]
        + padded[1:-1, 2:]
        - 4.0 * padded[1:-1, 1:-1]
    )


def shifted(value, axis, up):
    count = lax.axis_size(axis)
    pairs = [(i, i + 1) for i in range(count - 1)]
    return lax.ppermute(value, axis, pairs if up else [(b, a) for a, b in pairs])


def quantize(heights):
    return jnp.round(heights * H_SCALE).astype(I32)


def smoothness(heights, top, bottom):
    tall = jnp.concatenate([top, heights, bottom], axis=0)
    left = shifted(tall[:, -2:], "dx", True)
    right = shifted(tall[:, :2], "dx", False)
    wide = jnp.concatenate([left, tall, right], axis=1)
    field = laplace(wide)
    rows, cols = heights.shape
    row_ids = jnp.arange(rows + 2)
    col_ids = jnp.arange(cols + 2)
    row_keep = ~(
        (row_ids == 0) & (lax.axis_index("dy") == 0)
        | (row_ids == rows + 1) & (lax.axis_index("dy") == lax.axis_size("dy") - 1)
    )
    col_keep = ~(
        (col_ids == 0) & (lax.axis_index("dx") == 0)
        | (col_ids == cols + 1) & (lax.axis_index("dx") == lax.axis_size("dx") - 1)
    )
    return SMOOTHING_WEIGHT * laplace(jnp.where(row_keep[:, None] & col_keep[None, :], field, 0.0))


def finish_sums(parts):
    ids = jnp.arange(C, dtype=F32)
    coord = (ids - 0.5 * (C - 1)) / C
    edge = jnp.where((ids == 0) | (ids == C - 1), 1.0, 0.5)
    start = (jnp.arange(8, dtype=F32) - 0.5 * (C - 1)) / C
    x_sum, x_row, y_sum, y_row, e_sum = (parts[:, n] for n in range(5))
    x_v = x_row / C + x_sum * start[None, :, None]
    y_v = y_row / C + y_sum * start[None, :, None]

    def total(v):
        return jnp.sum(v, axis=(1, 2))

    pose = [
        total(x_sum * edge),
        total(x_sum * (edge * coord)),
        total(x_v * edge),
        total(y_sum) * 0.5,
        total(y_sum * coord) * 0.5,
        total(y_v) * 0.5,
    ]
    return jnp.concatenate(
        [jnp.stack(pose, axis=-1) / C, (total(e_sum) / (C * C))[:, None]], axis=-1
    )


def per_device(
    heights, albedo, observed, resample, exposure, sun_azimuth, sun_elevation, send_plan, recv_plan
):
    offsets = send_plan[0, 0, 0:2].reshape(2, 16, 2).transpose(1, 0, 2)
    offsets = lax.all_to_all(offsets, "dy", split_axis=0, concat_axis=0, tiled=True)
    row_off = offsets[:, 0].reshape(-1)
    col_off = offsets[:, 1].reshape(-1)
    slots = jnp.arange(32, dtype=I32)
    match = recv_plan[0, 0][None, :] == slots[:, None]
    used = jnp.any(match, axis=1).astype(I32)
    image = jnp.sum(jnp.where(match, jnp.arange(16, dtype=I32)[None, :], 0), axis=1)
    table = jnp.stack([used, image, row_off, col_off])
    relative = jnp.array(NEAR + MIDDLE + FAR + LAST, I32)
    place = lax.axis_index("dy")
    tile_ids = ((place // 4 + relative[:, 1]) % 4) * 4 + (place % 4 + relative[:, 0]) % 4
    slot_ids = (2 * tile_ids[:, None] + jnp.arange(2, dtype=I32)[None, :]).reshape(-1)
    table = jnp.sum(
        jnp.where(slot_ids[None, :, None] == slots[None, None, :], table[:, None, :], 0), axis=2
    )

    def plan_of(first, count):
        part = table[:, 2 * first : 2 * (first + count)]
        return part[0], next_images(part[0], part[1]), part[2], part[3]

    sun = sun_vectors(sun_azimuth[0], sun_elevation[0]).reshape(-1)
    gain = jnp.exp(exposure[0])

    top = shifted(heights[-2:], "dy", True)
    bottom = shifted(heights[:2], "dy", False)
    left = shifted(heights[:, -1], "dx", True)
    right = shifted(heights[:, 0], "dx", False)
    sides = pack(quantize(left), quantize(right)).reshape(2, 1, HALF)
    sides = jnp.concatenate([sides, jnp.zeros((2, 1, T - HALF), I32)], axis=2)
    ends = pack(quantize(jnp.stack([top[1:2], bottom[0:1]])), 0)
    words = pack(quantize(heights), jnp.round((albedo - 1.0) * A_SCALE).astype(I32))
    words = jnp.concatenate(
        [words.reshape(2, HALF, T), sides, ends, jnp.zeros((2, PIECE - HALF - 2, T), I32)], axis=1
    )
    near = send({way: words for way in STEPS})
    middle = send_middle(near)
    far = send_far(middle)
    last = send_last(far, 136)
    order = ["x+", "x-", "y+", "y-"]
    whole = ((0, 0), (0, 1))
    out_near, parts = run_tiles(
        [words] + [near[k] for k in order],
        [((n, 0), (n, 1)) for n in range(5)],
        resample, observed, plan_of(0, 5), sun, gain,
    )
    out_middle, more = run_tiles(
        [middle[k] for k in order],
        [
            ((2, 1), (0, 1)),
            ((3, 1), (0, 2)),
            ((2, 2), (1, 1)),
            ((3, 2), (1, 2)),
            ((0, 0), (1, 0)),
            ((2, 0), (3, 0)),
        ],
        resample, observed, plan_of(5, 6), sun, gain,
    )
    parts = parts + more
    out_far, more = run_tiles(
        [far[k] for k in order],
        [((0, 0), (1, 0)), ((0, 1), (1, 1)), ((2, 0), (3, 0)), ((2, 1), (3, 1))],
        resample, observed, plan_of(11, 4), sun, gain,
    )
    parts = parts + more
    out_last, more = run_tiles([last], [whole], resample, observed, plan_of(15, 1), sun, gain)
    parts = parts + more
    smooth = smoothness(heights, top, bottom)
    crop_sums = finish_sums(parts)
    arrived = lax.all_to_all(crop_sums[:, None], "dy", split_axis=0, concat_axis=0, tiled=True)
    camera = arrived.sum(axis=0)
    own = return_sums(out_near, out_middle, out_far, out_last, 144)
    from_below = shifted(own[0, HALF], "dy", False)
    from_above = shifted(own[1, HALF], "dy", True)
    from_right = shifted(own[:, HALF + 1, :HALF].reshape(-1), "dx", False)
    from_left = shifted(own[:, HALF + 2, :HALF].reshape(-1), "dx", True)
    row_ids = lax.broadcasted_iota(I32, (T, T), 0)
    col_ids = lax.broadcasted_iota(I32, (T, T), 1)
    data = own[:, :HALF].reshape(T, T)
    data = data + jnp.where(row_ids == T - 1, from_below[None, :], 0.0)
    data = data + jnp.where(row_ids == 0, from_above[None, :], 0.0)
    data = data + jnp.where(col_ids == T - 1, from_right[:, None], 0.0)
    data = data + jnp.where(col_ids == 0, from_left[:, None], 0.0)
    return (data + smooth, camera[None])


def solution(mesh):
    placed = (
        P("dy", "dx"),
        P("dy", "dx"),
        P(("dy", "dx"), None, None),
        P(("dy", "dx"), None, None, None),
        P("dx", None),
        P("dx", None),
        P("dx", None),
        P("dy", "dx", None, None),
        P("dy", "dx", None),
    )

    return jax.shard_map(
        per_device,
        mesh=mesh,
        in_specs=placed,
        out_specs=(P("dy", "dx"), P("dx", "dy", None)),
        check_vma=False,
    )
```

```python
import functools

import jax
import jax.numpy as jnp
from jax import lax
from jax.experimental import pallas as pl
from jax.experimental.pallas import tpu as pltpu
from jax.sharding import PartitionSpec as P


SMOOTHING_WEIGHT = 0.02
H_SCALE = 8191.0
A_SCALE = 65534.0
T = 512
C = 384
HALF = 256
PIECE = 264
BACK = 272
CH = 32
F32 = jnp.float32
BF16 = jnp.bfloat16
I32 = jnp.int32


def pack(high, low):
    return lax.shift_left(high, 16) | (low & 0xFFFF)


def high_of(word):
    return lax.shift_right_arithmetic(word, 16).astype(F32)


def low_of(word):
    return lax.shift_right_arithmetic(lax.shift_left(word, 16), 16).astype(F32)


def tile_kernel(pieces, operands, *refs):
    used, image, row_off, col_off, sun, gain = refs[:6]
    tiles = refs[6 : 6 + operands]
    (
        res_ref, obs_ref,
        out_ref, sums_ref,
        rim, hbuf, hcol, sx_ref, sy_ref, w_ref, r2_ref, gx_ref, gy_ref,
        shaded, tbuf, pbuf, weighted, grad,
    ) = refs[6 + operands :]
    step = pl.program_id(0)
    first = (step // 2) * 2
    slot_odd = step % 2
    mine = used[step] == 1
    any_used = used[first] + used[first + 1] > 0
    lane = lax.broadcasted_iota(I32, (CH, 128), 1)
    at_first = lane == 0
    at_last = lane == 127

    def lanes(b):
        return slice(128 * b, 128 * (b + 1))

    @pl.when(step == 0)
    def _():
        sums_ref[...] = jnp.zeros_like(sums_ref)

    for t, sources in enumerate(pieces):

        @pl.when((step == 2 * t) & any_used)
        def _(sources=sources):
            for half, (operand, at) in enumerate(sources):
                ref = tiles[operand]
                rim[half] = ref[at, HALF:PIECE]

                def unpack(k, _, ref=ref, at=at, half=half):
                    base = pl.multiple_of(k * CH, CH)
                    to = pl.multiple_of(base + HALF * half, CH)
                    for b in range(4):
                        words = ref[at, pl.ds(base, CH), lanes(b)]
                        hbuf[b, pl.ds(to + 8, CH)] = high_of(words)
                        w_ref[b, pl.ds(to, CH)] = low_of(words) * (1.0 / A_SCALE) + 1.0
                    return 0

                lax.fori_loop(0, HALF // CH, unpack, 0)

    @pl.when((slot_odd == 0) & any_used)
    def _():
        row_id = lax.broadcasted_iota(I32, (32, 256), 0)
        side = lax.broadcasted_iota(I32, (32, 256), 1) // 128
        scale = jnp.where(row_id == 16 * side, 256.0, 0.0) + jnp.where(
            row_id == 16 * side + 8, 1.0, 0.0
        )
        for half in range(2):
            words = rim[half, :, 0:HALF]
            high = lax.shift_right_arithmetic(words, 16)
            low = lax.shift_right_arithmetic(lax.shift_left(words, 16), 16)
            parts = jnp.concatenate(
                [
                    lax.shift_right_arithmetic(high, 8),
                    high & 255,
                    lax.shift_right_arithmetic(low, 8),
                    low & 255,
                ],
                axis=0,
            ).astype(F32).astype(BF16)
            columns = lax.dot_general(
                parts, scale.astype(BF16), (((0,), (0,)), ((), ())), preferred_element_type=F32
            )
            for side_id in range(2):
                hcol[side_id, HALF * half : HALF * (half + 1)] = columns[:, lanes(side_id)]
        top = high_of(rim[0])
        bottom = high_of(rim[1])
        for b in range(4):
            hbuf[b, 7:8] = top[1:2, lanes(b)]
            hbuf[b, T + 8 : T + 9] = bottom[1:2, lanes(b)]
            gy_ref[b, 0:8] = jnp.zeros((8, 128), F32)
            gy_ref[b, T + 8 : T + 16] = jnp.zeros((8, 128), F32)

        def slope(k, _):
            base = pl.multiple_of(k * CH, CH)
            rows = pl.ds(base, CH)
            here = [hbuf[b, pl.ds(base + 8, CH)] for b in range(4)]
            right_turn = [pltpu.roll(h, 1, 1) for h in here]
            left_turn = [pltpu.roll(h, 127, 1) for h in here]
            before = [hcol[0, rows]] + right_turn[:3]
            after = left_turn[1:] + [hcol[1, rows]]
            for b in range(4):
                left = jnp.where(at_first, before[b], right_turn[b])
                right = jnp.where(at_last, after[b], left_turn[b])
                sx = (right - left) * (0.5 / H_SCALE)
                sy = (hbuf[b, pl.ds(base + 9, CH)] - hbuf[b, pl.ds(base + 7, CH)]) * (
                    0.5 / H_SCALE
                )
                r = lax.rsqrt(1.0 + sx * sx + sy * sy)
                sx_ref[b, rows] = sx
                sy_ref[b, rows] = sy
                w_ref[b, rows] = w_ref[b, rows] * r
                r2_ref[b, rows] = r * r
                gx_ref[b, rows] = jnp.zeros((CH, 128), F32)
                gy_ref[b, pl.ds(base + 8, CH)] = jnp.zeros((CH, 128), F32)
            return 0

        lax.fori_loop(0, T // CH, slope, 0, unroll=2)

    @pl.when(mine)
    def _():
        m = image[step]
        oy = pl.multiple_of(row_off[step], 128)
        ob = col_off[step] // 128
        s1 = sun[m]
        s2 = sun[16 + m]
        s3 = sun[32 + m]
        e = gain[m]

        def shade(k, _):
            base = pl.multiple_of(k * CH, CH)
            rows = pl.ds(pl.multiple_of(oy + base, CH), CH)
            for b in range(3):
                q = s3 - s1 * sx_ref[ob + b, rows] - s2 * sy_ref[ob + b, rows]
                shaded[pl.ds(base, CH), lanes(b)] = (w_ref[ob + b, rows] * q).astype(BF16)
                tbuf[b, pl.ds(base, CH)] = q * r2_ref[ob + b, rows]
            return 0

        lax.fori_loop(0, C // CH, shade, 0, unroll=2)
        row_mat = res_ref[0, 0]
        col_mat = res_ref[0, 1]
        first_pass = jnp.dot(row_mat, shaded[...], preferred_element_type=F32).astype(BF16)
        predicted = e * lax.dot_general(
            first_pass, col_mat, (((1,), (1,)), ((), ())), preferred_element_type=F32
        )
        for b in range(3):
            pbuf[b, 8 : 8 + C] = predicted[:, lanes(b)]
            pbuf[b, 7:8] = 2.0 * pbuf[b, 8:9] - pbuf[b, 9:10]
            pbuf[b, C + 8 : C + 9] = 2.0 * pbuf[b, C + 7 : C + 8] - pbuf[b, C + 6 : C + 7]

        def add_up(v, base, total, by_row):
            groups = [v[8 * g : 8 * g + 8] for g in range(CH // 8)]
            tail = groups[-1]
            lead = tail
            for g in range(CH // 8 - 2, 0, -1):
                tail = groups[g] + tail
                lead = lead + tail
            tail = groups[0] + tail
            return total + tail, by_row + lead * 8.0 + tail * base

        def terms(k, carry):
            base = pl.multiple_of(k * CH, CH)
            at = base.astype(F32)
            rows = pl.ds(base, CH)
            here = [pbuf[b, pl.ds(base + 8, CH)] for b in range(3)]
            right_turn = [pltpu.roll(p, 1, 1) for p in here]
            left_turn = [pltpu.roll(p, 127, 1) for p in here]
            before = [here[0]] + right_turn[:2]
            after = left_turn[1:] + [here[2]]
            result = []
            for b in range(3):
                a_x, a_xg, a_y, a_yg, a_e = carry[b]
                p = here[b]
                residual = p - obs_ref[0, rows, lanes(b)].astype(F32)
                weighted[rows, lanes(b)] = (e * residual).astype(BF16)
                left = jnp.where(at_first, before[b], right_turn[b])
                right = jnp.where(at_last, after[b], left_turn[b])
                a_x, a_xg = add_up(residual * (right - left), at, a_x, a_xg)
                down = pbuf[b, pl.ds(base + 9, CH)]
                up = pbuf[b, pl.ds(base + 7, CH)]
                a_y, a_yg = add_up(residual * (down - up), at, a_y, a_yg)
                squares = residual * p
                a_e = a_e + squares.reshape(CH // 8, 8, 128).sum(axis=0)
                result.append((a_x, a_xg, a_y, a_yg, a_e))
            return tuple(result)

        zero = jnp.zeros((8, 128), F32)
        parts = lax.fori_loop(0, C // CH, terms, ((zero,) * 5,) * 3, unroll=3)
        for b in range(3):
            for n in range(5):
                sums_ref[m, n, :, lanes(b)] = parts[b][n]
        back_pass = lax.dot_general(
            row_mat, weighted[...], (((0,), (0,)), ((), ())), preferred_element_type=F32
        ).astype(BF16)
        crop_grad = jnp.dot(back_pass, col_mat, preferred_element_type=F32)
        for b in range(3):
            grad[b] = crop_grad[:, lanes(b)]

        def pull(k, _):
            base = pl.multiple_of(k * CH, CH)
            rows = pl.ds(pl.multiple_of(oy + base, CH), CH)
            rows_y = pl.ds(pl.multiple_of(oy + base + 8, 8), CH)
            for b in range(3):
                t = tbuf[b, pl.ds(base, CH)]
                wg = w_ref[ob + b, rows] * grad[b, pl.ds(base, CH)]
                gx_ref[ob + b, rows] = gx_ref[ob + b, rows] - wg * (s1 + t * sx_ref[ob + b, rows])
                gy_ref[ob + b, rows_y] = gy_ref[ob + b, rows_y] - wg * (
                    s2 + t * sy_ref[ob + b, rows]
                )
            return 0

        lax.fori_loop(0, C // CH, pull, 0, unroll=2)

    @pl.when((slot_odd == 1) & any_used)
    def _():
        def stencil(k, _):
            base = pl.multiple_of(k * CH, CH)
            rows = pl.ds(base, CH)
            half = k // (HALF // CH)
            to = pl.ds(pl.multiple_of(base - half * HALF, CH), CH)
            here = [gx_ref[b, rows] for b in range(4)]
            right_turn = [pltpu.roll(g, 1, 1) for g in here]
            left_turn = [pltpu.roll(g, 127, 1) for g in here]
            blank = jnp.zeros((CH, 128), F32)
            before = [blank] + right_turn[:3]
            after = left_turn[1:] + [blank]
            for b in range(4):
                left = jnp.where(at_first, before[b], right_turn[b])
                right = jnp.where(at_last, after[b], left_turn[b])
                up = gy_ref[b, pl.ds(base + 7, CH)]
                down = gy_ref[b, pl.ds(base + 9, CH)]
                total = (left - right) + (up - down)
                out_ref[0, half, to, lanes(b)] = (0.5 * total).astype(BF16)
            return 0

        lax.fori_loop(0, T // CH, stencil, 0, unroll=2)
        sub = lax.broadcasted_iota(I32, (16, 128), 0)
        lane16 = lax.broadcasted_iota(I32, (16, 128), 1)
        pick_low = jnp.where((sub == 1) & (lane16 == 0), -0.5, 0.0).astype(BF16)
        pick_high = jnp.where((sub == 2) & (lane16 == 127), 0.5, 0.0).astype(BF16)
        cross = (((1,), (1,)), ((), ()))
        for half in range(2):
            rows = slice(HALF * half, HALF * (half + 1))
            spill = lax.dot_general(
                pick_low, gx_ref[0, rows].astype(BF16), cross, preferred_element_type=F32
            ) + lax.dot_general(
                pick_high, gx_ref[3, rows].astype(BF16), cross, preferred_element_type=F32
            )
            for b in range(4):
                edge = 0.5 * gy_ref[b, T + 7 : T + 8] if half else -0.5 * gy_ref[b, 8:9]
                rest = spill[:, lanes(b)] if b < 2 else jnp.zeros((16, 128), F32)
                out_ref[0, half, HALF:BACK, lanes(b)] = jnp.where(sub == 0, edge, rest).astype(
                    BF16
                )

    @pl.when((slot_odd == 1) & jnp.logical_not(any_used))
    def _():
        out_ref[...] = jnp.zeros_like(out_ref)


SCRATCH = [
    pltpu.VMEM((2, PIECE - HALF, T), I32),
    pltpu.VMEM((4, T + 16, 128), F32),
    pltpu.VMEM((2, T, 128), F32),
    pltpu.VMEM((4, T, 128), F32),
    pltpu.VMEM((4, T, 128), F32),
    pltpu.VMEM((4, T, 128), F32),
    pltpu.VMEM((4, T, 128), F32),
    pltpu.VMEM((4, T, 128), F32),
    pltpu.VMEM((4, T + 16, 128), F32),
    pltpu.VMEM((C, C), BF16),
    pltpu.VMEM((3, C, 128), F32),
    pltpu.VMEM((3, C + 16, 128), F32),
    pltpu.VMEM((C, C), BF16),
    pltpu.VMEM((3, C, 128), F32),
]


def run_tiles(arrays, pieces, resample, observed, plan, sun, gain):
    used, image, row_off, col_off = plan
    count = len(pieces)
    tile_specs = [pl.BlockSpec(v.shape, lambda i, *s: (0, 0, 0)) for v in arrays]
    grid_spec = pltpu.PrefetchScalarGridSpec(
        num_scalar_prefetch=6,
        grid=(2 * count,),
        in_specs=tile_specs
        + [
            pl.BlockSpec((1, 2, C, C), lambda i, u, m, *s: (m[i], 0, 0, 0)),
            pl.BlockSpec((1, C, C), lambda i, u, m, *s: (m[i], 0, 0)),
        ],
        out_specs=[
            pl.BlockSpec((1, 2, BACK, T), lambda i, *s: (i // 2, 0, 0, 0)),
            pl.BlockSpec((16, 5, 8, C), lambda i, *s: (0, 0, 0, 0)),
        ],
        scratch_shapes=SCRATCH,
    )
    return pl.pallas_call(
        functools.partial(tile_kernel, pieces, len(arrays)),
        grid_spec=grid_spec,
        out_shape=[
            jax.ShapeDtypeStruct((count, 2, BACK, T), BF16),
            jax.ShapeDtypeStruct((16, 5, 8, C), F32),
        ],
        compiler_params=pltpu.CompilerParams(dimension_semantics=("arbitrary",)),
        cost_estimate=pl.CostEstimate(
            flops=count * 8 * C * C * C, bytes_accessed=count * 8_000_000, transcendentals=0
        ),
    )(used, image, row_off, col_off, sun, gain, *arrays, resample, observed)


def around(step_x, step_y):
    return [
        (4 * y + x, 4 * ((y + step_y) % 4) + (x + step_x) % 4) for y in range(4) for x in range(4)
    ]


STEPS = {"x+": around(1, 0), "x-": around(-1, 0), "y+": around(0, 1), "y-": around(0, -1)}
STEPS["x2"] = around(2, 0)
STEPS["y2"] = around(0, 2)
WAYS = ("x+", "x-", "y+", "y-")
NEAR = [(0, 0), (-1, 0), (1, 0), (0, -1), (0, 1)]
MIDDLE = [(-1, -1), (-1, 1), (1, -1), (1, 1), (2, 0), (0, 2)]
FAR = [(2, -1), (2, 1), (-1, 2), (1, 2), (2, 2)]


def send(messages):
    return {way: lax.ppermute(v, "dy", STEPS[way]) for way, v in messages.items()}


def send_middle(near):
    a = {k: v[0] for k, v in near.items()}
    b = {k: v[1] for k, v in near.items()}
    return send(
        {
            "x+": jnp.stack([a["x+"], b["y+"], b["y-"]]),
            "x-": jnp.stack([b["x-"], b["y+"], b["y-"]]),
            "y+": jnp.stack([a["y+"], a["x+"], a["x-"]]),
            "y-": jnp.stack([b["y-"], a["x+"], a["x-"]]),
        }
    )


def send_far(middle):
    return send(
        {
            "x+": jnp.stack([middle["y+"][1], middle["y-"][1]]),
            "x-": middle["x-"][1:3],
            "y+": middle["y+"][1:3],
            "y-": jnp.stack([middle["x+"][2], middle["x-"][2]]),
            "x2": middle["y+"][0:1],
            "y2": middle["x-"][0:1],
        }
    )


def return_sums(near, middle, far):
    def wide(v):
        return v.astype(F32)

    def slim(v):
        return v.astype(BF16)

    got = send(
        {
            "x-": far[0:2, 0],
            "x+": far[0:2, 1],
            "y-": far[2:4, 0],
            "y+": far[2:4, 1],
            "x2": far[4, 0],
            "y2": far[4, 1],
        }
    )
    b_20 = slim(wide(middle[4, 1]) + wide(got["y2"]))
    a_02 = slim(wide(middle[5, 0]) + wide(got["x2"]))
    a_mm = slim(wide(middle[0, 0]) + wide(got["x-"][0]) + wide(got["y-"][0]))
    a_mp = slim(wide(middle[1, 0]) + wide(got["x-"][1]))
    b_mp = slim(wide(middle[1, 1]) + wide(got["y+"][0]))
    a_pm = slim(wide(middle[2, 0]) + wide(got["y-"][1]))
    b_pm = slim(wide(middle[2, 1]) + wide(got["x+"][0]))
    b_pp = slim(wide(middle[3, 1]) + wide(got["x+"][1]) + wide(got["y+"][1]))
    got = send(
        {
            "x-": jnp.stack([middle[4, 0], middle[0, 1], b_mp]),
            "x+": jnp.stack([b_20, b_pm, b_pp]),
            "y-": jnp.stack([a_02, a_mm, a_pm]),
            "y+": jnp.stack([middle[5, 1], a_mp, middle[3, 0]]),
        }
    )
    xm, xp, ym, yp = (wide(got[k]) for k in ("x-", "x+", "y-", "y+"))
    mine = wide(near)
    got = send(
        {
            "x-": slim(jnp.stack([mine[1, 0] + xm[0] + ym[1] + yp[1], mine[1, 1]])),
            "x+": slim(jnp.stack([mine[2, 0] + ym[2] + yp[2], mine[2, 1] + xp[0]])),
            "y-": slim(jnp.stack([mine[3, 0] + ym[0], mine[3, 1] + xm[1] + xp[1]])),
            "y+": slim(jnp.stack([mine[4, 0], mine[4, 1] + xm[2] + xp[2] + yp[0]])),
        }
    )
    return mine[0] + wide(got["x-"]) + wide(got["x+"]) + wide(got["y-"]) + wide(got["y+"])


def next_images(used, image):
    count = used.shape[0]
    ids = jnp.arange(count, dtype=I32)
    is_used = used == 1
    ahead = jnp.min(
        jnp.where(is_used[None, :] & (ids[None, :] >= ids[:, None]), ids[None, :], count), axis=1
    )
    last = jnp.maximum(jnp.max(jnp.where(is_used, ids, -1)), 0)
    at = jnp.where(ahead < count, ahead, last)
    return jnp.sum(jnp.where(at[:, None] == ids[None, :], image[None, :], 0), axis=1)


def sun_vectors(azimuth, elevation):
    return jnp.stack(
        [
            jnp.cos(elevation) * jnp.cos(azimuth),
            jnp.cos(elevation) * jnp.sin(azimuth),
            jnp.sin(elevation),
        ]
    )


def laplace(padded):
    return (
        padded[:-2, 1:-1]
        + padded[2:, 1:-1]
        + padded[1:-1, :-2]
        + padded[1:-1, 2:]
        - 4.0 * padded[1:-1, 1:-1]
    )


def shifted(value, axis, up):
    count = lax.axis_size(axis)
    pairs = [(i, i + 1) for i in range(count - 1)]
    return lax.ppermute(value, axis, pairs if up else [(b, a) for a, b in pairs])


def quantize(heights):
    return jnp.round(heights * H_SCALE).astype(I32)


def smoothness(heights, top, bottom):
    tall = jnp.concatenate([top, heights, bottom], axis=0)
    left = shifted(tall[:, -2:], "dx", True)
    right = shifted(tall[:, :2], "dx", False)
    wide = jnp.concatenate([left, tall, right], axis=1)
    field = laplace(wide)
    rows, cols = heights.shape
    row_ids = jnp.arange(rows + 2)
    col_ids = jnp.arange(cols + 2)
    row_keep = ~(
        (row_ids == 0) & (lax.axis_index("dy") == 0)
        | (row_ids == rows + 1) & (lax.axis_index("dy") == lax.axis_size("dy") - 1)
    )
    col_keep = ~(
        (col_ids == 0) & (lax.axis_index("dx") == 0)
        | (col_ids == cols + 1) & (lax.axis_index("dx") == lax.axis_size("dx") - 1)
    )
    return SMOOTHING_WEIGHT * laplace(jnp.where(row_keep[:, None] & col_keep[None, :], field, 0.0))


def finish_sums(parts):
    ids = jnp.arange(C, dtype=F32)
    coord = (ids - 0.5 * (C - 1)) / C
    edge = jnp.where((ids == 0) | (ids == C - 1), 1.0, 0.5)
    start = (jnp.arange(8, dtype=F32) - 0.5 * (C - 1)) / C
    x_sum, x_row, y_sum, y_row, e_sum = (parts[:, n] for n in range(5))
    x_v = x_row / C + x_sum * start[None, :, None]
    y_v = y_row / C + y_sum * start[None, :, None]

    def total(v):
        return jnp.sum(v, axis=(1, 2))

    pose = [
        total(x_sum * edge),
        total(x_sum * (edge * coord)),
        total(x_v * edge),
        total(y_sum) * 0.5,
        total(y_sum * coord) * 0.5,
        total(y_v) * 0.5,
    ]
    return jnp.concatenate(
        [jnp.stack(pose, axis=-1) / C, (total(e_sum) / (C * C))[:, None]], axis=-1
    )


def per_device(
    heights, albedo, observed, resample, exposure, sun_azimuth, sun_elevation, send_plan, recv_plan
):
    offsets = send_plan[0, 0, 0:2].reshape(2, 16, 2).transpose(1, 0, 2)
    offsets = lax.all_to_all(offsets, "dy", split_axis=0, concat_axis=0, tiled=True)
    row_off = offsets[:, 0].reshape(-1)
    col_off = offsets[:, 1].reshape(-1)
    slots = jnp.arange(32, dtype=I32)
    match = recv_plan[0, 0][None, :] == slots[:, None]
    used = jnp.any(match, axis=1).astype(I32)
    image = jnp.sum(jnp.where(match, jnp.arange(16, dtype=I32)[None, :], 0), axis=1)
    table = jnp.stack([used, image, row_off, col_off])
    relative = jnp.array(NEAR + MIDDLE + FAR, I32)
    place = lax.axis_index("dy")
    tile_ids = ((place // 4 + relative[:, 1]) % 4) * 4 + (place % 4 + relative[:, 0]) % 4
    slot_ids = (2 * tile_ids[:, None] + jnp.arange(2, dtype=I32)[None, :]).reshape(-1)
    table = jnp.sum(
        jnp.where(slot_ids[None, :, None] == slots[None, None, :], table[:, None, :], 0), axis=2
    )

    def plan_of(first, count):
        part = table[:, 2 * first : 2 * (first + count)]
        return part[0], next_images(part[0], part[1]), part[2], part[3]

    sun = sun_vectors(sun_azimuth[0], sun_elevation[0]).reshape(-1)
    gain = jnp.exp(exposure[0])

    top = shifted(heights[-2:], "dy", True)
    bottom = shifted(heights[:2], "dy", False)
    left = shifted(heights[:, -1], "dx", True)
    right = shifted(heights[:, 0], "dx", False)
    sides = pack(quantize(left), quantize(right)).reshape(2, 1, HALF)
    sides = jnp.concatenate([sides, jnp.zeros((2, 1, T - HALF), I32)], axis=2)
    ends = pack(quantize(jnp.stack([top[1:2], bottom[0:1]])), 0)
    words = pack(quantize(heights), jnp.round((albedo - 1.0) * A_SCALE).astype(I32))
    words = jnp.concatenate(
        [words.reshape(2, HALF, T), sides, ends, jnp.zeros((2, PIECE - HALF - 2, T), I32)], axis=1
    )
    near = send({way: words for way in WAYS})
    middle = send_middle(near)
    far = send_far(middle)
    order = WAYS
    out_near, parts = run_tiles(
        [words] + [near[k] for k in order],
        [((n, 0), (n, 1)) for n in range(5)],
        resample, observed, plan_of(0, 5), sun, gain,
    )
    out_middle, more = run_tiles(
        [middle[k] for k in order],
        [
            ((2, 1), (0, 1)),
            ((3, 1), (0, 2)),
            ((2, 2), (1, 1)),
            ((3, 2), (1, 2)),
            ((0, 0), (1, 0)),
            ((2, 0), (3, 0)),
        ],
        resample, observed, plan_of(5, 6), sun, gain,
    )
    parts = parts + more
    out_far, more = run_tiles(
        [far[k] for k in order] + [far["x2"], far["y2"]],
        [
            ((0, 0), (1, 0)),
            ((0, 1), (1, 1)),
            ((2, 0), (3, 0)),
            ((2, 1), (3, 1)),
            ((4, 0), (5, 0)),
        ],
        resample, observed, plan_of(11, 5), sun, gain,
    )
    parts = parts + more
    smooth = smoothness(heights, top, bottom)
    crop_sums = finish_sums(parts)
    arrived = lax.all_to_all(crop_sums[:, None], "dy", split_axis=0, concat_axis=0, tiled=True)
    camera = arrived.sum(axis=0)
    own = return_sums(out_near, out_middle, out_far)
    from_below = shifted(own[0, HALF], "dy", False)
    from_above = shifted(own[1, HALF], "dy", True)
    from_right = shifted(own[:, HALF + 1, :HALF].reshape(-1), "dx", False)
    from_left = shifted(own[:, HALF + 2, :HALF].reshape(-1), "dx", True)
    row_ids = lax.broadcasted_iota(I32, (T, T), 0)
    col_ids = lax.broadcasted_iota(I32, (T, T), 1)
    data = own[:, :HALF].reshape(T, T)
    data = data + jnp.where(row_ids == T - 1, from_below[None, :], 0.0)
    data = data + jnp.where(row_ids == 0, from_above[None, :], 0.0)
    data = data + jnp.where(col_ids == T - 1, from_right[:, None], 0.0)
    data = data + jnp.where(col_ids == 0, from_left[:, None], 0.0)
    return (data + smooth, camera[None])


def solution(mesh):
    placed = (
        P("dy", "dx"),
        P("dy", "dx"),
        P(("dy", "dx"), None, None),
        P(("dy", "dx"), None, None, None),
        P("dx", None),
        P("dx", None),
        P("dx", None),
        P("dy", "dx", None, None),
        P("dy", "dx", None),
    )

    return jax.shard_map(
        per_device,
        mesh=mesh,
        in_specs=placed,
        out_specs=(P("dy", "dx"), P("dx", "dy", None)),
        check_vma=False,
    )
```

```python
import functools

import jax
import jax.numpy as jnp
from jax import lax
from jax.experimental import pallas as pl
from jax.experimental.pallas import tpu as pltpu
from jax.sharding import PartitionSpec as P


SMOOTHING_WEIGHT = 0.02
H_SCALE = 8191.0
A_SCALE = 65534.0
T = 512
C = 384
HALF = 256
PIECE = 264
BACK = 272
CH = 32
F32 = jnp.float32
BF16 = jnp.bfloat16
I32 = jnp.int32


def pack(high, low):
    return lax.shift_left(high, 16) | (low & 0xFFFF)


def high_of(word):
    return lax.shift_right_arithmetic(word, 16).astype(F32)


def low_of(word):
    return lax.shift_right_arithmetic(lax.shift_left(word, 16), 16).astype(F32)


def tile_kernel(pieces, operands, *refs):
    used, image, row_off, col_off, sun, gain = refs[:6]
    tiles = refs[6 : 6 + operands]
    (
        res_ref, obs_ref,
        out_ref, sums_ref,
        rim, hbuf, hcol, sx_ref, sy_ref, w_ref, r2_ref, gx_ref, gy_ref,
        shaded, tbuf, pbuf, weighted, grad,
    ) = refs[6 + operands :]
    step = pl.program_id(0)
    first = (step // 2) * 2
    slot_odd = step % 2
    mine = used[step] == 1
    any_used = used[first] + used[first + 1] > 0
    lane = lax.broadcasted_iota(I32, (CH, 128), 1)
    at_first = lane == 0
    at_last = lane == 127

    def lanes(b):
        return slice(128 * b, 128 * (b + 1))

    @pl.when(step == 0)
    def _():
        sums_ref[...] = jnp.zeros_like(sums_ref)

    for t, sources in enumerate(pieces):

        @pl.when((step == 2 * t) & any_used)
        def _(sources=sources):
            for half, (operand, at) in enumerate(sources):
                ref = tiles[operand]
                rim[half] = ref[at, HALF:PIECE]

                def unpack(k, _, ref=ref, at=at, half=half):
                    base = pl.multiple_of(k * CH, CH)
                    to = pl.multiple_of(base + HALF * half, CH)
                    for b in range(4):
                        words = ref[at, pl.ds(base, CH), lanes(b)]
                        hbuf[b, pl.ds(to + 8, CH)] = high_of(words)
                        w_ref[b, pl.ds(to, CH)] = low_of(words) * (1.0 / A_SCALE) + 1.0
                    return 0

                lax.fori_loop(0, HALF // CH, unpack, 0)

    @pl.when((slot_odd == 0) & any_used)
    def _():
        row_id = lax.broadcasted_iota(I32, (32, 256), 0)
        side = lax.broadcasted_iota(I32, (32, 256), 1) // 128
        scale = jnp.where(row_id == 16 * side, 256.0, 0.0) + jnp.where(
            row_id == 16 * side + 8, 1.0, 0.0
        )
        for half in range(2):
            words = rim[half, :, 0:HALF]
            high = lax.shift_right_arithmetic(words, 16)
            low = lax.shift_right_arithmetic(lax.shift_left(words, 16), 16)
            parts = jnp.concatenate(
                [
                    lax.shift_right_arithmetic(high, 8),
                    high & 255,
                    lax.shift_right_arithmetic(low, 8),
                    low & 255,
                ],
                axis=0,
            ).astype(F32).astype(BF16)
            columns = lax.dot_general(
                parts, scale.astype(BF16), (((0,), (0,)), ((), ())), preferred_element_type=F32
            )
            for side_id in range(2):
                hcol[side_id, HALF * half : HALF * (half + 1)] = columns[:, lanes(side_id)]
        top = high_of(rim[0])
        bottom = high_of(rim[1])
        for b in range(4):
            hbuf[b, 7:8] = top[1:2, lanes(b)]
            hbuf[b, T + 8 : T + 9] = bottom[1:2, lanes(b)]
            gy_ref[b, 0:8] = jnp.zeros((8, 128), F32)
            gy_ref[b, T + 8 : T + 16] = jnp.zeros((8, 128), F32)

        def slope(k, _):
            base = pl.multiple_of(k * CH, CH)
            rows = pl.ds(base, CH)
            here = [hbuf[b, pl.ds(base + 8, CH)] for b in range(4)]
            right_turn = [pltpu.roll(h, 1, 1) for h in here]
            left_turn = [pltpu.roll(h, 127, 1) for h in here]
            before = [hcol[0, rows]] + right_turn[:3]
            after = left_turn[1:] + [hcol[1, rows]]
            for b in range(4):
                left = jnp.where(at_first, before[b], right_turn[b])
                right = jnp.where(at_last, after[b], left_turn[b])
                sx = (right - left) * (0.5 / H_SCALE)
                sy = (hbuf[b, pl.ds(base + 9, CH)] - hbuf[b, pl.ds(base + 7, CH)]) * (
                    0.5 / H_SCALE
                )
                r = lax.rsqrt(1.0 + sx * sx + sy * sy)
                sx_ref[b, rows] = sx
                sy_ref[b, rows] = sy
                w_ref[b, rows] = w_ref[b, rows] * r
                r2_ref[b, rows] = r * r
                gx_ref[b, rows] = jnp.zeros((CH, 128), F32)
                gy_ref[b, pl.ds(base + 8, CH)] = jnp.zeros((CH, 128), F32)
            return 0

        lax.fori_loop(0, T // CH, slope, 0, unroll=4)

    @pl.when(mine)
    def _():
        m = image[step]
        oy = pl.multiple_of(row_off[step], 128)
        ob = col_off[step] // 128
        s1 = sun[m]
        s2 = sun[16 + m]
        s3 = sun[32 + m]
        e = gain[m]

        def shade(k, _):
            base = pl.multiple_of(k * CH, CH)
            rows = pl.ds(pl.multiple_of(oy + base, CH), CH)
            for b in range(3):
                q = s3 - s1 * sx_ref[ob + b, rows] - s2 * sy_ref[ob + b, rows]
                shaded[pl.ds(base, CH), lanes(b)] = (w_ref[ob + b, rows] * q).astype(BF16)
                tbuf[b, pl.ds(base, CH)] = q * r2_ref[ob + b, rows]
            return 0

        lax.fori_loop(0, C // CH, shade, 0, unroll=4)
        row_mat = res_ref[0, 0]
        col_mat = res_ref[0, 1]
        first_pass = jnp.dot(row_mat, shaded[...], preferred_element_type=F32).astype(BF16)
        predicted = e * lax.dot_general(
            first_pass, col_mat, (((1,), (1,)), ((), ())), preferred_element_type=F32
        )
        for b in range(3):
            pbuf[b, 8 : 8 + C] = predicted[:, lanes(b)]
            pbuf[b, 7:8] = 2.0 * pbuf[b, 8:9] - pbuf[b, 9:10]
            pbuf[b, C + 8 : C + 9] = 2.0 * pbuf[b, C + 7 : C + 8] - pbuf[b, C + 6 : C + 7]

        def add_up(v, base, total, by_row):
            groups = [v[8 * g : 8 * g + 8] for g in range(CH // 8)]
            tail = groups[-1]
            lead = tail
            for g in range(CH // 8 - 2, 0, -1):
                tail = groups[g] + tail
                lead = lead + tail
            tail = groups[0] + tail
            return total + tail, by_row + lead * 8.0 + tail * base

        def terms(k, carry):
            base = pl.multiple_of(k * CH, CH)
            at = base.astype(F32)
            rows = pl.ds(base, CH)
            here = [pbuf[b, pl.ds(base + 8, CH)] for b in range(3)]
            right_turn = [pltpu.roll(p, 1, 1) for p in here]
            left_turn = [pltpu.roll(p, 127, 1) for p in here]
            before = [here[0]] + right_turn[:2]
            after = left_turn[1:] + [here[2]]
            result = []
            for b in range(3):
                a_x, a_xg, a_y, a_yg, a_e = carry[b]
                p = here[b]
                residual = p - obs_ref[0, rows, lanes(b)].astype(F32)
                weighted[rows, lanes(b)] = (e * residual).astype(BF16)
                left = jnp.where(at_first, before[b], right_turn[b])
                right = jnp.where(at_last, after[b], left_turn[b])
                a_x, a_xg = add_up(residual * (right - left), at, a_x, a_xg)
                down = pbuf[b, pl.ds(base + 9, CH)]
                up = pbuf[b, pl.ds(base + 7, CH)]
                a_y, a_yg = add_up(residual * (down - up), at, a_y, a_yg)
                squares = residual * p
                a_e = a_e + squares.reshape(CH // 8, 8, 128).sum(axis=0)
                result.append((a_x, a_xg, a_y, a_yg, a_e))
            return tuple(result)

        zero = jnp.zeros((8, 128), F32)
        parts = lax.fori_loop(0, C // CH, terms, ((zero,) * 5,) * 3, unroll=3)
        for b in range(3):
            for n in range(5):
                sums_ref[m, n, :, lanes(b)] = parts[b][n]
        back_pass = lax.dot_general(
            row_mat, weighted[...], (((0,), (0,)), ((), ())), preferred_element_type=F32
        ).astype(BF16)
        crop_grad = jnp.dot(back_pass, col_mat, preferred_element_type=F32)
        for b in range(3):
            grad[b] = crop_grad[:, lanes(b)]

        def pull(k, _):
            base = pl.multiple_of(k * CH, CH)
            rows = pl.ds(pl.multiple_of(oy + base, CH), CH)
            rows_y = pl.ds(pl.multiple_of(oy + base + 8, 8), CH)
            for b in range(3):
                t = tbuf[b, pl.ds(base, CH)]
                wg = w_ref[ob + b, rows] * grad[b, pl.ds(base, CH)]
                gx_ref[ob + b, rows] = gx_ref[ob + b, rows] - wg * (s1 + t * sx_ref[ob + b, rows])
                gy_ref[ob + b, rows_y] = gy_ref[ob + b, rows_y] - wg * (
                    s2 + t * sy_ref[ob + b, rows]
                )
            return 0

        lax.fori_loop(0, C // CH, pull, 0, unroll=4)

    @pl.when((slot_odd == 1) & any_used)
    def _():
        def stencil(k, _):
            base = pl.multiple_of(k * CH, CH)
            rows = pl.ds(base, CH)
            half = k // (HALF // CH)
            to = pl.ds(pl.multiple_of(base - half * HALF, CH), CH)
            here = [gx_ref[b, rows] for b in range(4)]
            right_turn = [pltpu.roll(g, 1, 1) for g in here]
            left_turn = [pltpu.roll(g, 127, 1) for g in here]
            blank = jnp.zeros((CH, 128), F32)
            before = [blank] + right_turn[:3]
            after = left_turn[1:] + [blank]
            for b in range(4):
                left = jnp.where(at_first, before[b], right_turn[b])
                right = jnp.where(at_last, after[b], left_turn[b])
                up = gy_ref[b, pl.ds(base + 7, CH)]
                down = gy_ref[b, pl.ds(base + 9, CH)]
                total = (left - right) + (up - down)
                out_ref[0, half, to, lanes(b)] = (0.5 * total).astype(BF16)
            return 0

        lax.fori_loop(0, T // CH, stencil, 0, unroll=4)
        sub = lax.broadcasted_iota(I32, (16, 128), 0)
        lane16 = lax.broadcasted_iota(I32, (16, 128), 1)
        pick_low = jnp.where((sub == 1) & (lane16 == 0), -0.5, 0.0).astype(BF16)
        pick_high = jnp.where((sub == 2) & (lane16 == 127), 0.5, 0.0).astype(BF16)
        cross = (((1,), (1,)), ((), ()))
        for half in range(2):
            rows = slice(HALF * half, HALF * (half + 1))
            spill = lax.dot_general(
                pick_low, gx_ref[0, rows].astype(BF16), cross, preferred_element_type=F32
            ) + lax.dot_general(
                pick_high, gx_ref[3, rows].astype(BF16), cross, preferred_element_type=F32
            )
            for b in range(4):
                edge = 0.5 * gy_ref[b, T + 7 : T + 8] if half else -0.5 * gy_ref[b, 8:9]
                rest = spill[:, lanes(b)] if b < 2 else jnp.zeros((16, 128), F32)
                out_ref[0, half, HALF:BACK, lanes(b)] = jnp.where(sub == 0, edge, rest).astype(
                    BF16
                )

    @pl.when((slot_odd == 1) & jnp.logical_not(any_used))
    def _():
        out_ref[...] = jnp.zeros_like(out_ref)


SCRATCH = [
    pltpu.VMEM((2, PIECE - HALF, T), I32),
    pltpu.VMEM((4, T + 16, 128), F32),
    pltpu.VMEM((2, T, 128), F32),
    pltpu.VMEM((4, T, 128), F32),
    pltpu.VMEM((4, T, 128), F32),
    pltpu.VMEM((4, T, 128), F32),
    pltpu.VMEM((4, T, 128), F32),
    pltpu.VMEM((4, T, 128), F32),
    pltpu.VMEM((4, T + 16, 128), F32),
    pltpu.VMEM((C, C), BF16),
    pltpu.VMEM((3, C, 128), F32),
    pltpu.VMEM((3, C + 16, 128), F32),
    pltpu.VMEM((C, C), BF16),
    pltpu.VMEM((3, C, 128), F32),
]


def run_tiles(arrays, pieces, resample, observed, plan, sun, gain):
    used, image, row_off, col_off = plan
    count = len(pieces)
    tile_specs = [pl.BlockSpec(v.shape, lambda i, *s: (0, 0, 0)) for v in arrays]
    grid_spec = pltpu.PrefetchScalarGridSpec(
        num_scalar_prefetch=6,
        grid=(2 * count,),
        in_specs=tile_specs
        + [
            pl.BlockSpec((1, 2, C, C), lambda i, u, m, *s: (m[i], 0, 0, 0)),
            pl.BlockSpec((1, C, C), lambda i, u, m, *s: (m[i], 0, 0)),
        ],
        out_specs=[
            pl.BlockSpec((1, 2, BACK, T), lambda i, *s: (i // 2, 0, 0, 0)),
            pl.BlockSpec((16, 5, 8, C), lambda i, *s: (0, 0, 0, 0)),
        ],
        scratch_shapes=SCRATCH,
    )
    return pl.pallas_call(
        functools.partial(tile_kernel, pieces, len(arrays)),
        grid_spec=grid_spec,
        out_shape=[
            jax.ShapeDtypeStruct((count, 2, BACK, T), BF16),
            jax.ShapeDtypeStruct((16, 5, 8, C), F32),
        ],
        compiler_params=pltpu.CompilerParams(dimension_semantics=("arbitrary",)),
        cost_estimate=pl.CostEstimate(
            flops=count * 8 * C * C * C, bytes_accessed=count * 8_000_000, transcendentals=0
        ),
    )(used, image, row_off, col_off, sun, gain, *arrays, resample, observed)


def around(step_x, step_y):
    return [
        (4 * y + x, 4 * ((y + step_y) % 4) + (x + step_x) % 4) for y in range(4) for x in range(4)
    ]


STEPS = {"x+": around(1, 0), "x-": around(-1, 0), "y+": around(0, 1), "y-": around(0, -1)}
STEPS["x2"] = around(2, 0)
STEPS["y2"] = around(0, 2)
WAYS = ("x+", "x-", "y+", "y-")
WAYS_BACK = ("x-", "x+", "y-", "y+")
NEAR = [(0, 0), (-1, 0), (1, 0), (0, -1), (0, 1)]
MIDDLE = [(-1, -1), (-1, 1), (1, -1), (1, 1), (2, 0), (0, 2)]
FAR = [(2, -1), (2, 1), (-1, 2), (1, 2), (2, 2)]


def send(messages):
    return {way: lax.ppermute(v, "dy", STEPS[way]) for way, v in messages.items()}


def send_middle(near):
    a = {k: v[0] for k, v in near.items()}
    b = {k: v[1] for k, v in near.items()}
    return send(
        {
            "x+": jnp.stack([a["x+"], b["y+"], b["y-"]]),
            "x-": jnp.stack([b["x-"], b["y+"], b["y-"]]),
            "y+": jnp.stack([a["y+"], a["x+"], a["x-"]]),
            "y-": jnp.stack([b["y-"], a["x+"], a["x-"]]),
        }
    )


def send_far(middle):
    return send(
        {
            "x+": jnp.stack([middle["y+"][1], middle["y-"][1]]),
            "x-": middle["x-"][1:3],
            "y+": middle["y+"][1:3],
            "y-": jnp.stack([middle["x+"][2], middle["x-"][2]]),
            "x2": middle["y+"][0:1],
            "y2": middle["x-"][0:1],
        }
    )


def return_sums(near, middle, far):
    def wide(v):
        return v.astype(F32)

    def slim(v):
        return v.astype(BF16)

    flat = far.reshape((10,) + far.shape[2:])
    got = send(
        {
            "x2": flat[8:9],
            "y2": flat[9:10],
            "x-": flat[0:3],
            "y-": flat[4:7],
            "x+": flat[3:4],
            "y+": flat[7:8],
        }
    )
    xm, xp, ym, yp = (got[k] for k in WAYS_BACK)
    b_20 = slim(wide(middle[4, 1]) + wide(got["y2"][0]))
    a_02 = slim(wide(middle[5, 0]) + wide(got["x2"][0]))
    a_mm = slim(wide(middle[0, 0]) + wide(xm[0]) + wide(ym[0]))
    b_mm = slim(wide(middle[0, 1]) + wide(xm[1]) + wide(ym[1]))
    a_mp = slim(wide(middle[1, 0]) + wide(xm[2]))
    a_pm = slim(wide(middle[2, 0]) + wide(ym[2]))
    b_pp = slim(wide(middle[3, 1]) + wide(xp[0]) + wide(yp[0]))
    got = send(
        {
            "x-": jnp.stack([middle[4, 0], b_mm, middle[1, 1]]),
            "x+": jnp.stack([b_20, middle[2, 1], b_pp]),
            "y-": jnp.stack([a_02, a_mm, a_pm]),
            "y+": jnp.stack([middle[5, 1], a_mp, middle[3, 0]]),
        }
    )
    xm, xp, ym, yp = (got[k] for k in WAYS_BACK)

    def total(*pieces):
        result = wide(pieces[0])
        for piece in pieces[1:]:
            result = result + wide(piece)
        return slim(result)

    got = send(
        {
            "x-": jnp.stack([total(near[1, 0], xm[0], ym[1], yp[1]), near[1, 1]]),
            "x+": jnp.stack([total(near[2, 0], ym[2], yp[2]), total(near[2, 1], xp[0])]),
            "y-": jnp.stack([total(near[3, 0], ym[0]), total(near[3, 1], xm[1], xp[1])]),
            "y+": jnp.stack([near[4, 0], total(near[4, 1], xm[2], xp[2], yp[0])]),
        }
    )
    result = wide(near[0])
    for way in WAYS_BACK:
        result = result + wide(got[way])
    return result


def next_images(used, image):
    count = used.shape[0]
    ids = jnp.arange(count, dtype=I32)
    is_used = used == 1
    ahead = jnp.min(
        jnp.where(is_used[None, :] & (ids[None, :] >= ids[:, None]), ids[None, :], count), axis=1
    )
    last = jnp.maximum(jnp.max(jnp.where(is_used, ids, -1)), 0)
    at = jnp.where(ahead < count, ahead, last)
    return jnp.sum(jnp.where(at[:, None] == ids[None, :], image[None, :], 0), axis=1)


def sun_vectors(azimuth, elevation):
    return jnp.stack(
        [
            jnp.cos(elevation) * jnp.cos(azimuth),
            jnp.cos(elevation) * jnp.sin(azimuth),
            jnp.sin(elevation),
        ]
    )


def laplace(padded):
    return (
        padded[:-2, 1:-1]
        + padded[2:, 1:-1]
        + padded[1:-1, :-2]
        + padded[1:-1, 2:]
        - 4.0 * padded[1:-1, 1:-1]
    )


def shifted(value, axis, up):
    count = lax.axis_size(axis)
    pairs = [(i, i + 1) for i in range(count - 1)]
    return lax.ppermute(value, axis, pairs if up else [(b, a) for a, b in pairs])


def quantize(heights):
    return jnp.round(heights * H_SCALE).astype(I32)


def smoothness(heights, top, bottom):
    tall = jnp.concatenate([top, heights, bottom], axis=0)
    left = shifted(tall[:, -2:], "dx", True)
    right = shifted(tall[:, :2], "dx", False)
    wide = jnp.concatenate([left, tall, right], axis=1)
    field = laplace(wide)
    rows, cols = heights.shape
    row_ids = jnp.arange(rows + 2)
    col_ids = jnp.arange(cols + 2)
    row_keep = ~(
        (row_ids == 0) & (lax.axis_index("dy") == 0)
        | (row_ids == rows + 1) & (lax.axis_index("dy") == lax.axis_size("dy") - 1)
    )
    col_keep = ~(
        (col_ids == 0) & (lax.axis_index("dx") == 0)
        | (col_ids == cols + 1) & (lax.axis_index("dx") == lax.axis_size("dx") - 1)
    )
    return SMOOTHING_WEIGHT * laplace(jnp.where(row_keep[:, None] & col_keep[None, :], field, 0.0))


def finish_sums(parts):
    ids = jnp.arange(C, dtype=F32)
    coord = (ids - 0.5 * (C - 1)) / C
    edge = jnp.where((ids == 0) | (ids == C - 1), 1.0, 0.5)
    start = (jnp.arange(8, dtype=F32) - 0.5 * (C - 1)) / C
    x_sum, x_row, y_sum, y_row, e_sum = (parts[:, n] for n in range(5))
    x_v = x_row / C + x_sum * start[None, :, None]
    y_v = y_row / C + y_sum * start[None, :, None]

    def total(v):
        return jnp.sum(v, axis=(1, 2))

    pose = [
        total(x_sum * edge),
        total(x_sum * (edge * coord)),
        total(x_v * edge),
        total(y_sum) * 0.5,
        total(y_sum * coord) * 0.5,
        total(y_v) * 0.5,
    ]
    return jnp.concatenate(
        [jnp.stack(pose, axis=-1) / C, (total(e_sum) / (C * C))[:, None]], axis=-1
    )


def per_device(
    heights, albedo, observed, resample, exposure, sun_azimuth, sun_elevation, send_plan, recv_plan
):
    offsets = send_plan[0, 0, 0:2].reshape(2, 16, 2).transpose(1, 0, 2)
    offsets = lax.all_to_all(offsets, "dy", split_axis=0, concat_axis=0, tiled=True)
    row_off = offsets[:, 0].reshape(-1)
    col_off = offsets[:, 1].reshape(-1)
    slots = jnp.arange(32, dtype=I32)
    match = recv_plan[0, 0][None, :] == slots[:, None]
    used = jnp.any(match, axis=1).astype(I32)
    image = jnp.sum(jnp.where(match, jnp.arange(16, dtype=I32)[None, :], 0), axis=1)
    table = jnp.stack([used, image, row_off, col_off])
    relative = jnp.array(NEAR + MIDDLE + FAR, I32)
    place = lax.axis_index("dy")
    tile_ids = ((place // 4 + relative[:, 1]) % 4) * 4 + (place % 4 + relative[:, 0]) % 4
    slot_ids = (2 * tile_ids[:, None] + jnp.arange(2, dtype=I32)[None, :]).reshape(-1)
    table = jnp.sum(
        jnp.where(slot_ids[None, :, None] == slots[None, None, :], table[:, None, :], 0), axis=2
    )

    def plan_of(first, count):
        part = table[:, 2 * first : 2 * (first + count)]
        return part[0], next_images(part[0], part[1]), part[2], part[3]

    sun = sun_vectors(sun_azimuth[0], sun_elevation[0]).reshape(-1)
    gain = jnp.exp(exposure[0])

    top = shifted(heights[-2:], "dy", True)
    bottom = shifted(heights[:2], "dy", False)
    left = shifted(heights[:, -1], "dx", True)
    right = shifted(heights[:, 0], "dx", False)
    sides = pack(quantize(left), quantize(right)).reshape(2, 1, HALF)
    sides = jnp.concatenate([sides, jnp.zeros((2, 1, T - HALF), I32)], axis=2)
    ends = pack(quantize(jnp.stack([top[1:2], bottom[0:1]])), 0)
    words = pack(quantize(heights), jnp.round((albedo - 1.0) * A_SCALE).astype(I32))
    words = jnp.concatenate(
        [words.reshape(2, HALF, T), sides, ends, jnp.zeros((2, PIECE - HALF - 2, T), I32)], axis=1
    )
    near = send({way: words for way in WAYS})
    middle = send_middle(near)
    far = send_far(middle)
    order = WAYS
    out_near, parts = run_tiles(
        [words] + [near[k] for k in order],
        [((n, 0), (n, 1)) for n in range(5)],
        resample, observed, plan_of(0, 5), sun, gain,
    )
    out_middle, more = run_tiles(
        [middle[k] for k in order],
        [
            ((2, 1), (0, 1)),
            ((3, 1), (0, 2)),
            ((2, 2), (1, 1)),
            ((3, 2), (1, 2)),
            ((0, 0), (1, 0)),
            ((2, 0), (3, 0)),
        ],
        resample, observed, plan_of(5, 6), sun, gain,
    )
    parts = parts + more
    out_far, more = run_tiles(
        [far[k] for k in order] + [far["x2"], far["y2"]],
        [
            ((0, 0), (1, 0)),
            ((0, 1), (1, 1)),
            ((2, 0), (3, 0)),
            ((2, 1), (3, 1)),
            ((4, 0), (5, 0)),
        ],
        resample, observed, plan_of(11, 5), sun, gain,
    )
    parts = parts + more
    smooth = smoothness(heights, top, bottom)
    crop_sums = finish_sums(parts)
    arrived = lax.all_to_all(crop_sums[:, None], "dy", split_axis=0, concat_axis=0, tiled=True)
    camera = arrived.sum(axis=0)
    own = return_sums(out_near, out_middle, out_far)
    from_below = shifted(own[0, HALF], "dy", False)
    from_above = shifted(own[1, HALF], "dy", True)
    from_right = shifted(own[:, HALF + 1, :HALF].reshape(-1), "dx", False)
    from_left = shifted(own[:, HALF + 2, :HALF].reshape(-1), "dx", True)
    row_ids = lax.broadcasted_iota(I32, (T, T), 0)
    col_ids = lax.broadcasted_iota(I32, (T, T), 1)
    data = own[:, :HALF].reshape(T, T)
    data = data + jnp.where(row_ids == T - 1, from_below[None, :], 0.0)
    data = data + jnp.where(row_ids == 0, from_above[None, :], 0.0)
    data = data + jnp.where(col_ids == T - 1, from_right[:, None], 0.0)
    data = data + jnp.where(col_ids == 0, from_left[:, None], 0.0)
    return (data + smooth, camera[None])


def solution(mesh):
    placed = (
        P("dy", "dx"),
        P("dy", "dx"),
        P(("dy", "dx"), None, None),
        P(("dy", "dx"), None, None, None),
        P("dx", None),
        P("dx", None),
        P("dx", None),
        P("dy", "dx", None, None),
        P("dy", "dx", None),
    )

    return jax.shard_map(
        per_device,
        mesh=mesh,
        in_specs=placed,
        out_specs=(P("dy", "dx"), P("dx", "dy", None)),
        check_vma=False,
    )
```

```python
import functools

import jax
import jax.numpy as jnp
from jax import lax
from jax.experimental import pallas as pl
from jax.experimental.pallas import tpu as pltpu
from jax.sharding import PartitionSpec as P


SMOOTHING_WEIGHT = 0.02
H_SCALE = 8191.0
A_SCALE = 65534.0
T = 512
C = 384
HALF = 256
PIECE = 264
BACK = 272
CH = 32
F32 = jnp.float32
BF16 = jnp.bfloat16
I32 = jnp.int32


def pack(high, low):
    return lax.shift_left(high, 16) | (low & 0xFFFF)


def high_of(word):
    return lax.shift_right_arithmetic(word, 16).astype(F32)


def low_of(word):
    return lax.shift_right_arithmetic(lax.shift_left(word, 16), 16).astype(F32)


def tile_kernel(pieces, operands, *refs):
    used, image, row_off, col_off, sun, gain = refs[:6]
    tiles = refs[6 : 6 + operands]
    (
        res_ref, obs_ref,
        out_ref, sums_ref,
        rim, words_ref, hbuf, hcol, sx_ref, sy_ref, w_ref, r2_ref, gx_ref, gy_ref,
        shaded, tbuf, pbuf, weighted, grad,
    ) = refs[6 + operands :]
    step = pl.program_id(0)
    first = (step // 2) * 2
    slot_odd = step % 2
    mine = used[step] == 1
    any_used = used[first] + used[first + 1] > 0
    low_row = jnp.minimum(
        jnp.where(used[first] == 1, row_off[first], 128),
        jnp.where(used[first + 1] == 1, row_off[first + 1], 128),
    )
    high_row = C + jnp.maximum(
        jnp.where(used[first] == 1, row_off[first], 0),
        jnp.where(used[first + 1] == 1, row_off[first + 1], 0),
    )
    low_block = low_row // 128
    high_block = high_row // 128
    lane = lax.broadcasted_iota(I32, (CH, 128), 1)
    at_first = lane == 0
    at_last = lane == 127

    def lanes(b):
        return slice(128 * b, 128 * (b + 1))

    @pl.when(step == 0)
    def _():
        sums_ref[...] = jnp.zeros_like(sums_ref)

    for t, sources in enumerate(pieces):

        @pl.when((step == 2 * t) & any_used)
        def _(sources=sources):
            for half, (operand, at) in enumerate(sources):
                ref = tiles[operand]
                rim[half] = ref[at, HALF:PIECE]

                def unpack(k, _, ref=ref, at=at, half=half):
                    base = pl.multiple_of(k * 64, 64)
                    to = pl.multiple_of(base + HALF * half, 64)
                    for b in range(4):
                        words = ref[at, pl.ds(base, 64), lanes(b)]
                        hbuf[b, pl.ds(to + 8, 64)] = high_of(words)
                        words_ref[b, pl.ds(to, 64)] = words
                    return 0

                if half:
                    lax.fori_loop(0, high_block, unpack, 0)
                else:
                    lax.fori_loop(low_block, 4, unpack, 0)

    @pl.when((slot_odd == 0) & any_used)
    def _():
        row_id = lax.broadcasted_iota(I32, (32, 256), 0)
        side = lax.broadcasted_iota(I32, (32, 256), 1) // 128
        scale = jnp.where(row_id == 16 * side, 256.0, 0.0) + jnp.where(
            row_id == 16 * side + 8, 1.0, 0.0
        )
        for half in range(2):
            words = rim[half, :, 0:HALF]
            high = lax.shift_right_arithmetic(words, 16)
            low = lax.shift_right_arithmetic(lax.shift_left(words, 16), 16)
            parts = jnp.concatenate(
                [
                    lax.shift_right_arithmetic(high, 8),
                    high & 255,
                    lax.shift_right_arithmetic(low, 8),
                    low & 255,
                ],
                axis=0,
            ).astype(F32).astype(BF16)
            columns = lax.dot_general(
                parts, scale.astype(BF16), (((0,), (0,)), ((), ())), preferred_element_type=F32
            )
            for side_id in range(2):
                hcol[side_id, HALF * half : HALF * (half + 1)] = columns[:, lanes(side_id)]
        top = high_of(rim[0])
        bottom = high_of(rim[1])
        for b in range(4):
            hbuf[b, 7:8] = top[1:2, lanes(b)]
            hbuf[b, T + 8 : T + 9] = bottom[1:2, lanes(b)]
            for at in (0, 8, 128, C + 8, T, T + 8):
                gy_ref[b, at : at + 8] = jnp.zeros((8, 128), F32)
        for b in (0, 3):
            gx_ref[b, 0:128] = jnp.zeros((128, 128), F32)
            gx_ref[b, C:T] = jnp.zeros((128, 128), F32)

        def slope(k):
            base = pl.multiple_of(k * CH, CH)
            rows = pl.ds(base, CH)
            here = [hbuf[b, pl.ds(base + 8, CH)] for b in range(4)]
            right_turn = [pltpu.roll(h, 1, 1) for h in here]
            left_turn = [pltpu.roll(h, 127, 1) for h in here]
            before = [hcol[0, rows]] + right_turn[:3]
            after = left_turn[1:] + [hcol[1, rows]]
            for b in range(4):
                left = jnp.where(at_first, before[b], right_turn[b])
                right = jnp.where(at_last, after[b], left_turn[b])
                sx = (right - left) * (0.5 / H_SCALE)
                sy = (hbuf[b, pl.ds(base + 9, CH)] - hbuf[b, pl.ds(base + 7, CH)]) * (
                    0.5 / H_SCALE
                )
                albedo = low_of(words_ref[b, rows]) * (1.0 / A_SCALE) + 1.0
                r = lax.rsqrt(1.0 + sx * sx + sy * sy)
                sx_ref[b, rows] = sx
                sy_ref[b, rows] = sy
                w_ref[b, rows] = albedo * r
                r2_ref[b, rows] = r * r
                gx_ref[b, rows] = jnp.zeros((CH, 128), F32)
                gy_ref[b, pl.ds(base + 8, CH)] = jnp.zeros((CH, 128), F32)

        def slope_block(k, _):
            for n in range(4):
                slope(4 * k + n)
            return 0

        lax.fori_loop(low_block, high_block, slope_block, 0)

    @pl.when(mine)
    def _():
        m = image[step]
        oy = pl.multiple_of(row_off[step], 128)
        ob = col_off[step] // 128
        s1 = sun[m]
        s2 = sun[16 + m]
        s3 = sun[32 + m]
        e = gain[m]

        def shade(k):
            base = k * CH
            rows = pl.ds(pl.multiple_of(oy + base, CH), CH)
            for b in range(3):
                q = s3 - s1 * sx_ref[ob + b, rows] - s2 * sy_ref[ob + b, rows]
                shaded[pl.ds(base, CH), lanes(b)] = (w_ref[ob + b, rows] * q).astype(BF16)
                tbuf[b, pl.ds(base, CH)] = q * r2_ref[ob + b, rows]

        for k in range(C // CH):
            shade(k)
        row_mat = res_ref[0, 0]
        col_mat = res_ref[0, 1]
        first_pass = jnp.dot(row_mat, shaded[...], preferred_element_type=F32).astype(BF16)

        def predict(low, high):
            block = e * lax.dot_general(
                first_pass[low:high],
                col_mat,
                (((1,), (1,)), ((), ())),
                preferred_element_type=F32,
            )
            for b in range(3):
                pbuf[b, 8 + low : 8 + high] = block[:, lanes(b)]
                if low == 0:
                    pbuf[b, 7:8] = 2.0 * block[0:1, lanes(b)] - block[1:2, lanes(b)]
                if high == C:
                    end = high - low
                    pbuf[b, C + 8 : C + 9] = (
                        2.0 * block[end - 1 : end, lanes(b)] - block[end - 2 : end - 1, lanes(b)]
                    )

        def add_up(v, base, total, by_row):
            groups = [v[8 * g : 8 * g + 8] for g in range(CH // 8)]
            tail = groups[-1]
            lead = tail
            for g in range(CH // 8 - 2, 0, -1):
                tail = groups[g] + tail
                lead = lead + tail
            tail = groups[0] + tail
            return total + tail, by_row + lead * 8.0 + tail * base

        def terms(k, carry):
            base = k * CH
            at = float(base)
            rows = pl.ds(base, CH)
            here = [pbuf[b, pl.ds(base + 8, CH)] for b in range(3)]
            right_turn = [pltpu.roll(p, 1, 1) for p in here]
            left_turn = [pltpu.roll(p, 127, 1) for p in here]
            before = [here[0]] + right_turn[:2]
            after = left_turn[1:] + [here[2]]
            result = []
            for b in range(3):
                a_x, a_xg, a_y, a_yg, a_e = carry[b]
                p = here[b]
                residual = p - obs_ref[0, rows, lanes(b)].astype(F32)
                weighted[rows, lanes(b)] = (e * residual).astype(BF16)
                left = jnp.where(at_first, before[b], right_turn[b])
                right = jnp.where(at_last, after[b], left_turn[b])
                a_x, a_xg = add_up(residual * (right - left), at, a_x, a_xg)
                down = pbuf[b, pl.ds(base + 9, CH)]
                up = pbuf[b, pl.ds(base + 7, CH)]
                a_y, a_yg = add_up(residual * (down - up), at, a_y, a_yg)
                squares = residual * p
                a_e = a_e + squares.reshape(CH // 8, 8, 128).sum(axis=0)
                result.append((a_x, a_xg, a_y, a_yg, a_e))
            return tuple(result)

        zero = jnp.zeros((8, 128), F32)
        parts = ((zero,) * 5,) * 3
        predict(0, 256)
        for k in range(0, 7):
            parts = terms(k, parts)
        predict(256, 384)
        tall = (((0,), (0,)), ((), ()))
        for k in range(7, 12):
            parts = terms(k, parts)
        back = lax.dot_general(row_mat, weighted[...], tall, preferred_element_type=F32)
        for b in range(3):
            for n in range(5):
                sums_ref[m, n, :, lanes(b)] = parts[b][n]
        back_pass = back.astype(BF16)

        def pull(k):
            base = k * CH
            rows = pl.ds(pl.multiple_of(oy + base, CH), CH)
            rows_y = pl.ds(pl.multiple_of(oy + base + 8, 8), CH)
            for b in range(3):
                t = tbuf[b, pl.ds(base, CH)]
                wg = w_ref[ob + b, rows] * grad[b, pl.ds(base, CH)]
                gx_ref[ob + b, rows] = gx_ref[ob + b, rows] - wg * (s1 + t * sx_ref[ob + b, rows])
                gy_ref[ob + b, rows_y] = gy_ref[ob + b, rows_y] - wg * (
                    s2 + t * sy_ref[ob + b, rows]
                )

        for low, high in ((0, 256), (256, C)):
            block = jnp.dot(back_pass[low:high], col_mat, preferred_element_type=F32)
            for b in range(3):
                grad[b, low:high] = block[:, lanes(b)]
            for k in range(low // CH, high // CH):
                pull(k)

    @pl.when((slot_odd == 1) & any_used)
    def _():
        def stencil(k, half):
            base = pl.multiple_of(k * CH, CH)
            rows = pl.ds(base, CH)
            to = pl.ds(pl.multiple_of(base - half * HALF, CH), CH)
            here = [gx_ref[b, rows] for b in range(4)]
            right_turn = [pltpu.roll(g, 1, 1) for g in here]
            left_turn = [pltpu.roll(g, 127, 1) for g in here]
            blank = jnp.zeros((CH, 128), F32)
            before = [blank] + right_turn[:3]
            after = left_turn[1:] + [blank]
            for b in range(4):
                left = jnp.where(at_first, before[b], right_turn[b])
                right = jnp.where(at_last, after[b], left_turn[b])
                up = gy_ref[b, pl.ds(base + 7, CH)]
                down = gy_ref[b, pl.ds(base + 9, CH)]
                total = (left - right) + (up - down)
                out_ref[0, half, to, lanes(b)] = (0.5 * total).astype(BF16)

        def stencil_block(k, _):
            for n in range(4):
                stencil(4 * k + n, k // 2)
            return 0

        lax.fori_loop(low_block, high_block, stencil_block, 0)
        sub = lax.broadcasted_iota(I32, (16, 128), 0)
        lane16 = lax.broadcasted_iota(I32, (16, 128), 1)

        @pl.when(low_block == 1)
        def _():
            for b in range(4):
                out_ref[0, 0, 0:112, lanes(b)] = jnp.zeros((112, 128), BF16)
                edge = jnp.where(sub == 15, -0.5 * gy_ref[b, 136:137], 0.0)
                out_ref[0, 0, 112:128, lanes(b)] = edge.astype(BF16)

        @pl.when(high_block == 3)
        def _():
            for b in range(4):
                edge = jnp.where(sub == 0, 0.5 * gy_ref[b, C + 7 : C + 8], 0.0)
                out_ref[0, 1, 128:144, lanes(b)] = edge.astype(BF16)
                out_ref[0, 1, 144:256, lanes(b)] = jnp.zeros((112, 128), BF16)

        pick_low = jnp.where((sub == 1) & (lane16 == 0), -0.5, 0.0).astype(BF16)
        pick_high = jnp.where((sub == 2) & (lane16 == 127), 0.5, 0.0).astype(BF16)
        cross = (((1,), (1,)), ((), ()))
        for half in range(2):
            rows = slice(HALF * half, HALF * (half + 1))
            spill = lax.dot_general(
                pick_low, gx_ref[0, rows].astype(BF16), cross, preferred_element_type=F32
            ) + lax.dot_general(
                pick_high, gx_ref[3, rows].astype(BF16), cross, preferred_element_type=F32
            )
            for b in range(4):
                edge = 0.5 * gy_ref[b, T + 7 : T + 8] if half else -0.5 * gy_ref[b, 8:9]
                rest = spill[:, lanes(b)] if b < 2 else jnp.zeros((16, 128), F32)
                out_ref[0, half, HALF:BACK, lanes(b)] = jnp.where(sub == 0, edge, rest).astype(
                    BF16
                )

    @pl.when((slot_odd == 1) & jnp.logical_not(any_used))
    def _():
        out_ref[...] = jnp.zeros_like(out_ref)


SCRATCH = [
    pltpu.VMEM((2, PIECE - HALF, T), I32),
    pltpu.VMEM((4, T, 128), I32),
    pltpu.VMEM((4, T + 16, 128), F32),
    pltpu.VMEM((2, T, 128), F32),
    pltpu.VMEM((4, T, 128), F32),
    pltpu.VMEM((4, T, 128), F32),
    pltpu.VMEM((4, T, 128), F32),
    pltpu.VMEM((4, T, 128), F32),
    pltpu.VMEM((4, T, 128), F32),
    pltpu.VMEM((4, T + 16, 128), F32),
    pltpu.VMEM((C, C), BF16),
    pltpu.VMEM((3, C, 128), F32),
    pltpu.VMEM((3, C + 16, 128), F32),
    pltpu.VMEM((C, C), BF16),
    pltpu.VMEM((3, C, 128), F32),
]


def run_tiles(arrays, pieces, resample, observed, plan, sun, gain):
    used, image, row_off, col_off = plan
    count = len(pieces)
    tile_specs = [pl.BlockSpec(v.shape, lambda i, *s: (0, 0, 0)) for v in arrays]
    grid_spec = pltpu.PrefetchScalarGridSpec(
        num_scalar_prefetch=6,
        grid=(2 * count,),
        in_specs=tile_specs
        + [
            pl.BlockSpec((1, 2, C, C), lambda i, u, m, *s: (m[i], 0, 0, 0)),
            pl.BlockSpec((1, C, C), lambda i, u, m, *s: (m[i], 0, 0)),
        ],
        out_specs=[
            pl.BlockSpec((1, 2, BACK, T), lambda i, *s: (i // 2, 0, 0, 0)),
            pl.BlockSpec((16, 5, 8, C), lambda i, *s: (0, 0, 0, 0)),
        ],
        scratch_shapes=SCRATCH,
    )
    return pl.pallas_call(
        functools.partial(tile_kernel, pieces, len(arrays)),
        grid_spec=grid_spec,
        out_shape=[
            jax.ShapeDtypeStruct((count, 2, BACK, T), BF16),
            jax.ShapeDtypeStruct((16, 5, 8, C), F32),
        ],
        compiler_params=pltpu.CompilerParams(dimension_semantics=("arbitrary",)),
        cost_estimate=pl.CostEstimate(
            flops=count * 8 * C * C * C, bytes_accessed=count * 8_000_000, transcendentals=0
        ),
    )(used, image, row_off, col_off, sun, gain, *arrays, resample, observed)


def around(step_x, step_y):
    return [
        (4 * y + x, 4 * ((y + step_y) % 4) + (x + step_x) % 4) for y in range(4) for x in range(4)
    ]


STEPS = {"x+": around(1, 0), "x-": around(-1, 0), "y+": around(0, 1), "y-": around(0, -1)}
STEPS["x2"] = around(2, 0)
STEPS["y2"] = around(0, 2)
WAYS = ("x+", "x-", "y+", "y-")
WAYS_BACK = ("x-", "x+", "y-", "y+")
NEAR = [(0, 0), (-1, 0), (1, 0), (0, -1), (0, 1)]
MIDDLE = [(-1, -1), (-1, 1), (1, -1), (1, 1), (2, 0), (0, 2)]
FAR = [(2, -1), (2, 1), (-1, 2), (1, 2), (2, 2)]


def send(messages):
    return {way: lax.ppermute(v, "dy", STEPS[way]) for way, v in messages.items()}


def send_middle(near):
    a = {k: v[0] for k, v in near.items()}
    b = {k: v[1] for k, v in near.items()}
    return send(
        {
            "x+": jnp.stack([a["x+"], b["y+"], b["y-"]]),
            "x-": jnp.stack([b["x-"], b["y+"], b["y-"]]),
            "y+": jnp.stack([a["y+"], a["x+"], a["x-"]]),
            "y-": jnp.stack([b["y-"], a["x+"], a["x-"]]),
        }
    )


def send_far(middle):
    return send(
        {
            "x+": jnp.stack([middle["y+"][1], middle["y-"][1]]),
            "x-": middle["x-"][1:3],
            "y+": middle["y+"][1:3],
            "y-": jnp.stack([middle["x+"][2], middle["x-"][2]]),
            "x2": middle["y+"][0:1],
            "y2": middle["x-"][0:1],
        }
    )


def return_sums(near, middle, far):
    def wide(v):
        return v.astype(F32)

    def slim(v):
        return v.astype(BF16)

    flat = far.reshape((10,) + far.shape[2:])
    got = send(
        {
            "x2": flat[8:9],
            "y2": flat[9:10],
            "x-": flat[0:3],
            "y-": flat[4:7],
            "x+": flat[3:4],
            "y+": flat[7:8],
        }
    )
    xm, xp, ym, yp = (got[k] for k in WAYS_BACK)
    b_20 = slim(wide(middle[4, 1]) + wide(got["y2"][0]))
    a_02 = slim(wide(middle[5, 0]) + wide(got["x2"][0]))
    a_mm = slim(wide(middle[0, 0]) + wide(xm[0]) + wide(ym[0]))
    b_mm = slim(wide(middle[0, 1]) + wide(xm[1]) + wide(ym[1]))
    a_mp = slim(wide(middle[1, 0]) + wide(xm[2]))
    a_pm = slim(wide(middle[2, 0]) + wide(ym[2]))
    b_pp = slim(wide(middle[3, 1]) + wide(xp[0]) + wide(yp[0]))
    got = send(
        {
            "x-": jnp.stack([middle[4, 0], b_mm, middle[1, 1]]),
            "x+": jnp.stack([b_20, middle[2, 1], b_pp]),
            "y-": jnp.stack([a_02, a_mm, a_pm]),
            "y+": jnp.stack([middle[5, 1], a_mp, middle[3, 0]]),
        }
    )
    xm, xp, ym, yp = (got[k] for k in WAYS_BACK)

    def total(*pieces):
        result = wide(pieces[0])
        for piece in pieces[1:]:
            result = result + wide(piece)
        return slim(result)

    got = send(
        {
            "x-": jnp.stack([total(near[1, 0], xm[0], ym[1], yp[1]), near[1, 1]]),
            "x+": jnp.stack([total(near[2, 0], ym[2], yp[2]), total(near[2, 1], xp[0])]),
            "y-": jnp.stack([total(near[3, 0], ym[0]), total(near[3, 1], xm[1], xp[1])]),
            "y+": jnp.stack([near[4, 0], total(near[4, 1], xm[2], xp[2], yp[0])]),
        }
    )
    result = wide(near[0])
    for way in WAYS_BACK:
        result = result + wide(got[way])
    return result


def next_images(used, image):
    count = used.shape[0]
    ids = jnp.arange(count, dtype=I32)
    is_used = used == 1
    ahead = jnp.min(
        jnp.where(is_used[None, :] & (ids[None, :] >= ids[:, None]), ids[None, :], count), axis=1
    )
    last = jnp.maximum(jnp.max(jnp.where(is_used, ids, -1)), 0)
    at = jnp.where(ahead < count, ahead, last)
    return jnp.sum(jnp.where(at[:, None] == ids[None, :], image[None, :], 0), axis=1)


def sun_vectors(azimuth, elevation):
    return jnp.stack(
        [
            jnp.cos(elevation) * jnp.cos(azimuth),
            jnp.cos(elevation) * jnp.sin(azimuth),
            jnp.sin(elevation),
        ]
    )


def laplace(padded):
    return (
        padded[:-2, 1:-1]
        + padded[2:, 1:-1]
        + padded[1:-1, :-2]
        + padded[1:-1, 2:]
        - 4.0 * padded[1:-1, 1:-1]
    )


def shifted(value, axis, up):
    count = lax.axis_size(axis)
    pairs = [(i, i + 1) for i in range(count - 1)]
    return lax.ppermute(value, axis, pairs if up else [(b, a) for a, b in pairs])


def quantize(heights):
    return jnp.round(heights * H_SCALE).astype(I32)


def smoothness(heights, top, bottom):
    tall = jnp.concatenate([top, heights, bottom], axis=0)
    left = shifted(tall[:, -2:], "dx", True)
    right = shifted(tall[:, :2], "dx", False)
    wide = jnp.concatenate([left, tall, right], axis=1)
    field = laplace(wide)
    rows, cols = heights.shape
    row_ids = jnp.arange(rows + 2)
    col_ids = jnp.arange(cols + 2)
    row_keep = ~(
        (row_ids == 0) & (lax.axis_index("dy") == 0)
        | (row_ids == rows + 1) & (lax.axis_index("dy") == lax.axis_size("dy") - 1)
    )
    col_keep = ~(
        (col_ids == 0) & (lax.axis_index("dx") == 0)
        | (col_ids == cols + 1) & (lax.axis_index("dx") == lax.axis_size("dx") - 1)
    )
    return SMOOTHING_WEIGHT * laplace(jnp.where(row_keep[:, None] & col_keep[None, :], field, 0.0))


def finish_sums(parts):
    ids = jnp.arange(C, dtype=F32)
    coord = (ids - 0.5 * (C - 1)) / C
    edge = jnp.where((ids == 0) | (ids == C - 1), 1.0, 0.5)
    start = (jnp.arange(8, dtype=F32) - 0.5 * (C - 1)) / C
    x_sum, x_row, y_sum, y_row, e_sum = (parts[:, n] for n in range(5))
    x_v = x_row / C + x_sum * start[None, :, None]
    y_v = y_row / C + y_sum * start[None, :, None]

    def total(v):
        return jnp.sum(v, axis=(1, 2))

    pose = [
        total(x_sum * edge),
        total(x_sum * (edge * coord)),
        total(x_v * edge),
        total(y_sum) * 0.5,
        total(y_sum * coord) * 0.5,
        total(y_v) * 0.5,
    ]
    return jnp.concatenate(
        [jnp.stack(pose, axis=-1) / C, (total(e_sum) / (C * C))[:, None]], axis=-1
    )


def per_device(
    heights, albedo, observed, resample, exposure, sun_azimuth, sun_elevation, send_plan, recv_plan
):
    offsets = send_plan[0, 0, 0:2].reshape(2, 16, 2).transpose(1, 0, 2)
    offsets = lax.all_to_all(offsets, "dy", split_axis=0, concat_axis=0, tiled=True)
    row_off = offsets[:, 0].reshape(-1)
    col_off = offsets[:, 1].reshape(-1)
    slots = jnp.arange(32, dtype=I32)
    match = recv_plan[0, 0][None, :] == slots[:, None]
    used = jnp.any(match, axis=1).astype(I32)
    image = jnp.sum(jnp.where(match, jnp.arange(16, dtype=I32)[None, :], 0), axis=1)
    table = jnp.stack([used, image, row_off, col_off])
    relative = jnp.array(NEAR + MIDDLE + FAR, I32)
    place = lax.axis_index("dy")
    tile_ids = ((place // 4 + relative[:, 1]) % 4) * 4 + (place % 4 + relative[:, 0]) % 4
    slot_ids = (2 * tile_ids[:, None] + jnp.arange(2, dtype=I32)[None, :]).reshape(-1)
    table = jnp.sum(
        jnp.where(slot_ids[None, :, None] == slots[None, None, :], table[:, None, :], 0), axis=2
    )

    def plan_of(first, count):
        part = table[:, 2 * first : 2 * (first + count)]
        return part[0], next_images(part[0], part[1]), part[2], part[3]

    sun = sun_vectors(sun_azimuth[0], sun_elevation[0]).reshape(-1)
    gain = jnp.exp(exposure[0])

    top = shifted(heights[-2:], "dy", True)
    bottom = shifted(heights[:2], "dy", False)
    left = shifted(heights[:, -1], "dx", True)
    right = shifted(heights[:, 0], "dx", False)
    sides = pack(quantize(left), quantize(right)).reshape(2, 1, HALF)
    sides = jnp.concatenate([sides, jnp.zeros((2, 1, T - HALF), I32)], axis=2)
    ends = pack(quantize(jnp.stack([top[1:2], bottom[0:1]])), 0)
    words = pack(quantize(heights), jnp.round((albedo - 1.0) * A_SCALE).astype(I32))
    words = jnp.concatenate(
        [words.reshape(2, HALF, T), sides, ends, jnp.zeros((2, PIECE - HALF - 2, T), I32)], axis=1
    )
    near = send({way: words for way in WAYS})
    middle = send_middle(near)
    far = send_far(middle)
    order = WAYS
    out_near, parts = run_tiles(
        [words] + [near[k] for k in order],
        [((n, 0), (n, 1)) for n in range(5)],
        resample, observed, plan_of(0, 5), sun, gain,
    )
    out_middle, more = run_tiles(
        [middle[k] for k in order],
        [
            ((2, 1), (0, 1)),
            ((3, 1), (0, 2)),
            ((2, 2), (1, 1)),
            ((3, 2), (1, 2)),
            ((0, 0), (1, 0)),
            ((2, 0), (3, 0)),
        ],
        resample, observed, plan_of(5, 6), sun, gain,
    )
    parts = parts + more
    out_far, more = run_tiles(
        [far[k] for k in order] + [far["x2"], far["y2"]],
        [
            ((0, 0), (1, 0)),
            ((0, 1), (1, 1)),
            ((2, 0), (3, 0)),
            ((2, 1), (3, 1)),
            ((4, 0), (5, 0)),
        ],
        resample, observed, plan_of(11, 5), sun, gain,
    )
    parts = parts + more
    smooth = smoothness(heights, top, bottom)
    crop_sums = finish_sums(parts)
    arrived = lax.all_to_all(crop_sums[:, None], "dy", split_axis=0, concat_axis=0, tiled=True)
    camera = arrived.sum(axis=0)
    own = return_sums(out_near, out_middle, out_far)
    from_below = shifted(own[0, HALF], "dy", False)
    from_above = shifted(own[1, HALF], "dy", True)
    from_right = shifted(own[:, HALF + 1, :HALF].reshape(-1), "dx", False)
    from_left = shifted(own[:, HALF + 2, :HALF].reshape(-1), "dx", True)
    row_ids = lax.broadcasted_iota(I32, (T, T), 0)
    col_ids = lax.broadcasted_iota(I32, (T, T), 1)
    data = own[:, :HALF].reshape(T, T)
    data = data + jnp.where(row_ids == T - 1, from_below[None, :], 0.0)
    data = data + jnp.where(row_ids == 0, from_above[None, :], 0.0)
    data = data + jnp.where(col_ids == T - 1, from_right[:, None], 0.0)
    data = data + jnp.where(col_ids == 0, from_left[:, None], 0.0)
    return (data + smooth, camera[None])


def solution(mesh):
    placed = (
        P("dy", "dx"),
        P("dy", "dx"),
        P(("dy", "dx"), None, None),
        P(("dy", "dx"), None, None, None),
        P("dx", None),
        P("dx", None),
        P("dx", None),
        P("dy", "dx", None, None),
        P("dy", "dx", None),
    )

    return jax.shard_map(
        per_device,
        mesh=mesh,
        in_specs=placed,
        out_specs=(P("dy", "dx"), P("dx", "dy", None)),
        check_vma=False,
    )
```

```python
import functools

import jax
import jax.numpy as jnp
from jax import lax
from jax.experimental import pallas as pl
from jax.experimental.pallas import tpu as pltpu
from jax.sharding import PartitionSpec as P


SMOOTHING_WEIGHT = 0.02
H_SCALE = 8191.0
A_SCALE = 65534.0
T = 512
C = 384
HALF = 256
PIECE = 264
BACK = 272
CH = 32
F32 = jnp.float32
BF16 = jnp.bfloat16
I32 = jnp.int32


def pack(high, low):
    return lax.shift_left(high, 16) | (low & 0xFFFF)


def high_of(word):
    return lax.shift_right_arithmetic(word, 16).astype(F32)


def low_of(word):
    return lax.shift_right_arithmetic(lax.shift_left(word, 16), 16).astype(F32)


def tile_kernel(pieces, operands, *refs):
    used, image, row_off, col_off, sun, gain = refs[:6]
    tiles = refs[6 : 6 + operands]
    (
        res_ref, obs_ref,
        out_ref, sums_ref,
        rim, words_ref, hbuf, hcol, sx_ref, sy_ref, w_ref, r2_ref, gx_ref, gy_ref,
        shaded, tbuf, pbuf, weighted, grad,
    ) = refs[6 + operands :]
    step = pl.program_id(0)
    first = (step // 2) * 2
    slot_odd = step % 2
    mine = used[step] == 1
    any_used = used[first] + used[first + 1] > 0
    low_row = jnp.minimum(
        jnp.where(used[first] == 1, row_off[first], 128),
        jnp.where(used[first + 1] == 1, row_off[first + 1], 128),
    )
    high_row = C + jnp.maximum(
        jnp.where(used[first] == 1, row_off[first], 0),
        jnp.where(used[first + 1] == 1, row_off[first + 1], 0),
    )
    low_block = low_row // 128
    high_block = high_row // 128
    lane = lax.broadcasted_iota(I32, (CH, 128), 1)
    at_first = lane == 0
    at_last = lane == 127

    def lanes(b):
        return slice(128 * b, 128 * (b + 1))

    @pl.when(step == 0)
    def _():
        sums_ref[...] = jnp.zeros_like(sums_ref)

    for t, sources in enumerate(pieces):

        @pl.when((step == 2 * t) & any_used)
        def _(sources=sources):
            for half, (operand, at) in enumerate(sources):
                ref = tiles[operand]
                rim[half] = ref[at, HALF:PIECE]

                def unpack(k, _, ref=ref, at=at, half=half):
                    base = pl.multiple_of(k * 64, 64)
                    to = pl.multiple_of(base + HALF * half, 64)
                    for b in range(4):
                        words = ref[at, pl.ds(base, 64), lanes(b)]
                        hbuf[b, pl.ds(to + 8, 64)] = high_of(words)
                        words_ref[b, pl.ds(to, 64)] = words
                    return 0

                if half:
                    lax.fori_loop(0, high_block, unpack, 0)
                else:
                    lax.fori_loop(low_block, 4, unpack, 0)

    @pl.when((slot_odd == 0) & any_used)
    def _():
        row_id = lax.broadcasted_iota(I32, (32, 256), 0)
        side = lax.broadcasted_iota(I32, (32, 256), 1) // 128
        scale = jnp.where(row_id == 16 * side, 256.0, 0.0) + jnp.where(
            row_id == 16 * side + 8, 1.0, 0.0
        )
        for half in range(2):
            words = rim[half, :, 0:HALF]
            high = lax.shift_right_arithmetic(words, 16)
            low = lax.shift_right_arithmetic(lax.shift_left(words, 16), 16)
            parts = jnp.concatenate(
                [
                    lax.shift_right_arithmetic(high, 8),
                    high & 255,
                    lax.shift_right_arithmetic(low, 8),
                    low & 255,
                ],
                axis=0,
            ).astype(F32).astype(BF16)
            columns = lax.dot_general(
                parts, scale.astype(BF16), (((0,), (0,)), ((), ())), preferred_element_type=F32
            )
            for side_id in range(2):
                hcol[side_id, HALF * half : HALF * (half + 1)] = columns[:, lanes(side_id)]
        top = high_of(rim[0])
        bottom = high_of(rim[1])
        for b in range(4):
            hbuf[b, 7:8] = top[1:2, lanes(b)]
            hbuf[b, T + 8 : T + 9] = bottom[1:2, lanes(b)]
            for at in (0, 8, 128, C + 8, T, T + 8):
                gy_ref[b, at : at + 8] = jnp.zeros((8, 128), F32)
        for b in (0, 3):
            gx_ref[b, 0:128] = jnp.zeros((128, 128), F32)
            gx_ref[b, C:T] = jnp.zeros((128, 128), F32)

        def slope(k):
            base = pl.multiple_of(k * CH, CH)
            rows = pl.ds(base, CH)
            here = [hbuf[b, pl.ds(base + 8, CH)] for b in range(4)]
            right_turn = [pltpu.roll(h, 1, 1) for h in here]
            left_turn = [pltpu.roll(h, 127, 1) for h in here]
            before = [hcol[0, rows]] + right_turn[:3]
            after = left_turn[1:] + [hcol[1, rows]]
            for b in range(4):
                left = jnp.where(at_first, before[b], right_turn[b])
                right = jnp.where(at_last, after[b], left_turn[b])
                sx = (right - left) * (0.5 / H_SCALE)
                sy = (hbuf[b, pl.ds(base + 9, CH)] - hbuf[b, pl.ds(base + 7, CH)]) * (
                    0.5 / H_SCALE
                )
                albedo = low_of(words_ref[b, rows]) * (1.0 / A_SCALE) + 1.0
                r = lax.rsqrt(1.0 + sx * sx + sy * sy)
                sx_ref[b, rows] = sx
                sy_ref[b, rows] = sy
                w_ref[b, rows] = albedo * r
                r2_ref[b, rows] = r * r
                gx_ref[b, rows] = jnp.zeros((CH, 128), F32)
                gy_ref[b, pl.ds(base + 8, CH)] = jnp.zeros((CH, 128), F32)

        def slope_block(k, _):
            for n in range(4):
                slope(4 * k + n)
            return 0

        lax.fori_loop(low_block, high_block, slope_block, 0)

    @pl.when(mine)
    def _():
        m = image[step]
        oy = pl.multiple_of(row_off[step], 128)
        ob = col_off[step] // 128
        s1 = sun[m]
        s2 = sun[16 + m]
        s3 = sun[32 + m]
        e = gain[m]

        def shade(k):
            base = k * CH
            rows = pl.ds(pl.multiple_of(oy + base, CH), CH)
            for b in range(3):
                q = s3 - s1 * sx_ref[ob + b, rows] - s2 * sy_ref[ob + b, rows]
                shaded[pl.ds(base, CH), lanes(b)] = (w_ref[ob + b, rows] * q).astype(BF16)
                tbuf[b, pl.ds(base, CH)] = q * r2_ref[ob + b, rows]

        for k in range(C // CH):
            shade(k)
        row_mat = res_ref[0, 0]
        col_mat = res_ref[0, 1]
        first_pass = jnp.dot(row_mat, shaded[...], preferred_element_type=F32).astype(BF16)

        def predict(low, high):
            block = e * lax.dot_general(
                first_pass[low:high],
                col_mat,
                (((1,), (1,)), ((), ())),
                preferred_element_type=F32,
            )
            for b in range(3):
                pbuf[b, 8 + low : 8 + high] = block[:, lanes(b)]
                if low == 0:
                    pbuf[b, 7:8] = 2.0 * block[0:1, lanes(b)] - block[1:2, lanes(b)]
                if high == C:
                    end = high - low
                    pbuf[b, C + 8 : C + 9] = (
                        2.0 * block[end - 1 : end, lanes(b)] - block[end - 2 : end - 1, lanes(b)]
                    )

        def add_up(v, base, total, by_row):
            groups = [v[8 * g : 8 * g + 8] for g in range(CH // 8)]
            tail = groups[-1]
            lead = tail
            for g in range(CH // 8 - 2, 0, -1):
                tail = groups[g] + tail
                lead = lead + tail
            tail = groups[0] + tail
            return total + tail, by_row + lead * 8.0 + tail * base

        def terms(k, carry):
            base = k * CH
            at = float(base)
            rows = pl.ds(base, CH)
            here = [pbuf[b, pl.ds(base + 8, CH)] for b in range(3)]
            right_turn = [pltpu.roll(p, 1, 1) for p in here]
            left_turn = [pltpu.roll(p, 127, 1) for p in here]
            before = [here[0]] + right_turn[:2]
            after = left_turn[1:] + [here[2]]
            result = []
            for b in range(3):
                a_x, a_xg, a_y, a_yg, a_e = carry[b]
                p = here[b]
                residual = p - obs_ref[0, rows, lanes(b)].astype(F32)
                weighted[rows, lanes(b)] = (e * residual).astype(BF16)
                left = jnp.where(at_first, before[b], right_turn[b])
                right = jnp.where(at_last, after[b], left_turn[b])
                a_x, a_xg = add_up(residual * (right - left), at, a_x, a_xg)
                down = pbuf[b, pl.ds(base + 9, CH)]
                up = pbuf[b, pl.ds(base + 7, CH)]
                a_y, a_yg = add_up(residual * (down - up), at, a_y, a_yg)
                squares = residual * p
                a_e = a_e + squares.reshape(CH // 8, 8, 128).sum(axis=0)
                result.append((a_x, a_xg, a_y, a_yg, a_e))
            return tuple(result)

        zero = jnp.zeros((8, 128), F32)
        parts = ((zero,) * 5,) * 3
        predict(0, 256)
        for k in range(0, 7):
            parts = terms(k, parts)
        predict(256, 384)
        tall = (((0,), (0,)), ((), ()))
        for k in range(7, 12):
            parts = terms(k, parts)
        back = lax.dot_general(row_mat, weighted[...], tall, preferred_element_type=F32)
        for b in range(3):
            for n in range(5):
                sums_ref[m, n, :, lanes(b)] = parts[b][n]
        back_pass = back.astype(BF16)

        def pull(k):
            base = k * CH
            rows = pl.ds(pl.multiple_of(oy + base, CH), CH)
            rows_y = pl.ds(pl.multiple_of(oy + base + 8, 8), CH)
            for b in range(3):
                t = tbuf[b, pl.ds(base, CH)]
                wg = w_ref[ob + b, rows] * grad[b, pl.ds(base, CH)]
                gx_ref[ob + b, rows] = gx_ref[ob + b, rows] - wg * (s1 + t * sx_ref[ob + b, rows])
                gy_ref[ob + b, rows_y] = gy_ref[ob + b, rows_y] - wg * (
                    s2 + t * sy_ref[ob + b, rows]
                )

        for low, high in ((0, 256), (256, C)):
            block = jnp.dot(back_pass[low:high], col_mat, preferred_element_type=F32)
            for b in range(3):
                grad[b, low:high] = block[:, lanes(b)]
            for k in range(low // CH, high // CH):
                pull(k)

    @pl.when((slot_odd == 1) & any_used)
    def _():
        def stencil(k, half):
            base = pl.multiple_of(k * CH, CH)
            rows = pl.ds(base, CH)
            to = pl.ds(pl.multiple_of(base - half * HALF, CH), CH)
            here = [gx_ref[b, rows] for b in range(4)]
            right_turn = [pltpu.roll(g, 1, 1) for g in here]
            left_turn = [pltpu.roll(g, 127, 1) for g in here]
            blank = jnp.zeros((CH, 128), F32)
            before = [blank] + right_turn[:3]
            after = left_turn[1:] + [blank]
            for b in range(4):
                left = jnp.where(at_first, before[b], right_turn[b])
                right = jnp.where(at_last, after[b], left_turn[b])
                up = gy_ref[b, pl.ds(base + 7, CH)]
                down = gy_ref[b, pl.ds(base + 9, CH)]
                total = (left - right) + (up - down)
                out_ref[0, half, to, lanes(b)] = (0.5 * total).astype(BF16)

        def stencil_block(k, _):
            for n in range(4):
                stencil(4 * k + n, k // 2)
            return 0

        lax.fori_loop(low_block, high_block, stencil_block, 0)
        sub = lax.broadcasted_iota(I32, (16, 128), 0)
        lane16 = lax.broadcasted_iota(I32, (16, 128), 1)

        @pl.when(low_block == 1)
        def _():
            for b in range(4):
                out_ref[0, 0, 0:112, lanes(b)] = jnp.zeros((112, 128), BF16)
                edge = jnp.where(sub == 15, -0.5 * gy_ref[b, 136:137], 0.0)
                out_ref[0, 0, 112:128, lanes(b)] = edge.astype(BF16)

        @pl.when(high_block == 3)
        def _():
            for b in range(4):
                edge = jnp.where(sub == 0, 0.5 * gy_ref[b, C + 7 : C + 8], 0.0)
                out_ref[0, 1, 128:144, lanes(b)] = edge.astype(BF16)
                out_ref[0, 1, 144:256, lanes(b)] = jnp.zeros((112, 128), BF16)

        pick_low = jnp.where((sub == 1) & (lane16 == 0), -0.5, 0.0).astype(BF16)
        pick_high = jnp.where((sub == 2) & (lane16 == 127), 0.5, 0.0).astype(BF16)
        cross = (((1,), (1,)), ((), ()))
        for half in range(2):
            rows = slice(HALF * half, HALF * (half + 1))
            spill = lax.dot_general(
                pick_low, gx_ref[0, rows].astype(BF16), cross, preferred_element_type=F32
            ) + lax.dot_general(
                pick_high, gx_ref[3, rows].astype(BF16), cross, preferred_element_type=F32
            )
            for b in range(4):
                edge = 0.5 * gy_ref[b, T + 7 : T + 8] if half else -0.5 * gy_ref[b, 8:9]
                rest = spill[:, lanes(b)] if b < 2 else jnp.zeros((16, 128), F32)
                out_ref[0, half, HALF:BACK, lanes(b)] = jnp.where(sub == 0, edge, rest).astype(
                    BF16
                )

    @pl.when((slot_odd == 1) & jnp.logical_not(any_used))
    def _():
        out_ref[...] = jnp.zeros_like(out_ref)


SCRATCH = [
    pltpu.VMEM((2, PIECE - HALF, T), I32),
    pltpu.VMEM((4, T, 128), I32),
    pltpu.VMEM((4, T + 16, 128), F32),
    pltpu.VMEM((2, T, 128), F32),
    pltpu.VMEM((4, T, 128), F32),
    pltpu.VMEM((4, T, 128), F32),
    pltpu.VMEM((4, T, 128), F32),
    pltpu.VMEM((4, T, 128), F32),
    pltpu.VMEM((4, T, 128), F32),
    pltpu.VMEM((4, T + 16, 128), F32),
    pltpu.VMEM((C, C), BF16),
    pltpu.VMEM((3, C, 128), F32),
    pltpu.VMEM((3, C + 16, 128), F32),
    pltpu.VMEM((C, C), BF16),
    pltpu.VMEM((3, C, 128), F32),
]


def run_tiles(arrays, pieces, resample, observed, plan, sun, gain):
    used, image, row_off, col_off = plan
    count = len(pieces)
    tile_specs = [pl.BlockSpec(v.shape, lambda i, *s: (0, 0, 0)) for v in arrays]
    grid_spec = pltpu.PrefetchScalarGridSpec(
        num_scalar_prefetch=6,
        grid=(2 * count,),
        in_specs=tile_specs
        + [
            pl.BlockSpec((1, 2, C, C), lambda i, u, m, *s: (m[i], 0, 0, 0)),
            pl.BlockSpec((1, C, C), lambda i, u, m, *s: (m[i], 0, 0)),
        ],
        out_specs=[
            pl.BlockSpec((1, 2, BACK, T), lambda i, *s: (i // 2, 0, 0, 0)),
            pl.BlockSpec((16, 5, 8, C), lambda i, *s: (0, 0, 0, 0)),
        ],
        scratch_shapes=SCRATCH,
    )
    return pl.pallas_call(
        functools.partial(tile_kernel, pieces, len(arrays)),
        grid_spec=grid_spec,
        out_shape=[
            jax.ShapeDtypeStruct((count, 2, BACK, T), BF16),
            jax.ShapeDtypeStruct((16, 5, 8, C), F32),
        ],
        compiler_params=pltpu.CompilerParams(dimension_semantics=("arbitrary",)),
        cost_estimate=pl.CostEstimate(
            flops=count * 8 * C * C * C, bytes_accessed=count * 8_000_000, transcendentals=0
        ),
    )(used, image, row_off, col_off, sun, gain, *arrays, resample, observed)


def around(step_x, step_y):
    return [
        (4 * y + x, 4 * ((y + step_y) % 4) + (x + step_x) % 4) for y in range(4) for x in range(4)
    ]


STEPS = {"x+": around(1, 0), "x-": around(-1, 0), "y+": around(0, 1), "y-": around(0, -1)}
STEPS["x2"] = around(2, 0)
STEPS["y2"] = around(0, 2)
WAYS = ("x+", "x-", "y+", "y-")
WAYS_BACK = ("x-", "x+", "y-", "y+")
NEAR = [(0, 0), (-1, 0), (1, 0), (0, -1), (0, 1)]
MIDDLE = [(-1, -1), (-1, 1), (1, -1), (1, 1), (2, 0), (0, 2)]
FAR = [(2, -1), (2, 1), (-1, 2), (1, 2), (2, 2)]


def send(messages):
    return {way: lax.ppermute(v, "dy", STEPS[way]) for way, v in messages.items()}


def send_near(upper, lower):
    return send({way: upper for way in WAYS}), send({way: lower for way in WAYS})


def send_middle(upper, lower):
    ahead = send(
        {"x+": upper["x+"], "x-": lower["x-"], "y+": upper["y+"], "y-": lower["y-"]}
    )
    along_x = jnp.concatenate([lower["y+"], lower["y-"]])
    along_y = jnp.concatenate([upper["x+"], upper["x-"]])
    aside = send({"x+": along_x, "x-": along_x, "y+": along_y, "y-": along_y})
    return ahead, aside


def send_far(ahead, aside):
    pairs = send({"x-": aside["x-"], "y-": aside["y-"]})
    single = send(
        {
            "x2": ahead["y+"],
            "y2": ahead["x-"],
            "x-": ahead["y-"],
            "x+": ahead["y-"],
            "y-": ahead["x+"],
            "y+": ahead["x+"],
        }
    )
    return pairs, single


def return_sums(near, middle, far):
    def wide(v):
        return v.astype(F32)

    def slim(v):
        return v.astype(BF16)

    flat = far.reshape((10,) + far.shape[2:])
    got = send(
        {
            "x2": flat[8:9],
            "y2": flat[9:10],
            "x-": flat[0:3],
            "y-": flat[4:7],
            "x+": flat[3:4],
            "y+": flat[7:8],
        }
    )
    xm, xp, ym, yp = (got[k] for k in WAYS_BACK)
    b_20 = slim(wide(middle[4, 1]) + wide(got["y2"][0]))
    a_02 = slim(wide(middle[5, 0]) + wide(got["x2"][0]))
    a_mm = slim(wide(middle[0, 0]) + wide(xm[0]) + wide(ym[0]))
    b_mm = slim(wide(middle[0, 1]) + wide(xm[1]) + wide(ym[1]))
    a_mp = slim(wide(middle[1, 0]) + wide(xm[2]))
    a_pm = slim(wide(middle[2, 0]) + wide(ym[2]))
    b_pp = slim(wide(middle[3, 1]) + wide(xp[0]) + wide(yp[0]))
    got = send(
        {
            "x-": jnp.stack([middle[4, 0], b_mm, middle[1, 1]]),
            "x+": jnp.stack([b_20, middle[2, 1], b_pp]),
            "y-": jnp.stack([a_02, a_mm, a_pm]),
            "y+": jnp.stack([middle[5, 1], a_mp, middle[3, 0]]),
        }
    )
    xm, xp, ym, yp = (got[k] for k in WAYS_BACK)

    def total(*pieces):
        result = wide(pieces[0])
        for piece in pieces[1:]:
            result = result + wide(piece)
        return slim(result)

    got = send(
        {
            "x-": jnp.stack([total(near[1, 0], xm[0], ym[1], yp[1]), near[1, 1]]),
            "x+": jnp.stack([total(near[2, 0], ym[2], yp[2]), total(near[2, 1], xp[0])]),
            "y-": jnp.stack([total(near[3, 0], ym[0]), total(near[3, 1], xm[1], xp[1])]),
            "y+": jnp.stack([near[4, 0], total(near[4, 1], xm[2], xp[2], yp[0])]),
        }
    )
    result = wide(near[0])
    for way in WAYS_BACK:
        result = result + wide(got[way])
    return result


def next_images(used, image):
    count = used.shape[0]
    ids = jnp.arange(count, dtype=I32)
    is_used = used == 1
    ahead = jnp.min(
        jnp.where(is_used[None, :] & (ids[None, :] >= ids[:, None]), ids[None, :], count), axis=1
    )
    last = jnp.maximum(jnp.max(jnp.where(is_used, ids, -1)), 0)
    at = jnp.where(ahead < count, ahead, last)
    return jnp.sum(jnp.where(at[:, None] == ids[None, :], image[None, :], 0), axis=1)


def sun_vectors(azimuth, elevation):
    return jnp.stack(
        [
            jnp.cos(elevation) * jnp.cos(azimuth),
            jnp.cos(elevation) * jnp.sin(azimuth),
            jnp.sin(elevation),
        ]
    )


def laplace(padded):
    return (
        padded[:-2, 1:-1]
        + padded[2:, 1:-1]
        + padded[1:-1, :-2]
        + padded[1:-1, 2:]
        - 4.0 * padded[1:-1, 1:-1]
    )


def shifted(value, axis, up):
    count = lax.axis_size(axis)
    pairs = [(i, i + 1) for i in range(count - 1)]
    return lax.ppermute(value, axis, pairs if up else [(b, a) for a, b in pairs])


def quantize(heights):
    return jnp.round(heights * H_SCALE).astype(I32)


def smoothness(heights, top, bottom):
    tall = jnp.concatenate([top, heights, bottom], axis=0)
    left = shifted(tall[:, -2:], "dx", True)
    right = shifted(tall[:, :2], "dx", False)
    wide = jnp.concatenate([left, tall, right], axis=1)
    field = laplace(wide)
    rows, cols = heights.shape
    row_ids = jnp.arange(rows + 2)
    col_ids = jnp.arange(cols + 2)
    row_keep = ~(
        (row_ids == 0) & (lax.axis_index("dy") == 0)
        | (row_ids == rows + 1) & (lax.axis_index("dy") == lax.axis_size("dy") - 1)
    )
    col_keep = ~(
        (col_ids == 0) & (lax.axis_index("dx") == 0)
        | (col_ids == cols + 1) & (lax.axis_index("dx") == lax.axis_size("dx") - 1)
    )
    return SMOOTHING_WEIGHT * laplace(jnp.where(row_keep[:, None] & col_keep[None, :], field, 0.0))


def finish_sums(parts):
    ids = jnp.arange(C, dtype=F32)
    coord = (ids - 0.5 * (C - 1)) / C
    edge = jnp.where((ids == 0) | (ids == C - 1), 1.0, 0.5)
    start = (jnp.arange(8, dtype=F32) - 0.5 * (C - 1)) / C
    x_sum, x_row, y_sum, y_row, e_sum = (parts[:, n] for n in range(5))
    x_v = x_row / C + x_sum * start[None, :, None]
    y_v = y_row / C + y_sum * start[None, :, None]

    def total(v):
        return jnp.sum(v, axis=(1, 2))

    pose = [
        total(x_sum * edge),
        total(x_sum * (edge * coord)),
        total(x_v * edge),
        total(y_sum) * 0.5,
        total(y_sum * coord) * 0.5,
        total(y_v) * 0.5,
    ]
    return jnp.concatenate(
        [jnp.stack(pose, axis=-1) / C, (total(e_sum) / (C * C))[:, None]], axis=-1
    )


def per_device(
    heights, albedo, observed, resample, exposure, sun_azimuth, sun_elevation, send_plan, recv_plan
):
    offsets = send_plan[0, 0, 0:2].reshape(2, 16, 2).transpose(1, 0, 2)
    offsets = lax.all_to_all(offsets, "dy", split_axis=0, concat_axis=0, tiled=True)
    row_off = offsets[:, 0].reshape(-1)
    col_off = offsets[:, 1].reshape(-1)
    slots = jnp.arange(32, dtype=I32)
    match = recv_plan[0, 0][None, :] == slots[:, None]
    used = jnp.any(match, axis=1).astype(I32)
    image = jnp.sum(jnp.where(match, jnp.arange(16, dtype=I32)[None, :], 0), axis=1)
    table = jnp.stack([used, image, row_off, col_off])
    relative = jnp.array(NEAR + MIDDLE + FAR, I32)
    place = lax.axis_index("dy")
    tile_ids = ((place // 4 + relative[:, 1]) % 4) * 4 + (place % 4 + relative[:, 0]) % 4
    slot_ids = (2 * tile_ids[:, None] + jnp.arange(2, dtype=I32)[None, :]).reshape(-1)
    table = jnp.sum(
        jnp.where(slot_ids[None, :, None] == slots[None, None, :], table[:, None, :], 0), axis=2
    )

    def plan_of(first, count):
        part = table[:, 2 * first : 2 * (first + count)]
        return part[0], next_images(part[0], part[1]), part[2], part[3]

    sun = sun_vectors(sun_azimuth[0], sun_elevation[0]).reshape(-1)
    gain = jnp.exp(exposure[0])

    top = shifted(heights[-2:], "dy", True)
    bottom = shifted(heights[:2], "dy", False)
    left = shifted(heights[:, -1], "dx", True)
    right = shifted(heights[:, 0], "dx", False)
    sides = pack(quantize(left), quantize(right)).reshape(2, 1, HALF)
    sides = jnp.concatenate([sides, jnp.zeros((2, 1, T - HALF), I32)], axis=2)
    ends = pack(quantize(jnp.stack([top[1:2], bottom[0:1]])), 0)
    words = pack(quantize(heights), jnp.round((albedo - 1.0) * A_SCALE).astype(I32))
    blank = jnp.zeros((PIECE - HALF - 2, T), I32)
    upper, lower = (
        jnp.concatenate([words[HALF * n : HALF * (n + 1)], sides[n], ends[n], blank])[None]
        for n in range(2)
    )
    near_a, near_b = send_near(upper, lower)
    ahead, aside = send_middle(near_a, near_b)
    pairs, single = send_far(ahead, aside)
    out_near, parts = run_tiles(
        [upper] + [near_a[k] for k in WAYS] + [lower] + [near_b[k] for k in WAYS],
        [((n, 0), (n + 5, 0)) for n in range(5)],
        resample, observed, plan_of(0, 5), sun, gain,
    )
    out_middle, more = run_tiles(
        [aside[k] for k in WAYS] + [ahead[k] for k in WAYS],
        [
            ((2, 0), (0, 0)),
            ((3, 0), (0, 1)),
            ((2, 1), (1, 0)),
            ((3, 1), (1, 1)),
            ((4, 0), (5, 0)),
            ((6, 0), (7, 0)),
        ],
        resample, observed, plan_of(5, 6), sun, gain,
    )
    parts = parts + more
    out_far, more = run_tiles(
        [pairs["x-"], pairs["y-"]] + [single[k] for k in ("y+", "y-", "x+", "x-", "x2", "y2")],
        [
            ((2, 0), (0, 0)),
            ((3, 0), (0, 1)),
            ((1, 0), (4, 0)),
            ((1, 1), (5, 0)),
            ((6, 0), (7, 0)),
        ],
        resample, observed, plan_of(11, 5), sun, gain,
    )
    parts = parts + more
    smooth = smoothness(heights, top, bottom)
    crop_sums = finish_sums(parts)
    arrived = lax.all_to_all(crop_sums[:, None], "dy", split_axis=0, concat_axis=0, tiled=True)
    camera = arrived.sum(axis=0)
    own = return_sums(out_near, out_middle, out_far)
    from_below = shifted(own[0, HALF], "dy", False)
    from_above = shifted(own[1, HALF], "dy", True)
    from_right = shifted(own[:, HALF + 1, :HALF].reshape(-1), "dx", False)
    from_left = shifted(own[:, HALF + 2, :HALF].reshape(-1), "dx", True)
    row_ids = lax.broadcasted_iota(I32, (T, T), 0)
    col_ids = lax.broadcasted_iota(I32, (T, T), 1)
    data = own[:, :HALF].reshape(T, T)
    data = data + jnp.where(row_ids == T - 1, from_below[None, :], 0.0)
    data = data + jnp.where(row_ids == 0, from_above[None, :], 0.0)
    data = data + jnp.where(col_ids == T - 1, from_right[:, None], 0.0)
    data = data + jnp.where(col_ids == 0, from_left[:, None], 0.0)
    return (data + smooth, camera[None])


def solution(mesh):
    placed = (
        P("dy", "dx"),
        P("dy", "dx"),
        P(("dy", "dx"), None, None),
        P(("dy", "dx"), None, None, None),
        P("dx", None),
        P("dx", None),
        P("dx", None),
        P("dy", "dx", None, None),
        P("dy", "dx", None),
    )

    return jax.shard_map(
        per_device,
        mesh=mesh,
        in_specs=placed,
        out_specs=(P("dy", "dx"), P("dx", "dy", None)),
        check_vma=False,
    )
```

```python
import functools

import jax
import jax.numpy as jnp
from jax import lax
from jax.experimental import pallas as pl
from jax.experimental.pallas import tpu as pltpu
from jax.sharding import PartitionSpec as P


SMOOTHING_WEIGHT = 0.02
H_SCALE = 8191.0
A_SCALE = 65534.0
T = 512
C = 384
HALF = 256
PIECE = 264
BACK = 272
CH = 32
F32 = jnp.float32
BF16 = jnp.bfloat16
I32 = jnp.int32


def pack(high, low):
    return lax.shift_left(high, 16) | (low & 0xFFFF)


def high_of(word):
    return lax.shift_right_arithmetic(word, 16).astype(F32)


def low_of(word):
    return lax.shift_right_arithmetic(lax.shift_left(word, 16), 16).astype(F32)


def tile_kernel(pieces, operands, *refs):
    used, image, row_off, col_off, sun, gain = refs[:6]
    tiles = refs[6 : 6 + operands]
    (
        res_ref, obs_ref,
        out_ref, sums_ref,
        rim, words_ref, hbuf, hcol, sx_ref, sy_ref, w_ref, r2_ref, gx_ref, gy_ref,
        shaded, tbuf, pbuf, weighted, grad,
    ) = refs[6 + operands :]
    step = pl.program_id(0)
    first = (step // 2) * 2
    slot_odd = step % 2
    mine = used[step] == 1
    any_used = used[first] + used[first + 1] > 0
    low_row = jnp.minimum(
        jnp.where(used[first] == 1, row_off[first], 128),
        jnp.where(used[first + 1] == 1, row_off[first + 1], 128),
    )
    high_row = C + jnp.maximum(
        jnp.where(used[first] == 1, row_off[first], 0),
        jnp.where(used[first + 1] == 1, row_off[first + 1], 0),
    )
    low_block = low_row // 128
    high_block = high_row // 128
    lane = lax.broadcasted_iota(I32, (CH, 128), 1)
    at_first = lane == 0
    at_last = lane == 127

    def lanes(b):
        return slice(128 * b, 128 * (b + 1))

    @pl.when(step == 0)
    def _():
        sums_ref[...] = jnp.zeros_like(sums_ref)

    for t, sources in enumerate(pieces):

        @pl.when((step == 2 * t) & any_used)
        def _(sources=sources):
            for half, (operand, at) in enumerate(sources):
                ref = tiles[operand]
                rim[half] = ref[at, HALF:PIECE]

                def unpack(k, _, ref=ref, at=at, half=half):
                    base = pl.multiple_of(k * 64, 64)
                    to = pl.multiple_of(base + HALF * half, 64)
                    for b in range(4):
                        words = ref[at, pl.ds(base, 64), lanes(b)]
                        hbuf[b, pl.ds(to + 8, 64)] = high_of(words)
                        words_ref[b, pl.ds(to, 64)] = words
                    return 0

                if half:
                    lax.fori_loop(0, high_block, unpack, 0)
                else:
                    lax.fori_loop(low_block, 4, unpack, 0)

    @pl.when((slot_odd == 0) & any_used)
    def _():
        row_id = lax.broadcasted_iota(I32, (32, 256), 0)
        side = lax.broadcasted_iota(I32, (32, 256), 1) // 128
        scale = jnp.where(row_id == 16 * side, 256.0, 0.0) + jnp.where(
            row_id == 16 * side + 8, 1.0, 0.0
        )
        for half in range(2):
            words = rim[half, :, 0:HALF]
            high = lax.shift_right_arithmetic(words, 16)
            low = lax.shift_right_arithmetic(lax.shift_left(words, 16), 16)
            parts = jnp.concatenate(
                [
                    lax.shift_right_arithmetic(high, 8),
                    high & 255,
                    lax.shift_right_arithmetic(low, 8),
                    low & 255,
                ],
                axis=0,
            ).astype(F32).astype(BF16)
            columns = lax.dot_general(
                parts, scale.astype(BF16), (((0,), (0,)), ((), ())), preferred_element_type=F32
            )
            for side_id in range(2):
                hcol[side_id, HALF * half : HALF * (half + 1)] = columns[:, lanes(side_id)]
        top = high_of(rim[0])
        bottom = high_of(rim[1])
        for b in range(4):
            hbuf[b, 7:8] = top[1:2, lanes(b)]
            hbuf[b, T + 8 : T + 9] = bottom[1:2, lanes(b)]
            for at in (0, 8, 128, C + 8, T, T + 8):
                gy_ref[b, at : at + 8] = jnp.zeros((8, 128), F32)
        for b in (0, 3):
            gx_ref[b, 0:128] = jnp.zeros((128, 128), F32)
            gx_ref[b, C:T] = jnp.zeros((128, 128), F32)

        def slope(k):
            base = pl.multiple_of(k * CH, CH)
            rows = pl.ds(base, CH)
            here = [hbuf[b, pl.ds(base + 8, CH)] for b in range(4)]
            right_turn = [pltpu.roll(h, 1, 1) for h in here]
            left_turn = [pltpu.roll(h, 127, 1) for h in here]
            before = [hcol[0, rows]] + right_turn[:3]
            after = left_turn[1:] + [hcol[1, rows]]
            for b in range(4):
                left = jnp.where(at_first, before[b], right_turn[b])
                right = jnp.where(at_last, after[b], left_turn[b])
                sx = (right - left) * (0.5 / H_SCALE)
                sy = (hbuf[b, pl.ds(base + 9, CH)] - hbuf[b, pl.ds(base + 7, CH)]) * (
                    0.5 / H_SCALE
                )
                albedo = low_of(words_ref[b, rows]) * (1.0 / A_SCALE) + 1.0
                r = lax.rsqrt(1.0 + sx * sx + sy * sy)
                sx_ref[b, rows] = sx
                sy_ref[b, rows] = sy
                w_ref[b, rows] = albedo * r
                r2_ref[b, rows] = r * r
                gx_ref[b, rows] = jnp.zeros((CH, 128), F32)
                gy_ref[b, pl.ds(base + 8, CH)] = jnp.zeros((CH, 128), F32)

        def slope_block(k, _):
            for n in range(4):
                slope(4 * k + n)
            return 0

        lax.fori_loop(low_block, high_block, slope_block, 0)

    @pl.when(mine)
    def _():
        m = image[step]
        oy = pl.multiple_of(row_off[step], 128)
        ob = col_off[step] // 128
        s1 = sun[m]
        s2 = sun[16 + m]
        s3 = sun[32 + m]
        e = gain[m]

        def shade(k):
            base = k * CH
            rows = pl.ds(pl.multiple_of(oy + base, CH), CH)
            for b in range(3):
                q = s3 - s1 * sx_ref[ob + b, rows] - s2 * sy_ref[ob + b, rows]
                shaded[pl.ds(base, CH), lanes(b)] = (w_ref[ob + b, rows] * q).astype(BF16)
                tbuf[b, pl.ds(base, CH)] = q * r2_ref[ob + b, rows]

        for k in range(C // CH):
            shade(k)
        row_mat = res_ref[0, 0]
        col_mat = res_ref[0, 1]
        first_pass = jnp.dot(row_mat, shaded[...], preferred_element_type=F32).astype(BF16)

        def predict(low, high):
            block = e * lax.dot_general(
                first_pass[low:high],
                col_mat,
                (((1,), (1,)), ((), ())),
                preferred_element_type=F32,
            )
            for b in range(3):
                pbuf[b, 8 + low : 8 + high] = block[:, lanes(b)]
                if low == 0:
                    pbuf[b, 7:8] = 2.0 * block[0:1, lanes(b)] - block[1:2, lanes(b)]
                if high == C:
                    end = high - low
                    pbuf[b, C + 8 : C + 9] = (
                        2.0 * block[end - 1 : end, lanes(b)] - block[end - 2 : end - 1, lanes(b)]
                    )

        def add_up(v, base, total, by_row):
            groups = [v[8 * g : 8 * g + 8] for g in range(CH // 8)]
            tail = groups[-1]
            lead = tail
            for g in range(CH // 8 - 2, 0, -1):
                tail = groups[g] + tail
                lead = lead + tail
            tail = groups[0] + tail
            return total + tail, by_row + lead * 8.0 + tail * base

        def terms(k, carry):
            base = k * CH
            at = float(base)
            rows = pl.ds(base, CH)
            here = [pbuf[b, pl.ds(base + 8, CH)] for b in range(3)]
            right_turn = [pltpu.roll(p, 1, 1) for p in here]
            left_turn = [pltpu.roll(p, 127, 1) for p in here]
            before = [here[0]] + right_turn[:2]
            after = left_turn[1:] + [here[2]]
            result = []
            for b in range(3):
                a_x, a_xg, a_y, a_yg, a_e = carry[b]
                p = here[b]
                residual = p - obs_ref[0, rows, lanes(b)].astype(F32)
                weighted[rows, lanes(b)] = (e * residual).astype(BF16)
                left = jnp.where(at_first, before[b], right_turn[b])
                right = jnp.where(at_last, after[b], left_turn[b])
                a_x, a_xg = add_up(residual * (right - left), at, a_x, a_xg)
                down = pbuf[b, pl.ds(base + 9, CH)]
                up = pbuf[b, pl.ds(base + 7, CH)]
                a_y, a_yg = add_up(residual * (down - up), at, a_y, a_yg)
                squares = residual * p
                a_e = a_e + squares.reshape(CH // 8, 8, 128).sum(axis=0)
                result.append((a_x, a_xg, a_y, a_yg, a_e))
            return tuple(result)

        zero = jnp.zeros((8, 128), F32)
        parts = ((zero,) * 5,) * 3
        predict(0, 256)
        for k in range(0, 7):
            parts = terms(k, parts)
        predict(256, 384)
        tall = (((0,), (0,)), ((), ()))
        for k in range(7, 12):
            parts = terms(k, parts)
        back = lax.dot_general(row_mat, weighted[...], tall, preferred_element_type=F32)
        for b in range(3):
            for n in range(5):
                sums_ref[m, n, :, lanes(b)] = parts[b][n]
        back_pass = back.astype(BF16)

        def pull(k):
            base = k * CH
            rows = pl.ds(pl.multiple_of(oy + base, CH), CH)
            rows_y = pl.ds(pl.multiple_of(oy + base + 8, 8), CH)
            for b in range(3):
                t = tbuf[b, pl.ds(base, CH)]
                wg = w_ref[ob + b, rows] * grad[b, pl.ds(base, CH)]
                gx_ref[ob + b, rows] = gx_ref[ob + b, rows] - wg * (s1 + t * sx_ref[ob + b, rows])
                gy_ref[ob + b, rows_y] = gy_ref[ob + b, rows_y] - wg * (
                    s2 + t * sy_ref[ob + b, rows]
                )

        for low, high in ((0, 256), (256, C)):
            block = jnp.dot(back_pass[low:high], col_mat, preferred_element_type=F32)
            for b in range(3):
                grad[b, low:high] = block[:, lanes(b)]
            for k in range(low // CH, high // CH):
                pull(k)

    @pl.when((slot_odd == 1) & any_used)
    def _():
        def stencil(k, half):
            base = pl.multiple_of(k * CH, CH)
            rows = pl.ds(base, CH)
            to = pl.ds(pl.multiple_of(base - half * HALF, CH), CH)
            here = [gx_ref[b, rows] for b in range(4)]
            right_turn = [pltpu.roll(g, 1, 1) for g in here]
            left_turn = [pltpu.roll(g, 127, 1) for g in here]
            blank = jnp.zeros((CH, 128), F32)
            before = [blank] + right_turn[:3]
            after = left_turn[1:] + [blank]
            for b in range(4):
                left = jnp.where(at_first, before[b], right_turn[b])
                right = jnp.where(at_last, after[b], left_turn[b])
                up = gy_ref[b, pl.ds(base + 7, CH)]
                down = gy_ref[b, pl.ds(base + 9, CH)]
                total = (left - right) + (up - down)
                out_ref[0, half, to, lanes(b)] = (0.5 * total).astype(BF16)

        def stencil_block(k, _):
            for n in range(4):
                stencil(4 * k + n, k // 2)
            return 0

        lax.fori_loop(low_block, high_block, stencil_block, 0)
        sub = lax.broadcasted_iota(I32, (16, 128), 0)
        lane16 = lax.broadcasted_iota(I32, (16, 128), 1)

        @pl.when(low_block == 1)
        def _():
            for b in range(4):
                out_ref[0, 0, 0:112, lanes(b)] = jnp.zeros((112, 128), BF16)
                edge = jnp.where(sub == 15, -0.5 * gy_ref[b, 136:137], 0.0)
                out_ref[0, 0, 112:128, lanes(b)] = edge.astype(BF16)

        @pl.when(high_block == 3)
        def _():
            for b in range(4):
                edge = jnp.where(sub == 0, 0.5 * gy_ref[b, C + 7 : C + 8], 0.0)
                out_ref[0, 1, 128:144, lanes(b)] = edge.astype(BF16)
                out_ref[0, 1, 144:256, lanes(b)] = jnp.zeros((112, 128), BF16)

        pick_low = jnp.where((sub == 1) & (lane16 == 0), -0.5, 0.0).astype(BF16)
        pick_high = jnp.where((sub == 2) & (lane16 == 127), 0.5, 0.0).astype(BF16)
        cross = (((1,), (1,)), ((), ()))
        for half in range(2):
            rows = slice(HALF * half, HALF * (half + 1))
            spill = lax.dot_general(
                pick_low, gx_ref[0, rows].astype(BF16), cross, preferred_element_type=F32
            ) + lax.dot_general(
                pick_high, gx_ref[3, rows].astype(BF16), cross, preferred_element_type=F32
            )
            for b in range(4):
                edge = 0.5 * gy_ref[b, T + 7 : T + 8] if half else -0.5 * gy_ref[b, 8:9]
                rest = spill[:, lanes(b)] if b < 2 else jnp.zeros((16, 128), F32)
                out_ref[0, half, HALF:BACK, lanes(b)] = jnp.where(sub == 0, edge, rest).astype(
                    BF16
                )

    @pl.when((slot_odd == 1) & jnp.logical_not(any_used))
    def _():
        out_ref[...] = jnp.zeros_like(out_ref)


SCRATCH = [
    pltpu.VMEM((2, PIECE - HALF, T), I32),
    pltpu.VMEM((4, T, 128), I32),
    pltpu.VMEM((4, T + 16, 128), F32),
    pltpu.VMEM((2, T, 128), F32),
    pltpu.VMEM((4, T, 128), F32),
    pltpu.VMEM((4, T, 128), F32),
    pltpu.VMEM((4, T, 128), F32),
    pltpu.VMEM((4, T, 128), F32),
    pltpu.VMEM((4, T, 128), F32),
    pltpu.VMEM((4, T + 16, 128), F32),
    pltpu.VMEM((C, C), BF16),
    pltpu.VMEM((3, C, 128), F32),
    pltpu.VMEM((3, C + 16, 128), F32),
    pltpu.VMEM((C, C), BF16),
    pltpu.VMEM((3, C, 128), F32),
]


def run_tiles(arrays, pieces, resample, observed, plan, sun, gain):
    used, image, row_off, col_off = plan
    count = len(pieces)
    tile_specs = [pl.BlockSpec(v.shape, lambda i, *s: (0, 0, 0)) for v in arrays]
    grid_spec = pltpu.PrefetchScalarGridSpec(
        num_scalar_prefetch=6,
        grid=(2 * count,),
        in_specs=tile_specs
        + [
            pl.BlockSpec((1, 2, C, C), lambda i, u, m, *s: (m[i], 0, 0, 0)),
            pl.BlockSpec((1, C, C), lambda i, u, m, *s: (m[i], 0, 0)),
        ],
        out_specs=[
            pl.BlockSpec((1, 2, BACK, T), lambda i, *s: (i // 2, 0, 0, 0)),
            pl.BlockSpec((16, 5, 8, C), lambda i, *s: (0, 0, 0, 0)),
        ],
        scratch_shapes=SCRATCH,
    )
    return pl.pallas_call(
        functools.partial(tile_kernel, pieces, len(arrays)),
        grid_spec=grid_spec,
        out_shape=[
            jax.ShapeDtypeStruct((count, 2, BACK, T), BF16),
            jax.ShapeDtypeStruct((16, 5, 8, C), F32),
        ],
        compiler_params=pltpu.CompilerParams(dimension_semantics=("arbitrary",)),
        cost_estimate=pl.CostEstimate(
            flops=count * 8 * C * C * C, bytes_accessed=count * 8_000_000, transcendentals=0
        ),
    )(used, image, row_off, col_off, sun, gain, *arrays, resample, observed)


def around(step_x, step_y):
    return [
        (4 * y + x, 4 * ((y + step_y) % 4) + (x + step_x) % 4) for y in range(4) for x in range(4)
    ]


STEPS = {"x+": around(1, 0), "x-": around(-1, 0), "y+": around(0, 1), "y-": around(0, -1)}
STEPS["x2"] = around(2, 0)
STEPS["y2"] = around(0, 2)
WAYS = ("x+", "x-", "y+", "y-")
WAYS_BACK = ("x-", "x+", "y-", "y+")
NEAR = [(0, 0), (-1, 0), (1, 0), (0, -1), (0, 1)]
MIDDLE = [(-1, -1), (-1, 1), (1, -1), (1, 1), (2, 0), (0, 2)]
FAR = [(2, -1), (2, 1), (-1, 2), (1, 2), (2, 2)]


def send(messages):
    return {way: lax.ppermute(v, "dy", STEPS[way]) for way, v in messages.items()}


def send_near(upper, lower):
    return send({way: upper for way in WAYS}), send({way: lower for way in WAYS})


def send_middle(upper, lower):
    ahead = send(
        {"x+": upper["x+"], "x-": lower["x-"], "y+": upper["y+"], "y-": lower["y-"]}
    )
    along_x = jnp.concatenate([lower["y+"], lower["y-"]])
    along_y = jnp.concatenate([upper["x+"], upper["x-"]])
    aside = send({"x+": along_x, "x-": along_x, "y+": along_y, "y-": along_y})
    return ahead, aside


def send_far(ahead, aside):
    pairs = send({"x-": aside["x-"], "y-": aside["y-"]})
    single = send(
        {
            "x2": ahead["y+"],
            "y2": ahead["x-"],
            "x-": ahead["y-"],
            "x+": ahead["y-"],
            "y-": ahead["x+"],
            "y+": ahead["x+"],
        }
    )
    return pairs, single


def return_sums(near, middle, far):
    def wide(v):
        return v.astype(F32)

    def slim(v):
        return v.astype(BF16)

    flat = far.reshape((10,) + far.shape[2:])
    got = send(
        {
            "x2": flat[8:9],
            "y2": flat[9:10],
            "x-": flat[0:3],
            "y-": flat[4:7],
            "x+": flat[3:4],
            "y+": flat[7:8],
        }
    )
    xm, xp, ym, yp = (got[k] for k in WAYS_BACK)
    b_20 = slim(wide(middle[4, 1]) + wide(got["y2"][0]))
    a_02 = slim(wide(middle[5, 0]) + wide(got["x2"][0]))
    a_mm = slim(wide(middle[0, 0]) + wide(xm[0]) + wide(ym[0]))
    b_mm = slim(wide(middle[0, 1]) + wide(xm[1]) + wide(ym[1]))
    a_mp = slim(wide(middle[1, 0]) + wide(xm[2]))
    a_pm = slim(wide(middle[2, 0]) + wide(ym[2]))
    b_pp = slim(wide(middle[3, 1]) + wide(xp[0]) + wide(yp[0]))
    got = send(
        {
            "x-": jnp.stack([middle[4, 0], b_mm, middle[1, 1]]),
            "x+": jnp.stack([b_20, middle[2, 1], b_pp]),
            "y-": jnp.stack([a_02, a_mm, a_pm]),
            "y+": jnp.stack([middle[5, 1], a_mp, middle[3, 0]]),
        }
    )
    xm, xp, ym, yp = (got[k] for k in WAYS_BACK)

    def total(*pieces):
        result = wide(pieces[0])
        for piece in pieces[1:]:
            result = result + wide(piece)
        return slim(result)

    got = send(
        {
            "x-": jnp.stack([total(near[1, 0], xm[0], ym[1], yp[1]), near[1, 1]]),
            "x+": jnp.stack([total(near[2, 0], ym[2], yp[2]), total(near[2, 1], xp[0])]),
            "y-": jnp.stack([total(near[3, 0], ym[0]), total(near[3, 1], xm[1], xp[1])]),
            "y+": jnp.stack([near[4, 0], total(near[4, 1], xm[2], xp[2], yp[0])]),
        }
    )
    return [near[0]] + [got[way] for way in WAYS_BACK]


def next_images(used, image):
    count = used.shape[0]
    ids = jnp.arange(count, dtype=I32)
    is_used = used == 1
    ahead = jnp.min(
        jnp.where(is_used[None, :] & (ids[None, :] >= ids[:, None]), ids[None, :], count), axis=1
    )
    last = jnp.maximum(jnp.max(jnp.where(is_used, ids, -1)), 0)
    at = jnp.where(ahead < count, ahead, last)
    return jnp.sum(jnp.where(at[:, None] == ids[None, :], image[None, :], 0), axis=1)


def sun_vectors(azimuth, elevation):
    return jnp.stack(
        [
            jnp.cos(elevation) * jnp.cos(azimuth),
            jnp.cos(elevation) * jnp.sin(azimuth),
            jnp.sin(elevation),
        ]
    )


def laplace(padded):
    return (
        padded[:-2, 1:-1]
        + padded[2:, 1:-1]
        + padded[1:-1, :-2]
        + padded[1:-1, 2:]
        - 4.0 * padded[1:-1, 1:-1]
    )


def shifted(value, axis, up):
    count = lax.axis_size(axis)
    pairs = [(i, i + 1) for i in range(count - 1)]
    return lax.ppermute(value, axis, pairs if up else [(b, a) for a, b in pairs])


def quantize(heights):
    return jnp.round(heights * H_SCALE).astype(I32)


def smoothness(heights, top, bottom):
    tall = jnp.concatenate([top, heights, bottom], axis=0)
    left = shifted(tall[:, -2:], "dx", True)
    right = shifted(tall[:, :2], "dx", False)
    wide = jnp.concatenate([left, tall, right], axis=1)
    field = laplace(wide)
    rows, cols = heights.shape
    row_ids = jnp.arange(rows + 2)
    col_ids = jnp.arange(cols + 2)
    row_keep = ~(
        (row_ids == 0) & (lax.axis_index("dy") == 0)
        | (row_ids == rows + 1) & (lax.axis_index("dy") == lax.axis_size("dy") - 1)
    )
    col_keep = ~(
        (col_ids == 0) & (lax.axis_index("dx") == 0)
        | (col_ids == cols + 1) & (lax.axis_index("dx") == lax.axis_size("dx") - 1)
    )
    return SMOOTHING_WEIGHT * laplace(jnp.where(row_keep[:, None] & col_keep[None, :], field, 0.0))


def finish_sums(parts):
    ids = jnp.arange(C, dtype=F32)
    coord = (ids - 0.5 * (C - 1)) / C
    edge = jnp.where((ids == 0) | (ids == C - 1), 1.0, 0.5)
    start = (jnp.arange(8, dtype=F32) - 0.5 * (C - 1)) / C
    x_sum, x_row, y_sum, y_row, e_sum = (parts[:, n] for n in range(5))
    x_v = x_row / C + x_sum * start[None, :, None]
    y_v = y_row / C + y_sum * start[None, :, None]

    def total(v):
        return jnp.sum(v, axis=(1, 2))

    pose = [
        total(x_sum * edge),
        total(x_sum * (edge * coord)),
        total(x_v * edge),
        total(y_sum) * 0.5,
        total(y_sum * coord) * 0.5,
        total(y_v) * 0.5,
    ]
    return jnp.concatenate(
        [jnp.stack(pose, axis=-1) / C, (total(e_sum) / (C * C))[:, None]], axis=-1
    )


def per_device(
    heights, albedo, observed, resample, exposure, sun_azimuth, sun_elevation, send_plan, recv_plan
):
    offsets = send_plan[0, 0, 0:2].reshape(2, 16, 2).transpose(1, 0, 2)
    offsets = lax.all_to_all(offsets, "dy", split_axis=0, concat_axis=0, tiled=True)
    row_off = offsets[:, 0].reshape(-1)
    col_off = offsets[:, 1].reshape(-1)
    slots = jnp.arange(32, dtype=I32)
    relative = jnp.array(NEAR + MIDDLE + FAR, I32)
    place = lax.axis_index("dy")
    tile_ids = ((place // 4 + relative[:, 1]) % 4) * 4 + (place % 4 + relative[:, 0]) % 4
    slot_ids = (2 * tile_ids[:, None] + jnp.arange(2, dtype=I32)[None, :]).reshape(-1)
    match = recv_plan[0, 0][None, :] == slot_ids[:, None]
    used = jnp.any(match, axis=1).astype(I32)
    image = jnp.sum(jnp.where(match, jnp.arange(16, dtype=I32)[None, :], 0), axis=1)
    owned = []
    for low, high in ((0, 10), (10, 22), (22, 32)):
        part = used[low:high]
        owned.append((part, next_images(part, image[low:high])))
    chosen = slot_ids[:, None] == slots[None, :]
    table = jnp.sum(jnp.where(chosen[None], jnp.stack([row_off, col_off])[:, None, :], 0), axis=2)

    def plan_of(group, first, count):
        part = table[:, 2 * first : 2 * (first + count)]
        return owned[group] + (part[0], part[1])

    sun = sun_vectors(sun_azimuth[0], sun_elevation[0]).reshape(-1)
    gain = jnp.exp(exposure[0])

    top = shifted(heights[-2:], "dy", True)
    bottom = shifted(heights[:2], "dy", False)
    left = shifted(heights[:, -1], "dx", True)
    right = shifted(heights[:, 0], "dx", False)
    sides = pack(quantize(left), quantize(right)).reshape(2, 1, HALF)
    sides = jnp.concatenate([sides, jnp.zeros((2, 1, T - HALF), I32)], axis=2)
    ends = pack(quantize(jnp.stack([top[1:2], bottom[0:1]])), 0)
    words = pack(quantize(heights), jnp.round((albedo - 1.0) * A_SCALE).astype(I32))
    blank = jnp.zeros((PIECE - HALF - 2, T), I32)
    upper, lower = (
        jnp.concatenate([words[HALF * n : HALF * (n + 1)], sides[n], ends[n], blank])[None]
        for n in range(2)
    )
    near_a, near_b = send_near(upper, lower)
    ahead, aside = send_middle(near_a, near_b)
    pairs, single = send_far(ahead, aside)
    out_near, parts = run_tiles(
        [upper] + [near_a[k] for k in WAYS] + [lower] + [near_b[k] for k in WAYS],
        [((n, 0), (n + 5, 0)) for n in range(5)],
        resample, observed, plan_of(0, 0, 5), sun, gain,
    )
    out_middle, more = run_tiles(
        [aside[k] for k in WAYS] + [ahead[k] for k in WAYS],
        [
            ((2, 0), (0, 0)),
            ((3, 0), (0, 1)),
            ((2, 1), (1, 0)),
            ((3, 1), (1, 1)),
            ((4, 0), (5, 0)),
            ((6, 0), (7, 0)),
        ],
        resample, observed, plan_of(1, 5, 6), sun, gain,
    )
    parts = parts + more
    out_far, more = run_tiles(
        [pairs["x-"], pairs["y-"]] + [single[k] for k in ("y+", "y-", "x+", "x-", "x2", "y2")],
        [
            ((2, 0), (0, 0)),
            ((3, 0), (0, 1)),
            ((1, 0), (4, 0)),
            ((1, 1), (5, 0)),
            ((6, 0), (7, 0)),
        ],
        resample, observed, plan_of(2, 11, 5), sun, gain,
    )
    parts = parts + more
    smooth = smoothness(heights, top, bottom)
    crop_sums = finish_sums(parts)
    arrived = lax.all_to_all(
        crop_sums[:, None], "dy", split_axis=0, concat_axis=0, tiled=True
    )
    camera = arrived.sum(axis=0)
    arrived = return_sums(out_near, out_middle, out_far)
    rim = sum(v[:, HALF : HALF + 3].astype(F32) for v in arrived)
    from_below = shifted(rim[0, 0], "dy", False)
    from_above = shifted(rim[1, 0], "dy", True)
    from_right = shifted(rim[:, 1, :HALF].reshape(-1), "dx", False)
    from_left = shifted(rim[:, 2, :HALF].reshape(-1), "dx", True)
    row_ids = lax.broadcasted_iota(I32, (T, T), 0)
    col_ids = lax.broadcasted_iota(I32, (T, T), 1)
    data = sum(v[:, :HALF].astype(F32) for v in arrived).reshape(T, T)
    data = data + jnp.where(row_ids == T - 1, from_below[None, :], 0.0)
    data = data + jnp.where(row_ids == 0, from_above[None, :], 0.0)
    data = data + jnp.where(col_ids == T - 1, from_right[:, None], 0.0)
    data = data + jnp.where(col_ids == 0, from_left[:, None], 0.0)
    return (data + smooth, camera[None])


def solution(mesh):
    placed = (
        P("dy", "dx"),
        P("dy", "dx"),
        P(("dy", "dx"), None, None),
        P(("dy", "dx"), None, None, None),
        P("dx", None),
        P("dx", None),
        P("dx", None),
        P("dy", "dx", None, None),
        P("dy", "dx", None),
    )

    return jax.shard_map(
        per_device,
        mesh=mesh,
        in_specs=placed,
        out_specs=(P("dy", "dx"), P("dx", "dy", None)),
        check_vma=False,
    )
```
